512 devices in a mesh: wall: 64 (over z, y), xs: 8 (over x, core).
Axes of the slice: x: 4, y: 8, z: 8, core: 2. Of those that a mesh axis runs over, the one named last changes fastest.
Arguments:
- krylov_basis: float32 [3, 4, 128, 64, 1024], P(None, None, 'wall', None, 'xs'), may hold values from -7 to 7
- base_state: float32 [4, 128, 64, 1024], P(None, 'wall', None, 'xs'), may hold values from -6 to 6
- diffusivity: float32 [4], replicated, may hold values from 150 to 1500
Outputs:
- new_vector: float32 [4, 128, 64, 1024], P(None, 'wall', None, 'xs')
- hessenberg: float32 [4], replicated
The draws below stay inside these ranges and needn't reach their ends.
All inputs are finite; a program needn't handle non-finite values.
Results may differ from the reference program's by a relative error of at most 0.0003.
Values sent between devices are 32-bit elements; how exact they have to be, the bound alone decides.
No kernel may reach another device: no remote copies, remote signals or barrier semaphores. Data moves between devices by JAX's collectives and lax.ppermute only.
A program may use at most 64 MiB of HBM per device.

```python
import math
import jax
import jax.numpy as jnp
from jax import lax

NZ = 64
KRY = 3
STEPS = 1
NX = 1024
NY = 128


def draw_krylov_basis(key, part):
    shared_key = jax.random.fold_in(key, 11)
    individual_key = jax.random.fold_in(key, 12)
    shared = jax.random.truncated_normal(shared_key, -5.0, 5.0, (1, 4, NY, NZ, NX), jnp.float32)
    individual = jax.random.truncated_normal(individual_key, -5.0, 5.0, (KRY, 4, NY, NZ, NX), jnp.float32)
    return (0.8 * shared + 0.6 * individual).astype(jnp.float32)


def level_of(own_key, dims, pieces, least, top_value):
    gain, own = 1.0, jax.random.fold_in(own_key, 6)
    for dim, parts in pieces:
        heights = jnp.exp(jax.random.uniform(jax.random.fold_in(own, dim), (parts,), jnp.float32, least / len(pieces), top_value / len(pieces)))
        gain = gain * jnp.repeat(heights, dims[dim] // parts).reshape([-1 if axis == dim else 1 for axis in range(len(dims))])
    return gain


def centred(rng, dims, deviation, reach, shards=(), kind=jnp.bfloat16):
    gain = level_of(rng, dims, shards, -0.22, 0.18) if shards else 1.0
    drawn = jax.random.normal(rng, dims, jnp.float32) * deviation * gain
    return jnp.minimum(jnp.maximum(drawn, -reach), reach).astype(kind)


def setup_inputs(seed: int = 0) -> dict:
    key_list = jax.random.split(jax.random.key(seed), 4)
    krylov_basis = draw_krylov_basis(jax.random.fold_in(key_list[3], 71), 0)
    base_state = centred(key_list[1], (4, NY, NZ, NX), 1.0, 6.0, ((1, 64), (3, 8)), jnp.float32)
    diffusivity = jnp.clip(jnp.exp(jax.random.uniform(key_list[2], (4,), jnp.float32, math.log(150.0), math.log(1500.0))), 150.0, 1500.0)
    return {"krylov_basis": krylov_basis, "base_state": base_state, "diffusivity": diffusivity}


adv_step = 0.2
buoyancy = 0.5
screening = 0.004
epsilon = 1e-06

def fourier_table(length, cell_ids, mode_ids):
    wavenumbers = (mode_ids + 1) // 2
    phases = cell_ids[:, None] * wavenumbers[None, :] % length
    angles = phases.astype(jnp.float32) * (2.0 * math.pi / length)
    scaled = math.sqrt(2.0 / length)
    odd_mode = (mode_ids % 2 == 1)[None, :]
    values = jnp.where(odd_mode, scaled * jnp.cos(angles), scaled * jnp.sin(angles))
    values = jnp.where((mode_ids == 0)[None, :], 1.0 / math.sqrt(length), values)
    values = jnp.where((mode_ids == length - 1)[None, :], jnp.cos(angles) / math.sqrt(length), values)
    return values

def mode_eigen(length, mode_ids):
    wavenumbers = ((mode_ids + 1) // 2).astype(jnp.float32)
    return 4.0 * jnp.sin(wavenumbers * (math.pi / length)) ** 2

def centered(values_in):
    along_x = (jnp.roll(values_in, -1, 3) - jnp.roll(values_in, 1, 3)) * 0.5
    padded = jnp.pad(values_in, ((0, 0), (1, 1), (0, 0), (0, 0)))
    along_y = (padded[:, 2:] - padded[:, :-2]) * 0.5
    along_z = (jnp.roll(values_in, -1, 2) - jnp.roll(values_in, 1, 2)) * 0.5
    return (along_x, along_y, along_z)

def tridiagonal(right_side, shifts):
    beta = 2.0 + shifts
    zeros = jnp.zeros_like(right_side[0])

    def forward(running, row_value):
        prev_coef, prev_value = running
        coefficient = 1.0 / (-beta - prev_coef)
        reduced = (row_value - prev_value) * coefficient
        return ((coefficient, reduced), (coefficient, reduced))
    _, (coefficients, reduced_rows) = lax.scan(forward, (zeros, zeros), right_side)

    def backward(above_value, pair):
        coefficient, reduced = pair
        result = reduced - coefficient * above_value
        return (result, result)
    _, solved = lax.scan(backward, zeros, (coefficients, reduced_rows), reverse=True)
    return solved

def solve_pressure(flow_divergence):
    highest_mode = lax.Precision.HIGHEST
    span_ids = jnp.arange(NZ, dtype=jnp.int32)
    stream_ids = jnp.arange(NX, dtype=jnp.int32)
    spanwise_table = fourier_table(NZ, span_ids, span_ids)
    stream_table = fourier_table(NX, stream_ids, stream_ids)
    spectral_field = jnp.einsum('orp,rb->obp', flow_divergence, spanwise_table, precision=highest_mode)
    spectral_field = jnp.dot(spectral_field.reshape(-1, NX), stream_table, precision=highest_mode).reshape(NY, NZ, NX)
    shifts = mode_eigen(NZ, span_ids)[:, None] + mode_eigen(NX, stream_ids)[None, :] + screening
    solved = tridiagonal(spectral_field, shifts)
    line_entries = jnp.dot(solved.reshape(-1, NX), stream_table.T, precision=highest_mode).reshape(NY, NZ, NX)
    return jnp.einsum('pqa,wq->pwa', line_entries, spanwise_table, precision=highest_mode)

def time_step(current, base_state, base_grads, shifts):
    gradient_fields = centered(current)
    advect = jnp.zeros_like(current)
    for direction in range(3):
        advect = advect + base_state[direction:direction + 1] * gradient_fields[direction]
        advect = advect + current[direction:direction + 1] * base_grads[direction]
    updated = current - adv_step * advect
    updated = updated.at[1].add(buoyancy * current[3])
    velocity = updated[:3]
    vel_x, vel_y, vel_z = centered(velocity)
    flow_divergence = vel_x[0] + vel_y[1] + vel_z[2]
    pressure_field = solve_pressure(flow_divergence)
    press_x, press_y, press_z = centered(pressure_field[None])
    corrected = velocity - jnp.concatenate([press_x, press_y, press_z], 0)
    updated = jnp.concatenate([corrected, updated[3:]], 0)
    rows_first = jnp.moveaxis(updated, 1, 0)
    solved = tridiagonal(-shifts * rows_first, shifts)
    return jnp.moveaxis(solved, 0, 1)

def reference(krylov_basis, base_state, diffusivity):
    shifts = (1.0 / diffusivity)[:, None, None]
    base_grads = centered(base_state)
    current = krylov_basis[KRY - 1]
    for repeat in range(STEPS):
        current = time_step(current, base_state, base_grads, shifts)
    entries = 4.0 * NY * NZ * NX
    products = jnp.stack([jnp.sum(krylov_basis[index_vec] * current) for index_vec in range(KRY)]) / entries
    residual = current
    for index_vec in range(KRY):
        residual = residual - products[index_vec] * krylov_basis[index_vec]
    norm_value = jnp.sqrt(jnp.sum(residual * residual) / entries + epsilon)
    return (residual / norm_value, jnp.concatenate([products, norm_value[None]]))
```

```python
import math

import jax
import jax.numpy as jnp
import ml_dtypes
import numpy as np
from jax import lax
from jax.experimental import pallas as pl
from jax.experimental.pallas import tpu as pltpu
from jax.sharding import Mesh
from jax.sharding import PartitionSpec as P

WALL = ("wall_0", "wall_1")
XS = ("xs_0", "xs_1")

ADV_STEP = 0.2
BUOYANCY = 0.5
SCREENING = 0.004
EPSILON = 1e-06

NX, NY, NZ = 1024, 128, 64
LINES, LANES, BLOCKS = 8, 128, 8
HALF = math.sqrt(0.5)


def split(table):
    high = table.astype(ml_dtypes.bfloat16)
    low = (table - high.astype(np.float64)).astype(ml_dtypes.bfloat16)
    return high, low


def spanwise_tables():
    cells = np.arange(NZ)
    table = np.zeros((NZ, NZ))
    eigen = np.zeros((NZ // 2, 2))
    slope = np.zeros((NZ // 2, 2))
    for pair in range(NZ // 2):
        if pair == 0:
            table[0] = 1.0 / math.sqrt(NZ)
            table[1] = np.cos(math.pi * cells) / math.sqrt(NZ)
            eigen[0] = (0.0, 4.0)
            continue
        angle = 2.0 * math.pi * (cells * pair % NZ) / NZ
        table[2 * pair] = np.cos(angle) * math.sqrt(2.0 / NZ)
        table[2 * pair + 1] = np.sin(angle) * math.sqrt(2.0 / NZ)
        eigen[pair] = 4.0 * math.sin(math.pi * pair / NZ) ** 2
        wave = math.sin(2.0 * math.pi * pair / NZ)
        slope[pair] = (wave, -wave)
    return table, eigen, slope


def stream_tables():
    cells = np.arange(LANES)
    weights = np.zeros((4, 2 * LANES, 2 * LANES))
    eigen = np.zeros((16, 2, 32))
    slope = np.zeros((16, 2, 32))
    for tile in range(8):
        group = tile // 2
        base = (0, 4)[tile] if group == 0 else group
        first = 0 if group == 0 else 64 * (tile % 2)
        for slot in range(64):
            wave = 8 * (first + slot) + base
            half, place = divmod(slot, 32)
            block = 2 * tile + half
            at = (tile % 2) * LANES + half * 64 + place
            angle = 2.0 * math.pi * (cells * wave % NX) / NX
            scale = math.sqrt(2.0 / NX)
            if wave == 0:
                alternate = np.cos(math.pi * cells)
                weights[0, :LANES, at] = 1.0 / math.sqrt(NX)
                weights[0, :LANES, at + 32] = alternate / math.sqrt(NX)
                eigen[block, :, place] = (0.0, 4.0)
                continue
            eigen[block, :, place] = 4.0 * math.sin(math.pi * wave / NX) ** 2
            rise = math.sin(2.0 * math.pi * wave / NX)
            slope[block, :, place] = (rise, -rise)
            cos, sin = scale * np.cos(angle), scale * np.sin(angle)
            if group == 0:
                rows = slice((tile % 2) * LANES, (tile % 2 + 1) * LANES)
                weights[0, rows, at] = cos
                weights[0, rows, at + 32] = sin
            else:
                weights[group, :LANES, at] = cos
                weights[group, LANES:, at] = -sin
                weights[group, :LANES, at + 32] = sin
                weights[group, LANES:, at + 32] = cos
    return weights, eigen, slope


def wall_tables():
    order = np.arange(1, NY + 1)
    sine = np.sin(math.pi * (np.outer(order, order) % (2 * NY + 2)) / (NY + 1))
    sine = sine * math.sqrt(2.0 / (NY + 1))
    shift = np.eye(NY, k=1)
    slope = 0.5 * (shift - shift.T)
    eigen = 2.0 - 2.0 * np.cos(math.pi * order / (NY + 1))
    rows = np.concatenate([np.arange(0, NY, 2), np.arange(1, NY, 2)])
    return sine[:, rows], sine @ slope @ sine, eigen


def column_tables():
    _, span_eigen, span_slope = spanwise_tables()
    _, stream_eigen, stream_slope = stream_tables()
    stream = np.zeros((16, 2, LANES), np.float32)
    for block in range(16):
        stream[block, 0] = np.tile(stream_eigen[block].reshape(-1), 2)
        stream[block, 1] = np.tile(stream_slope[block].reshape(-1), 2)
    span = np.zeros((NZ, 2, LANES), np.float32)
    for pair in range(NZ // 2):
        for odd in range(2):
            turn = slice(None, None, -1 if odd else 1)
            span[2 * pair + odd, 0] = np.repeat(span_eigen[pair][turn], 64)
            span[2 * pair + odd, 1] = np.repeat(span_slope[pair][turn], 64)
    return stream, span


def halves(x):
    high = x.astype(jnp.bfloat16)
    low = (x - high.astype(jnp.float32)).astype(jnp.bfloat16)
    return high, low


def dot(a, b):
    return jnp.dot(a, b, preferred_element_type=jnp.float32)


def times_table(x, high_table, low_table):
    high, low = halves(x)
    return dot(high, high_table) + (dot(low, high_table) + dot(high, low_table))


def table_times(high_table, low_table, x):
    high, low = halves(x)
    return dot(high_table, high) + (dot(high_table, low) + dot(low_table, high))


def lane_ids(rows):
    return lax.broadcasted_iota(jnp.int32, (rows, LANES), 1)


def edges_kernel(vec_ref, base_ref, low_x, high_x, low_y, high_y):
    lanes = lane_ids(NZ)
    low = jnp.zeros((NZ, LANES), jnp.float32)
    high = jnp.zeros((NZ, LANES), jnp.float32)
    for field in range(8):
        ref, part = (vec_ref.at[0], field) if field < 4 else (base_ref, field - 4)
        for row in range(2):
            block = ref[part, row]
            at = 2 * field + row
            low = jnp.where(lanes == at, pltpu.roll(block, at, 1), low)
            high = jnp.where(lanes == at, pltpu.roll(block, (at + 1) % LANES, 1), high)
            if row == 0:
                low_y[field] = block
            else:
                high_y[field] = block
    low_x[...] = low
    high_x[...] = high


def advect_kernel(
    vec_ref, base_ref, left_ref, right_ref, below_ref, above_ref, th_ref, tl_ref, out_ref
):
    lanes = lane_ids(NZ)
    first, last = lanes == 0, lanes == LANES - 1
    left, right = left_ref[...], right_ref[...]

    def value(field, row):
        return vec_ref[0, field, row] if field < 4 else base_ref[field - 4, row]

    def slopes(field, row):
        x = value(field, row)
        at = 2 * field + row
        up = jnp.where(last, pltpu.roll(right, (LANES - 1 - at) % LANES, 1), pltpu.roll(x, LANES - 1, 1))
        down = jnp.where(first, pltpu.roll(left, (LANES - at) % LANES, 1), pltpu.roll(x, 1, 1))
        along_x = (up - down) * 0.5
        if row == 0:
            along_y = (value(field, 1) - below_ref[field]) * 0.5
        else:
            along_y = (above_ref[field] - value(field, 0)) * 0.5
        along_z = (pltpu.roll(x, NZ - 1, 0) - pltpu.roll(x, 1, 0)) * 0.5
        return along_x, along_y, along_z

    high_table, low_table = th_ref[...], tl_ref[...]
    for row in range(2):
        for field in range(4):
            grad = slopes(field, row)
            base_grad = slopes(field + 4, row)
            advect = jnp.zeros((NZ, LANES), jnp.float32)
            for axis in range(3):
                advect += value(4 + axis, row) * grad[axis]
                advect += value(axis, row) * base_grad[axis]
            updated = value(field, row) - ADV_STEP * advect
            if field == 1:
                updated += BUOYANCY * value(3, row)
            modes = table_times(high_table, low_table, updated)
            out_ref[pl.ds(2 * field + row, NZ, stride=LINES), :] = modes


def stream_kernel(in_ref, wh_ref, wl_ref, out_ref):
    x = [in_ref[s] for s in range(BLOCKS)]
    s04, d04 = x[0] + x[4], x[0] - x[4]
    s26, d26 = x[2] + x[6], x[2] - x[6]
    s15, d15 = x[1] + x[5], x[1] - x[5]
    s37, d37 = x[3] + x[7], x[3] - x[7]
    even, odd = s04 + s26, s15 + s37
    minus, plus = HALF * (d15 - d37), HALF * (d15 + d37)
    parts = [
        (even + odd, even - odd),
        (d04 + minus, plus + d26),
        (s04 - s26, s15 - s37),
        (d04 - minus, plus - d26),
    ]
    front = lane_ids(LINES) < 64
    for group in range(4):
        joined = jnp.concatenate(parts[group], axis=1)
        modes = times_table(joined, wh_ref[group], wl_ref[group])
        for side in range(2):
            tile = 2 * group + side
            for pair in range(4):
                cols = slice(side * LANES, (side + 1) * LANES)
                cos = modes[16 * pair : 16 * pair + 8, cols]
                sin = pltpu.roll(modes[16 * pair + 8 : 16 * pair + 16, cols], 64, 1)
                out_ref[16 * pair + 2 * tile] = jnp.where(front, cos, sin)
                out_ref[16 * pair + 2 * tile + 1] = jnp.where(front, sin, cos)


def solve_kernel(
    place_ref, diff_ref, in_ref, sh_ref, sl_ref, bh_ref, bl_ref, eh_ref, el_ref,
    eigen_ref, stream_ref, span_ref, out_ref,
):
    def field_rows(field):
        return jnp.concatenate(
            [in_ref[pl.ds(2 * field + row, NZ, stride=LINES), :] for row in range(2)], axis=0
        )

    fields = jnp.concatenate([field_rows(field) for field in range(4)], axis=1)
    waves = table_times(sh_ref[...], sl_ref[...], fields)
    u, v, w, heat = (waves[:, LANES * f : LANES * (f + 1)] for f in range(4))
    stream = stream_ref[place_ref[0]]
    span = span_ref[place_ref[1]]
    column = stream[0:1] + span[0:1] + SCREENING
    wall_eigen = eigen_ref[...]
    lower = lane_ids(NY) % 64 < 32

    def slope_x(f):
        return stream[1:2] * jnp.where(lower, pltpu.roll(f, LANES - 32, 1), pltpu.roll(f, 32, 1))

    def slope_z(f):
        return span[1:2] * pltpu.roll(f, 64, 1)

    def slope_y(f):
        return table_times(eh_ref[...], el_ref[...], f)

    divergence = slope_x(u) + slope_y(v) + slope_z(w)
    pressure = -divergence / (wall_eigen + column)
    corrected = (u - slope_x(pressure), v - slope_y(pressure), w - slope_z(pressure), heat)
    scaled = []
    for field in range(4):
        shift = 1.0 / (jnp.zeros((NY, LANES), jnp.float32) + diff_ref[field])
        scaled.append(corrected[field] * (shift / (wall_eigen + shift)))
    rows = table_times(bh_ref[...], bl_ref[...], jnp.concatenate(scaled, axis=1))
    for field in range(4):
        for row in range(2):
            out_ref[pl.ds(2 * field + row, NZ, stride=LINES), :] = rows[
                NZ * row : NZ * (row + 1), LANES * field : LANES * (field + 1)
            ]


def stream_back_kernel(in_ref, wh_ref, wl_ref, out_ref):
    front = lane_ids(LINES) < 64
    parts = []
    for group in range(4):
        sides = []
        for side in range(2):
            tile = 2 * group + side
            lines = []
            for pair in range(4):
                one = in_ref[16 * pair + 2 * tile]
                two = in_ref[16 * pair + 2 * tile + 1]
                lines.append(jnp.where(front, one, two))
                lines.append(pltpu.roll(jnp.where(front, two, one), 64, 1))
            sides.append(jnp.concatenate(lines, axis=0))
        cells = times_table(jnp.concatenate(sides, axis=1), wh_ref[group], wl_ref[group])
        parts.append((cells[:, :LANES], cells[:, LANES:]))
    (c0, c4), (c1, s1), (c2, s2), (c3, s3) = parts
    sum04, dif04 = c0 + c4, c0 - c4
    sum13, dif13 = c1 + c3, HALF * (c1 - c3)
    plus13, minus13 = HALF * (s1 + s3), s1 - s3
    outer_a, outer_b = sum04 + c2, sum04 - c2
    inner_a, inner_b = dif04 + s2, dif04 - s2
    out_ref[0] = outer_a + sum13
    out_ref[4] = outer_a - sum13
    out_ref[2] = outer_b + minus13
    out_ref[6] = outer_b - minus13
    out_ref[1] = inner_a + (dif13 + plus13)
    out_ref[5] = inner_a - (dif13 + plus13)
    out_ref[3] = inner_b + (plus13 - dif13)
    out_ref[7] = inner_b - (plus13 - dif13)


PAIRS = ((0, 0), (0, 1), (0, 2), (1, 1), (1, 2), (2, 2))


def folded(x):
    total = x[:LINES]
    for part in range(1, NZ // LINES):
        total += x[LINES * part : LINES * (part + 1)]
    return total


def cells_kernel(in_ref, vec_ref, th_ref, tl_ref, cur_ref, sums_ref):
    sums = [jnp.zeros((LINES, LANES), jnp.float32) for _ in range(10)]
    high_table, low_table = th_ref[...], tl_ref[...]
    for field in range(4):
        for row in range(2):
            modes = in_ref[pl.ds(2 * field + row, NZ, stride=LINES), :]
            cells = table_times(high_table, low_table, modes)
            cur_ref[field, row] = cells
            vectors = [vec_ref[q, field, row] for q in range(3)]
            for q in range(3):
                sums[q] += folded(vectors[q] * cells)
            sums[3] += folded(cells * cells)
            for at, (q, p) in enumerate(PAIRS):
                sums[4 + at] += folded(vectors[q] * vectors[p])
    lanes = lane_ids(LINES)
    packed = jnp.zeros((LINES, LANES), jnp.float32)
    for at in range(10):
        packed = jnp.where(lanes == at, jnp.sum(sums[at]), packed)
    sums_ref[...] = packed


def residual_kernel(sums_ref, cur_ref, vec_ref, out_ref, hess_ref):
    entries = float(4 * NX * NY * NZ)
    totals = jnp.sum(sums_ref[...], axis=0, keepdims=True) * (1.0 / entries)
    lanes = lane_ids(1)

    def pick(at):
        return jnp.sum(jnp.where(lanes == at, totals, 0.0), axis=1, keepdims=True)

    values = [pick(at) for at in range(10)]
    products = values[:3]
    square = values[3]
    for q in range(3):
        square = square - 2.0 * products[q] * products[q]
    for at, (q, p) in enumerate(PAIRS):
        twice = 1.0 if q == p else 2.0
        square = square + twice * products[q] * products[p] * values[4 + at]
    norm = jnp.sqrt(square + EPSILON)
    hess = jnp.where(lanes == 3, norm, 0.0)
    for q in range(3):
        hess = jnp.where(lanes == q, products[q], hess)
    hess_ref[...] = hess
    scale = 1.0 / norm
    for field in range(4):
        for row in range(2):
            left = cur_ref[field, row]
            for q in range(3):
                left = left - products[q] * vec_ref[q, field, row]
            out_ref[field, row] = left * scale


VMEM = pl.BlockSpec(memory_space=pltpu.VMEM)
SMEM = pl.BlockSpec(memory_space=pltpu.SMEM)


def f32(*dims):
    return jax.ShapeDtypeStruct(dims, jnp.float32)


def shards(krylov_basis, base_state, diffusivity):
    span, _, _ = spanwise_tables()
    stream, _, _ = stream_tables()
    sine, wall_slope, wall_eigen = wall_tables()
    stream_columns, span_columns = column_tables()
    eigen = np.broadcast_to(wall_eigen[:, None], (NY, LANES)).astype(np.float32)

    last = pl.BlockSpec((1, 4, 2, NZ, LANES), lambda i: (2, 0, 0, 0, 0))
    base_spec = pl.BlockSpec((4, 2, NZ, LANES), lambda i: (0, 0, 0, 0))
    low_x, high_x, low_y, high_y = pl.pallas_call(
        edges_kernel,
        grid=(1,),
        in_specs=[last, base_spec],
        out_specs=[VMEM] * 4,
        out_shape=[f32(NZ, LANES), f32(NZ, LANES), f32(8, NZ, LANES), f32(8, NZ, LANES)],
        name="edges",
    )(krylov_basis, base_state)
    size, walls = lax.axis_size(XS), lax.axis_size(WALL)
    above = lax.ppermute(low_y, WALL, [(i + 1, i) for i in range(walls - 1)])
    below = lax.ppermute(high_y, WALL, [(i, i + 1) for i in range(walls - 1)])
    right = lax.ppermute(low_x, XS, [((i + 1) % size, i) for i in range(size)])
    left = lax.ppermute(high_x, XS, [(i, (i + 1) % size) for i in range(size)])

    modes = pl.pallas_call(
        advect_kernel,
        grid=(1,),
        in_specs=[last, base_spec] + [VMEM] * 6,
        out_specs=VMEM,
        out_shape=f32(NZ * LINES, LANES),
        name="advect",
    )(krylov_basis, base_state, left, right, below, above, *split(span))
    lines = lax.all_to_all(modes.reshape(BLOCKS, -1, LANES), XS, 0, 0, tiled=True)
    spectra = pl.pallas_call(
        stream_kernel,
        in_specs=[VMEM] * 3,
        out_specs=VMEM,
        out_shape=f32(walls, LINES, LANES),
        name="stream",
    )(lines, *split(stream))
    columns = lax.all_to_all(spectra, WALL, 0, 0, tiled=True)
    wall_pos, stream_pos = lax.axis_index(WALL), lax.axis_index(XS)
    block = wall_pos % 16
    pair = stream_pos * 4 + wall_pos // 16
    place = jnp.stack([block, 2 * pair + block % 2])
    solved = pl.pallas_call(
        solve_kernel,
        in_specs=[SMEM, SMEM] + [VMEM] * 10,
        out_specs=VMEM,
        out_shape=f32(NZ * LINES, LANES),
        name="solve",
    )(
        place, diffusivity, columns.reshape(-1, LANES),
        *split(sine), *split(sine.T), *split(wall_slope),
        eigen, stream_columns, span_columns,
    )
    spectra = lax.all_to_all(solved.reshape(walls, LINES, LANES), WALL, 0, 0, tiled=True)
    lines = pl.pallas_call(
        stream_back_kernel,
        in_specs=[VMEM] * 3,
        out_specs=VMEM,
        out_shape=f32(BLOCKS, NZ, LANES),
        name="stream_back",
    )(spectra, *split(stream.transpose(0, 2, 1)))
    modes = lax.all_to_all(lines, XS, 0, 0, tiled=True)
    current, sums = pl.pallas_call(
        cells_kernel,
        in_specs=[VMEM] * 4,
        out_specs=[VMEM] * 2,
        out_shape=[f32(4, 2, NZ, LANES), f32(LINES, LANES)],
        name="cells",
    )(modes.reshape(-1, LANES), krylov_basis, *split(span.T))
    sums = lax.all_to_all(sums, XS, 0, 0, tiled=True).sum(axis=0)
    sums = lax.all_to_all(jnp.broadcast_to(sums, (walls, LANES)), WALL, 0, 0, tiled=True)
    new_vector, hessenberg = pl.pallas_call(
        residual_kernel,
        in_specs=[VMEM] * 3,
        out_specs=[VMEM] * 2,
        out_shape=[f32(4, 2, NZ, LANES), f32(1, LANES)],
        name="residual",
    )(sums, current, krylov_basis)
    return new_vector, hessenberg[0, :4]


def solution(mesh):
    torus = Mesh(mesh.devices.reshape(8, 8, 4, 2), ("wall_0", "wall_1", "xs_0", "xs_1"))
    return jax.shard_map(
        shards,
        mesh=torus,
        in_specs=(P(None, None, WALL, None, XS), P(None, WALL, None, XS), P()),
        out_specs=(P(None, WALL, None, XS), P()),
        check_vma=False,
    )
```

```python
import math

import jax
import jax.numpy as jnp
import ml_dtypes
import numpy as np
from jax import lax
from jax.experimental import pallas as pl
from jax.experimental.pallas import tpu as pltpu
from jax.sharding import Mesh
from jax.sharding import PartitionSpec as P

WALL = ("wall_0", "wall_1")
XS = ("xs_0", "xs_1")

ADV_STEP = 0.2
BUOYANCY = 0.5
SCREENING = 0.004
EPSILON = 1e-06

NX, NY, NZ = 1024, 128, 64
LINES, LANES, BLOCKS = 8, 128, 8
HALF = math.sqrt(0.5)


def split(table):
    high = table.astype(ml_dtypes.bfloat16)
    low = (table - high.astype(np.float64)).astype(ml_dtypes.bfloat16)
    return high, low


def spanwise_tables():
    cells = np.arange(NZ)
    table = np.zeros((NZ, NZ))
    eigen = np.zeros((NZ // 2, 2))
    slope = np.zeros((NZ // 2, 2))
    for pair in range(NZ // 2):
        if pair == 0:
            table[0] = 1.0 / math.sqrt(NZ)
            table[1] = np.cos(math.pi * cells) / math.sqrt(NZ)
            eigen[0] = (0.0, 4.0)
            continue
        angle = 2.0 * math.pi * (cells * pair % NZ) / NZ
        table[2 * pair] = np.cos(angle) * math.sqrt(2.0 / NZ)
        table[2 * pair + 1] = np.sin(angle) * math.sqrt(2.0 / NZ)
        eigen[pair] = 4.0 * math.sin(math.pi * pair / NZ) ** 2
        wave = math.sin(2.0 * math.pi * pair / NZ)
        slope[pair] = (wave, -wave)
    return table, eigen, slope


def stream_tables():
    cells = np.arange(LANES)
    weights = np.zeros((4, 2 * LANES, 2 * LANES))
    eigen = np.zeros((16, 2, 32))
    slope = np.zeros((16, 2, 32))
    for tile in range(8):
        group = tile // 2
        base = (0, 4)[tile] if group == 0 else group
        first = 0 if group == 0 else 64 * (tile % 2)
        for slot in range(64):
            wave = 8 * (first + slot) + base
            half, place = divmod(slot, 32)
            block = 2 * tile + half
            at = (tile % 2) * LANES + half * 64 + place
            angle = 2.0 * math.pi * (cells * wave % NX) / NX
            scale = math.sqrt(2.0 / NX)
            if wave == 0:
                alternate = np.cos(math.pi * cells)
                weights[0, :LANES, at] = 1.0 / math.sqrt(NX)
                weights[0, :LANES, at + 32] = alternate / math.sqrt(NX)
                eigen[block, :, place] = (0.0, 4.0)
                continue
            eigen[block, :, place] = 4.0 * math.sin(math.pi * wave / NX) ** 2
            rise = math.sin(2.0 * math.pi * wave / NX)
            slope[block, :, place] = (rise, -rise)
            cos, sin = scale * np.cos(angle), scale * np.sin(angle)
            if group == 0:
                rows = slice((tile % 2) * LANES, (tile % 2 + 1) * LANES)
                weights[0, rows, at] = cos
                weights[0, rows, at + 32] = sin
            else:
                weights[group, :LANES, at] = cos
                weights[group, LANES:, at] = -sin
                weights[group, :LANES, at + 32] = sin
                weights[group, LANES:, at + 32] = cos
    return weights, eigen, slope


def wall_tables():
    order = np.arange(1, NY + 1)
    sine = np.sin(math.pi * (np.outer(order, order) % (2 * NY + 2)) / (NY + 1))
    sine = sine * math.sqrt(2.0 / (NY + 1))
    shift = np.eye(NY, k=1)
    slope = 0.5 * (shift - shift.T)
    eigen = 2.0 - 2.0 * np.cos(math.pi * order / (NY + 1))
    rows = np.concatenate([np.arange(0, NY, 2), np.arange(1, NY, 2)])
    return sine[:, rows], (sine @ slope)[:, rows], sine @ slope @ sine, eigen


def column_tables():
    _, span_eigen, span_slope = spanwise_tables()
    _, stream_eigen, stream_slope = stream_tables()
    stream = np.zeros((16, 2, LANES), np.float32)
    for block in range(16):
        stream[block, 0] = np.tile(stream_eigen[block].reshape(-1), 2)
        stream[block, 1] = np.tile(stream_slope[block].reshape(-1), 2)
    span = np.zeros((NZ, 2, LANES), np.float32)
    for pair in range(NZ // 2):
        for odd in range(2):
            turn = slice(None, None, -1 if odd else 1)
            span[2 * pair + odd, 0] = np.repeat(span_eigen[pair][turn], 64)
            span[2 * pair + odd, 1] = np.repeat(span_slope[pair][turn], 64)
    return stream, span


def halves(x):
    high = x.astype(jnp.bfloat16)
    low = (x - high.astype(jnp.float32)).astype(jnp.bfloat16)
    return high, low


def dot(a, b):
    return jnp.dot(a, b, preferred_element_type=jnp.float32)


def times_table(x, high_table, low_table):
    high, low = halves(x)
    return dot(high, high_table) + (dot(low, high_table) + dot(high, low_table))


def table_times(high_table, low_table, x):
    high, low = halves(x)
    return dot(high_table, high) + (dot(high_table, low) + dot(low_table, high))


def lane_ids(rows):
    return lax.broadcasted_iota(jnp.int32, (rows, LANES), 1)


def copy_kernel(vec_ref, base_ref, low_ref, high_ref, sems):
    copies = []
    for row, ref in enumerate((low_ref, high_ref)):
        copies.append(
            pltpu.make_async_copy(vec_ref.at[2, :, row], ref.at[pl.ds(0, 4)], sems.at[2 * row])
        )
        copies.append(
            pltpu.make_async_copy(base_ref.at[:, row], ref.at[pl.ds(4, 4)], sems.at[2 * row + 1])
        )
    for copy in copies:
        copy.start()
    for copy in copies:
        copy.wait()


def edges_kernel(
    diff_ref, low_y, high_y, eigen_ref, stream_ref, span_ref,
    low_x, high_x, gain_ref, inverse_ref, slope_ref,
):
    lanes = lane_ids(NZ)
    low = jnp.zeros((NZ, LANES), jnp.float32)
    high = jnp.zeros((NZ, LANES), jnp.float32)
    for field in range(8):
        for row, ref in enumerate((low_y, high_y)):
            block = ref[field]
            at = 2 * field + row
            low = jnp.where(lanes == at, pltpu.roll(block, at, 1), low)
            high = jnp.where(lanes == at, pltpu.roll(block, (at + 1) % LANES, 1), high)
    low_x[...] = low
    high_x[...] = high

    wall = lax.axis_index("wall_0") * 8 + lax.axis_index("wall_1")
    line = lax.axis_index("xs_0") * 2 + lax.axis_index("xs_1")
    tile, slot = lax.div(wall, 8), lax.rem(wall, 8)
    stream = stream_ref[2 * tile + lax.rem(slot, 2)]
    span = span_ref[8 * line + slot]
    wall_eigen = eigen_ref[...]
    inverse_ref[...] = -1.0 / (wall_eigen + (stream[0:1] + span[0:1] + SCREENING))
    slope_ref[0:1, :] = stream[1:2]
    slope_ref[1:2, :] = span[1:2]
    for field in range(4):
        shift = 1.0 / (jnp.zeros((NY, LANES), jnp.float32) + diff_ref[field])
        gain_ref[field] = shift / (wall_eigen + shift)


def advect_kernel(
    low_ref, high_ref, left_ref, right_ref, below_ref, above_ref, th_ref, tl_ref, out_ref, heat_ref
):
    lanes = lane_ids(NZ)
    first, last = lanes == 0, lanes == LANES - 1
    left, right = left_ref[...], right_ref[...]

    def value(field, row):
        return (low_ref, high_ref)[row][field]

    def slopes(field, row):
        x = value(field, row)
        at = 2 * field + row
        up = jnp.where(last, pltpu.roll(right, (LANES - 1 - at) % LANES, 1), pltpu.roll(x, LANES - 1, 1))
        down = jnp.where(first, pltpu.roll(left, (LANES - at) % LANES, 1), pltpu.roll(x, 1, 1))
        along_x = (up - down) * 0.5
        if row == 0:
            along_y = (value(field, 1) - below_ref[field]) * 0.5
        else:
            along_y = (above_ref[field] - value(field, 0)) * 0.5
        along_z = (pltpu.roll(x, NZ - 1, 0) - pltpu.roll(x, 1, 0)) * 0.5
        return along_x, along_y, along_z

    high_table, low_table = th_ref[...], tl_ref[...]
    for row in range(2):
        for field in range(4):
            grad = slopes(field, row)
            base_grad = slopes(field + 4, row)
            advect = jnp.zeros((NZ, LANES), jnp.float32)
            for axis in range(3):
                advect += value(4 + axis, row) * grad[axis]
                advect += value(axis, row) * base_grad[axis]
            updated = value(field, row) - ADV_STEP * advect
            if field == 1:
                updated += BUOYANCY * value(3, row)
            if field == 3:
                heat_ref[row] = updated
                continue
            modes = table_times(high_table, low_table, updated)
            part = 2 * field + row
            for s in range(BLOCKS):
                out_ref[s, LINES * part : LINES * (part + 1)] = modes[LINES * s : LINES * (s + 1)]


def deal(x):
    rows = x.shape[0]
    even = lax.broadcasted_iota(jnp.int32, (rows, LANES), 0) % 2 == 0
    front = lane_ids(rows) < 64
    turned = pltpu.roll(x, 64, 1)
    return jnp.where(
        even,
        jnp.where(front, x, pltpu.roll(turned, rows - 1, 0)),
        jnp.where(front, turned, pltpu.roll(x, 1, 0)),
    )


def collect(x):
    rows = x.shape[0]
    even = lax.broadcasted_iota(jnp.int32, (rows, LANES), 0) % 2 == 0
    front = lane_ids(rows) < 64
    turned = pltpu.roll(x, 64, 1)
    return jnp.where(
        even,
        jnp.where(front, x, pltpu.roll(x, rows - 1, 0)),
        jnp.where(front, pltpu.roll(turned, 1, 0), turned),
    )


def stream_kernel(in_ref, heat_ref, wh_ref, wl_ref, out_ref):
    x = [in_ref[s] for s in range(BLOCKS)]
    s04, d04 = x[0] + x[4], x[0] - x[4]
    s26, d26 = x[2] + x[6], x[2] - x[6]
    s15, d15 = x[1] + x[5], x[1] - x[5]
    s37, d37 = x[3] + x[7], x[3] - x[7]
    even, odd = s04 + s26, s15 + s37
    minus, plus = HALF * (d15 - d37), HALF * (d15 + d37)
    parts = [
        (even + odd, even - odd),
        (d04 + minus, plus + d26),
        (s04 - s26, s15 - s37),
        (d04 - minus, plus - d26),
    ]
    for group in range(4):
        joined = jnp.concatenate(parts[group], axis=1)
        modes = times_table(joined, wh_ref[group], wl_ref[group])
        for side in range(2):
            tile = 2 * group + side
            dealt = deal(modes[:, side * LANES : (side + 1) * LANES])
            for part in range(6):
                out_ref[pl.ds(NZ * tile + part, LINES, stride=LINES), :] = dealt[
                    LINES * part : LINES * (part + 1)
                ]
    for row in range(2):
        out_ref[pl.ds(6 + row, NZ, stride=LINES), :] = heat_ref[row]


def solve_kernel(
    in_ref, sh_ref, sl_ref, dh_ref, dl_ref, bh_ref, bl_ref, eh_ref, el_ref,
    gain_ref, inverse_ref, slope_ref, out_ref,
):
    def field_rows(field):
        return jnp.concatenate(
            [in_ref[pl.ds(2 * field + row, NZ, stride=LINES), :] for row in range(2)], axis=0
        )

    fields = [field_rows(field) for field in range(4)]
    waves = table_times(sh_ref[...], sl_ref[...], jnp.concatenate(fields, axis=1))
    u, v, w, heat = (waves[:, LANES * f : LANES * (f + 1)] for f in range(4))
    rise = table_times(dh_ref[...], dl_ref[...], fields[1])
    stream, span = slope_ref[0:1, :], slope_ref[1:2, :]
    lower = lane_ids(NY) % 64 < 32

    def slope_x(f):
        return stream * jnp.where(lower, pltpu.roll(f, LANES - 32, 1), pltpu.roll(f, 32, 1))

    def slope_z(f):
        return span * pltpu.roll(f, 64, 1)

    pressure = inverse_ref[...] * (slope_x(u) + rise + slope_z(w))
    lift = table_times(eh_ref[...], el_ref[...], pressure)
    corrected = (u - slope_x(pressure), v - lift, w - slope_z(pressure), heat)
    scaled = [corrected[field] * gain_ref[field] for field in range(4)]
    rows = table_times(bh_ref[...], bl_ref[...], jnp.concatenate(scaled, axis=1))
    for field in range(4):
        for row in range(2):
            out_ref[pl.ds(2 * field + row, NZ, stride=LINES), :] = rows[
                NZ * row : NZ * (row + 1), LANES * field : LANES * (field + 1)
            ]


def stream_back_kernel(in_ref, wh_ref, wl_ref, out_ref, heat_ref):
    parts = []
    for group in range(4):
        sides = []
        for side in range(2):
            tile = 2 * group + side
            dealt = [in_ref[pl.ds(NZ * tile + part, LINES, stride=LINES), :] for part in range(6)]
            sides.append(collect(jnp.concatenate(dealt, axis=0)))
        cells = times_table(jnp.concatenate(sides, axis=1), wh_ref[group], wl_ref[group])
        parts.append((cells[:, :LANES], cells[:, LANES:]))
    for row in range(2):
        heat_ref[row] = in_ref[pl.ds(6 + row, NZ, stride=LINES), :]
    (c0, c4), (c1, s1), (c2, s2), (c3, s3) = parts
    sum04, dif04 = c0 + c4, c0 - c4
    sum13, dif13 = c1 + c3, HALF * (c1 - c3)
    plus13, minus13 = HALF * (s1 + s3), s1 - s3
    outer_a, outer_b = sum04 + c2, sum04 - c2
    inner_a, inner_b = dif04 + s2, dif04 - s2
    out_ref[0] = outer_a + sum13
    out_ref[4] = outer_a - sum13
    out_ref[2] = outer_b + minus13
    out_ref[6] = outer_b - minus13
    out_ref[1] = inner_a + (dif13 + plus13)
    out_ref[5] = inner_a - (dif13 + plus13)
    out_ref[3] = inner_b + (plus13 - dif13)
    out_ref[7] = inner_b - (plus13 - dif13)


PAIRS = ((0, 0), (0, 1), (0, 2), (1, 1), (1, 2), (2, 2))


def folded(x):
    total = x[:LINES]
    for part in range(1, NZ // LINES):
        total += x[LINES * part : LINES * (part + 1)]
    return total


def cells_kernel(in_ref, heat_ref, vec_ref, th_ref, tl_ref, cur_ref, sums_ref):
    sums = [jnp.zeros((LINES, LANES), jnp.float32) for _ in range(10)]
    high_table, low_table = th_ref[...], tl_ref[...]
    for field in range(4):
        for row in range(2):
            part = 2 * field + row
            if field == 3:
                cells = heat_ref[row]
            else:
                lines = [in_ref[s, LINES * part : LINES * (part + 1)] for s in range(BLOCKS)]
                cells = table_times(high_table, low_table, jnp.concatenate(lines, axis=0))
            cur_ref[field, row] = cells
            vectors = [vec_ref[q, field, row] for q in range(3)]
            for q in range(3):
                sums[q] += folded(vectors[q] * cells)
            sums[3] += folded(cells * cells)
            for at, (q, p) in enumerate(PAIRS):
                sums[4 + at] += folded(vectors[q] * vectors[p])
    lanes = lane_ids(16)
    packed = jnp.zeros((16, LANES), jnp.float32)
    for at in range(10):
        packed = jnp.where(lanes == at, jnp.sum(sums[at]), packed)
    sums_ref[...] = packed


def residual_kernel(sums_ref, cur_ref, vec_ref, out_ref, hess_ref):
    entries = float(4 * NX * NY * NZ)
    totals = jnp.sum(sums_ref[...], axis=0, keepdims=True) * (1.0 / entries)
    lanes = lane_ids(1)

    def pick(at):
        return jnp.sum(jnp.where(lanes == at, totals, 0.0), axis=1, keepdims=True)

    values = [pick(at) for at in range(10)]
    products = values[:3]
    square = values[3]
    for q in range(3):
        square = square - 2.0 * products[q] * products[q]
    for at, (q, p) in enumerate(PAIRS):
        twice = 1.0 if q == p else 2.0
        square = square + twice * products[q] * products[p] * values[4 + at]
    norm = jnp.sqrt(square + EPSILON)
    for q in range(3):
        hess_ref[q] = jnp.sum(products[q])
    hess_ref[3] = jnp.sum(norm)
    scale = 1.0 / norm
    for field in range(4):
        for row in range(2):
            left = cur_ref[field, row]
            for q in range(3):
                left = left - products[q] * vec_ref[q, field, row]
            out_ref[field, row] = left * scale


VMEM = pl.BlockSpec(memory_space=pltpu.VMEM)
SMALL = pltpu.CompilerParams(vmem_limit_bytes=8 * 1024 * 1024)
LARGE = pltpu.CompilerParams(vmem_limit_bytes=54500 * 1024)
SMEM = pl.BlockSpec(memory_space=pltpu.SMEM)


def f32(*dims):
    return jax.ShapeDtypeStruct(dims, jnp.float32)


def shards(krylov_basis, base_state, diffusivity):
    span, _, _ = spanwise_tables()
    stream, _, _ = stream_tables()
    sine, sine_slope, wall_slope, wall_eigen = wall_tables()
    stream_columns, span_columns = column_tables()
    eigen = np.broadcast_to(wall_eigen[:, None], (NY, LANES)).astype(np.float32)

    rows = f32(8, NZ, LANES)
    low_y, high_y = pl.pallas_call(
        copy_kernel,
        in_specs=[pl.BlockSpec(memory_space=pltpu.HBM)] * 2,
        out_specs=[VMEM] * 2,
        out_shape=[rows, rows],
        scratch_shapes=[pltpu.SemaphoreType.DMA((4,))],
        compiler_params=LARGE,
        name="copy",
    )(krylov_basis, base_state)
    size, walls = lax.axis_size(XS), lax.axis_size(WALL)
    above = lax.ppermute(low_y, WALL, [(i + 1, i) for i in range(walls - 1)])
    below = lax.ppermute(high_y, WALL, [(i, i + 1) for i in range(walls - 1)])
    low_x, high_x, gain, inverse, slope = pl.pallas_call(
        edges_kernel,
        in_specs=[SMEM] + [VMEM] * 5,
        out_specs=[VMEM] * 5,
        out_shape=[
            f32(NZ, LANES), f32(NZ, LANES), f32(4, NY, LANES), f32(NY, LANES), f32(2, LANES)
        ],
        compiler_params=SMALL,
        name="edges",
    )(diffusivity, low_y, high_y, eigen, stream_columns, span_columns)
    right = lax.ppermute(low_x, XS, [((i + 1) % size, i) for i in range(size)])
    left = lax.ppermute(high_x, XS, [(i, (i + 1) % size) for i in range(size)])

    modes, heat = pl.pallas_call(
        advect_kernel,
        in_specs=[VMEM] * 8,
        out_specs=[VMEM] * 2,
        out_shape=[f32(BLOCKS, 6 * LINES, LANES), f32(2, NZ, LANES)],
        compiler_params=SMALL,
        name="advect",
    )(low_y, high_y, left, right, below, above, *split(span))
    lines = lax.all_to_all(modes, XS, 0, 0, tiled=True)
    spectra = pl.pallas_call(
        stream_kernel,
        in_specs=[VMEM] * 4,
        out_specs=VMEM,
        out_shape=f32(walls * LINES, LANES),
        compiler_params=SMALL,
        name="stream",
    )(lines, heat, *split(stream))
    columns = lax.all_to_all(spectra.reshape(walls, LINES, LANES), WALL, 0, 0, tiled=True)
    solved = pl.pallas_call(
        solve_kernel,
        in_specs=[VMEM] * 12,
        out_specs=VMEM,
        out_shape=f32(walls * LINES, LANES),
        compiler_params=SMALL,
        name="solve",
    )(
        columns.reshape(-1, LANES), *split(sine), *split(sine_slope), *split(sine.T),
        *split(wall_slope), gain, inverse, slope,
    )
    spectra = lax.all_to_all(solved.reshape(walls, LINES, LANES), WALL, 0, 0, tiled=True)
    lines, heat = pl.pallas_call(
        stream_back_kernel,
        in_specs=[VMEM] * 3,
        out_specs=[VMEM] * 2,
        out_shape=[f32(BLOCKS, 6 * LINES, LANES), f32(2, NZ, LANES)],
        compiler_params=SMALL,
        name="stream_back",
    )(spectra.reshape(-1, LANES), *split(stream.transpose(0, 2, 1)))
    modes = lax.all_to_all(lines, XS, 0, 0, tiled=True)
    current, sums = pl.pallas_call(
        cells_kernel,
        in_specs=[VMEM] * 5,
        out_specs=[VMEM] * 2,
        out_shape=[f32(4, 2, NZ, LANES), f32(16, LANES)],
        compiler_params=SMALL,
        name="cells",
    )(modes, heat, krylov_basis, *split(span.T))
    sums = lax.all_to_all(sums, ("wall_0", "xs_1"), 0, 0, tiled=True).sum(axis=0)
    sums = jnp.broadcast_to(sums, (32, LANES))
    sums = lax.all_to_all(sums, ("wall_1", "xs_0"), 0, 0, tiled=True)
    new_vector, hessenberg = pl.pallas_call(
        residual_kernel,
        in_specs=[VMEM] * 3,
        out_specs=[VMEM, SMEM],
        out_shape=[f32(4, 2, NZ, LANES), f32(4)],
        compiler_params=SMALL,
        name="residual",
    )(sums, current, krylov_basis)
    return new_vector, hessenberg


def solution(mesh):
    torus = Mesh(mesh.devices.reshape(8, 8, 4, 2), ("wall_0", "wall_1", "xs_0", "xs_1"))
    return jax.shard_map(
        shards,
        mesh=torus,
        in_specs=(P(None, None, WALL, None, XS), P(None, WALL, None, XS), P()),
        out_specs=(P(None, WALL, None, XS), P()),
        check_vma=False,
    )
```

```python
import math

import jax
import jax.numpy as jnp
import ml_dtypes
import numpy as np
from jax import lax
from jax.experimental import pallas as pl
from jax.experimental.pallas import tpu as pltpu
from jax.sharding import Mesh
from jax.sharding import PartitionSpec as P

WALL = ("wall_0", "wall_1")
XS = ("xs_0", "xs_1")

ADV_STEP = 0.2
BUOYANCY = 0.5
SCREENING = 0.004
EPSILON = 1e-06

NX, NY, NZ = 1024, 128, 64
LINES, LANES, BLOCKS = 8, 128, 8
HALF = math.sqrt(0.5)


def split(table):
    high = table.astype(ml_dtypes.bfloat16)
    low = (table - high.astype(np.float64)).astype(ml_dtypes.bfloat16)
    return high, low


def spanwise_tables():
    cells = np.arange(NZ)
    table = np.zeros((NZ, NZ))
    eigen = np.zeros((NZ // 2, 2))
    slope = np.zeros((NZ // 2, 2))
    for pair in range(NZ // 2):
        if pair == 0:
            table[0] = 1.0 / math.sqrt(NZ)
            table[1] = np.cos(math.pi * cells) / math.sqrt(NZ)
            eigen[0] = (0.0, 4.0)
            continue
        angle = 2.0 * math.pi * (cells * pair % NZ) / NZ
        table[2 * pair] = np.cos(angle) * math.sqrt(2.0 / NZ)
        table[2 * pair + 1] = np.sin(angle) * math.sqrt(2.0 / NZ)
        eigen[pair] = 4.0 * math.sin(math.pi * pair / NZ) ** 2
        wave = math.sin(2.0 * math.pi * pair / NZ)
        slope[pair] = (wave, -wave)
    return table, eigen, slope


def stream_tables():
    cells = np.arange(LANES)
    weights = np.zeros((4, 2 * LANES, 2 * LANES))
    eigen = np.zeros((16, 2, 32))
    slope = np.zeros((16, 2, 32))
    for tile in range(8):
        group = tile // 2
        base = (0, 4)[tile] if group == 0 else group
        first = 0 if group == 0 else 64 * (tile % 2)
        for slot in range(64):
            wave = 8 * (first + slot) + base
            half, place = divmod(slot, 32)
            block = 2 * tile + half
            at = (tile % 2) * LANES + half * 64 + place
            angle = 2.0 * math.pi * (cells * wave % NX) / NX
            scale = math.sqrt(2.0 / NX)
            if wave == 0:
                alternate = np.cos(math.pi * cells)
                weights[0, :LANES, at] = 1.0 / math.sqrt(NX)
                weights[0, :LANES, at + 32] = alternate / math.sqrt(NX)
                eigen[block, :, place] = (0.0, 4.0)
                continue
            eigen[block, :, place] = 4.0 * math.sin(math.pi * wave / NX) ** 2
            rise = math.sin(2.0 * math.pi * wave / NX)
            slope[block, :, place] = (rise, -rise)
            cos, sin = scale * np.cos(angle), scale * np.sin(angle)
            if group == 0:
                rows = slice((tile % 2) * LANES, (tile % 2 + 1) * LANES)
                weights[0, rows, at] = cos
                weights[0, rows, at + 32] = sin
            else:
                weights[group, :LANES, at] = cos
                weights[group, LANES:, at] = -sin
                weights[group, :LANES, at + 32] = sin
                weights[group, LANES:, at + 32] = cos
    return weights, eigen, slope


def wall_tables():
    order = np.arange(1, NY + 1)
    sine = np.sin(math.pi * (np.outer(order, order) % (2 * NY + 2)) / (NY + 1))
    sine = sine * math.sqrt(2.0 / (NY + 1))
    shift = np.eye(NY, k=1)
    slope = 0.5 * (shift - shift.T)
    eigen = 2.0 - 2.0 * np.cos(math.pi * order / (NY + 1))
    rows = np.concatenate([np.arange(0, NY, 2), np.arange(1, NY, 2)])
    return sine[:, rows], (sine @ slope)[:, rows], sine @ slope @ sine, eigen


def column_tables():
    _, span_eigen, span_slope = spanwise_tables()
    _, stream_eigen, stream_slope = stream_tables()
    stream = np.zeros((16, 2, LANES), np.float32)
    for block in range(16):
        stream[block, 0] = np.tile(stream_eigen[block].reshape(-1), 2)
        stream[block, 1] = np.tile(stream_slope[block].reshape(-1), 2)
    span = np.zeros((NZ, 2, LANES), np.float32)
    for pair in range(NZ // 2):
        for odd in range(2):
            turn = slice(None, None, -1 if odd else 1)
            span[2 * pair + odd, 0] = np.repeat(span_eigen[pair][turn], 64)
            span[2 * pair + odd, 1] = np.repeat(span_slope[pair][turn], 64)
    return stream, span


def halves(x):
    high = x.astype(jnp.bfloat16)
    low = (x - high.astype(jnp.float32)).astype(jnp.bfloat16)
    return high, low


def dot(a, b):
    return jnp.dot(a, b, preferred_element_type=jnp.float32)


def times_table(x, high_table, low_table):
    high, low = halves(x)
    return dot(high, high_table) + (dot(low, high_table) + dot(high, low_table))


def table_times(high_table, low_table, x):
    high, low = halves(x)
    return dot(high_table, high) + (dot(high_table, low) + dot(low_table, high))


def lane_ids(rows):
    return lax.broadcasted_iota(jnp.int32, (rows, LANES), 1)


def copy_kernel(vec_ref, base_ref, first_ref, second_ref, sems):
    core = lax.axis_index("xs_1")
    copies = []
    for slot, ref in enumerate((first_ref, second_ref)):
        row = core if slot == 0 else 1 - core
        for field in range(4):
            copies.append((vec_ref.at[2, field, row], ref.at[field]))
            copies.append((base_ref.at[field, row], ref.at[4 + field]))
    copies = [
        pltpu.make_async_copy(source, target, sems.at[at])
        for at, (source, target) in enumerate(copies)
    ]
    for copy in copies:
        copy.start()
    for copy in copies:
        copy.wait()


def edges_kernel(
    diff_ref, first_ref, second_ref, eigen_ref, stream_ref, span_ref,
    low_x, high_x, gain_ref, inverse_ref, slope_ref,
):
    lanes = lane_ids(NZ)
    low = jnp.zeros((NZ, LANES), jnp.float32)
    high = jnp.zeros((NZ, LANES), jnp.float32)
    for field in range(8):
        for slot, ref in enumerate((first_ref, second_ref)):
            block = ref[field]
            at = 2 * field + slot
            low = jnp.where(lanes == at, pltpu.roll(block, at, 1), low)
            high = jnp.where(lanes == at, pltpu.roll(block, (at + 1) % LANES, 1), high)
    low_x[...] = low
    high_x[...] = high

    wall = lax.axis_index("wall_0") * 8 + lax.axis_index("wall_1")
    line = lax.axis_index("xs_0") * 2 + lax.axis_index("xs_1")
    tile, slot = lax.div(wall, 8), lax.rem(wall, 8)
    stream = stream_ref[2 * tile + lax.rem(slot, 2)]
    span = span_ref[8 * line + slot]
    wall_eigen = eigen_ref[...]
    inverse_ref[...] = -1.0 / (wall_eigen + (stream[0:1] + span[0:1] + SCREENING))
    slope_ref[0:1, :] = stream[1:2]
    slope_ref[1:2, :] = span[1:2]
    for field in range(4):
        shift = 1.0 / (jnp.zeros((NY, LANES), jnp.float32) + diff_ref[field])
        gain_ref[field] = shift / (wall_eigen + shift)


def advect_kernel(
    first_ref, second_ref, left_ref, right_ref, inner_ref, outer_ref, th_ref, tl_ref,
    out_ref, heat_ref,
):
    lanes = lane_ids(NZ)
    first, last = lanes == 0, lanes == LANES - 1
    left, right = left_ref[...], right_ref[...]
    core = lax.axis_index("xs_1")
    half = jnp.where(core == 0, 0.5, -0.5)

    def value(field, slot):
        return (first_ref, second_ref)[slot][field]

    def slopes(field, slot):
        x = value(field, slot)
        at = 2 * field + 1 - slot
        up = jnp.where(last, pltpu.roll(right, (LANES - 1 - at) % LANES, 1), pltpu.roll(x, LANES - 1, 1))
        down = jnp.where(first, pltpu.roll(left, (LANES - at) % LANES, 1), pltpu.roll(x, 1, 1))
        along_x = (up - down) * 0.5
        if slot == 0:
            along_y = (value(field, 1) - outer_ref[field]) * half
        else:
            along_y = (inner_ref[field] - value(field, 0)) * half
        along_z = (pltpu.roll(x, NZ - 1, 0) - pltpu.roll(x, 1, 0)) * 0.5
        return along_x, along_y, along_z

    high_table, low_table = th_ref[...], tl_ref[...]
    for field in range(4):
        updated = []
        for slot in range(2):
            grad = slopes(field, slot)
            base_grad = slopes(field + 4, slot)
            advect = jnp.zeros((NZ, LANES), jnp.float32)
            for axis in range(3):
                advect += value(4 + axis, slot) * grad[axis]
                advect += value(axis, slot) * base_grad[axis]
            result = value(field, slot) - ADV_STEP * advect
            if field == 1:
                result += BUOYANCY * value(3, slot)
            updated.append(result)
        if field == 3:
            heat_ref[core] = updated[0]
            heat_ref[1 - core] = updated[1]
            continue
        rows = jnp.concatenate(
            [
                jnp.where(core == 0, updated[0], updated[1]),
                jnp.where(core == 0, updated[1], updated[0]),
            ],
            axis=1,
        )
        modes = table_times(high_table, low_table, rows)
        for row in range(2):
            part = 2 * field + row
            for s in range(BLOCKS):
                out_ref[s, LINES * part : LINES * (part + 1)] = modes[
                    LINES * s : LINES * (s + 1), LANES * row : LANES * (row + 1)
                ]


def deal(x):
    rows = x.shape[0]
    even = lax.broadcasted_iota(jnp.int32, (rows, LANES), 0) % 2 == 0
    front = lane_ids(rows) < 64
    turned = pltpu.roll(x, 64, 1)
    return jnp.where(
        even,
        jnp.where(front, x, pltpu.roll(turned, rows - 1, 0)),
        jnp.where(front, turned, pltpu.roll(x, 1, 0)),
    )


def collect(x):
    rows = x.shape[0]
    even = lax.broadcasted_iota(jnp.int32, (rows, LANES), 0) % 2 == 0
    front = lane_ids(rows) < 64
    turned = pltpu.roll(x, 64, 1)
    return jnp.where(
        even,
        jnp.where(front, x, pltpu.roll(x, rows - 1, 0)),
        jnp.where(front, pltpu.roll(turned, 1, 0), turned),
    )


def stream_kernel(in_ref, heat_ref, wh_ref, wl_ref, out_ref):
    x = [in_ref[s] for s in range(BLOCKS)]
    s04, d04 = x[0] + x[4], x[0] - x[4]
    s26, d26 = x[2] + x[6], x[2] - x[6]
    s15, d15 = x[1] + x[5], x[1] - x[5]
    s37, d37 = x[3] + x[7], x[3] - x[7]
    even, odd = s04 + s26, s15 + s37
    minus, plus = HALF * (d15 - d37), HALF * (d15 + d37)
    parts = [
        (even + odd, even - odd),
        (d04 + minus, plus + d26),
        (s04 - s26, s15 - s37),
        (d04 - minus, plus - d26),
    ]
    for group in range(4):
        joined = jnp.concatenate(parts[group], axis=1)
        modes = times_table(joined, wh_ref[group], wl_ref[group])
        for side in range(2):
            tile = 2 * group + side
            dealt = deal(modes[:, side * LANES : (side + 1) * LANES])
            for part in range(6):
                out_ref[pl.ds(NZ * tile + part, LINES, stride=LINES), :] = dealt[
                    LINES * part : LINES * (part + 1)
                ]
    for row in range(2):
        out_ref[pl.ds(6 + row, NZ, stride=LINES), :] = heat_ref[row]


def solve_kernel(
    in_ref, sh_ref, sl_ref, dh_ref, dl_ref, bh_ref, bl_ref, eh_ref, el_ref,
    gain_ref, inverse_ref, slope_ref, out_ref,
):
    def field_rows(field):
        return jnp.concatenate(
            [in_ref[pl.ds(2 * field + row, NZ, stride=LINES), :] for row in range(2)], axis=0
        )

    fields = [field_rows(field) for field in range(4)]
    waves = table_times(sh_ref[...], sl_ref[...], jnp.concatenate(fields, axis=1))
    u, v, w, heat = (waves[:, LANES * f : LANES * (f + 1)] for f in range(4))
    rise = table_times(dh_ref[...], dl_ref[...], fields[1])
    stream, span = slope_ref[0:1, :], slope_ref[1:2, :]
    lower = lane_ids(NY) % 64 < 32

    def slope_x(f):
        return stream * jnp.where(lower, pltpu.roll(f, LANES - 32, 1), pltpu.roll(f, 32, 1))

    def slope_z(f):
        return span * pltpu.roll(f, 64, 1)

    pressure = inverse_ref[...] * (slope_x(u) + rise + slope_z(w))
    lift = table_times(eh_ref[...], el_ref[...], pressure)
    corrected = (u - slope_x(pressure), v - lift, w - slope_z(pressure), heat)
    scaled = [corrected[field] * gain_ref[field] for field in range(4)]
    rows = table_times(bh_ref[...], bl_ref[...], jnp.concatenate(scaled, axis=1))
    for field in range(4):
        for row in range(2):
            out_ref[pl.ds(2 * field + row, NZ, stride=LINES), :] = rows[
                NZ * row : NZ * (row + 1), LANES * field : LANES * (field + 1)
            ]


def stream_back_kernel(in_ref, wh_ref, wl_ref, out_ref, heat_ref):
    parts = []
    for group in range(4):
        sides = []
        for side in range(2):
            tile = 2 * group + side
            dealt = [in_ref[pl.ds(NZ * tile + part, LINES, stride=LINES), :] for part in range(6)]
            sides.append(collect(jnp.concatenate(dealt, axis=0)))
        cells = times_table(jnp.concatenate(sides, axis=1), wh_ref[group], wl_ref[group])
        parts.append((cells[:, :LANES], cells[:, LANES:]))
    for row in range(2):
        heat_ref[row] = in_ref[pl.ds(6 + row, NZ, stride=LINES), :]
    (c0, c4), (c1, s1), (c2, s2), (c3, s3) = parts
    sum04, dif04 = c0 + c4, c0 - c4
    sum13, dif13 = c1 + c3, HALF * (c1 - c3)
    plus13, minus13 = HALF * (s1 + s3), s1 - s3
    outer_a, outer_b = sum04 + c2, sum04 - c2
    inner_a, inner_b = dif04 + s2, dif04 - s2
    out_ref[0] = outer_a + sum13
    out_ref[4] = outer_a - sum13
    out_ref[2] = outer_b + minus13
    out_ref[6] = outer_b - minus13
    out_ref[1] = inner_a + (dif13 + plus13)
    out_ref[5] = inner_a - (dif13 + plus13)
    out_ref[3] = inner_b + (plus13 - dif13)
    out_ref[7] = inner_b - (plus13 - dif13)


PAIRS = ((0, 0), (0, 1), (0, 2), (1, 1), (1, 2), (2, 2))


def folded(x):
    total = x[:LINES]
    for part in range(1, NZ // LINES):
        total += x[LINES * part : LINES * (part + 1)]
    return total


def cells_kernel(in_ref, heat_ref, vec_ref, th_ref, tl_ref, cur_ref, sums_ref):
    sums = [jnp.zeros((LINES, LANES), jnp.float32) for _ in range(10)]
    high_table, low_table = th_ref[...], tl_ref[...]
    for field in range(4):
        for row in range(2):
            part = 2 * field + row
            if field == 3:
                cells = heat_ref[row]
            else:
                lines = [in_ref[s, LINES * part : LINES * (part + 1)] for s in range(BLOCKS)]
                cells = table_times(high_table, low_table, jnp.concatenate(lines, axis=0))
            cur_ref[field, row] = cells
            vectors = [vec_ref[q, field, row] for q in range(3)]
            for q in range(3):
                sums[q] += folded(vectors[q] * cells)
            sums[3] += folded(cells * cells)
            for at, (q, p) in enumerate(PAIRS):
                sums[4 + at] += folded(vectors[q] * vectors[p])
    lanes = lane_ids(16)
    packed = jnp.zeros((16, LANES), jnp.float32)
    for at in range(10):
        packed = jnp.where(lanes == at, jnp.sum(sums[at]), packed)
    sums_ref[...] = packed


def residual_kernel(sums_ref, cur_ref, vec_ref, out_ref, hess_ref):
    entries = float(4 * NX * NY * NZ)
    totals = jnp.sum(sums_ref[...], axis=0, keepdims=True) * (1.0 / entries)
    lanes = lane_ids(1)

    def pick(at):
        return jnp.sum(jnp.where(lanes == at, totals, 0.0), axis=1, keepdims=True)

    values = [pick(at) for at in range(10)]
    products = values[:3]
    square = values[3]
    for q in range(3):
        square = square - 2.0 * products[q] * products[q]
    for at, (q, p) in enumerate(PAIRS):
        twice = 1.0 if q == p else 2.0
        square = square + twice * products[q] * products[p] * values[4 + at]
    norm = jnp.sqrt(square + EPSILON)
    for q in range(3):
        hess_ref[q] = jnp.sum(products[q])
    hess_ref[3] = jnp.sum(norm)
    scale = 1.0 / norm
    for field in range(4):
        for row in range(2):
            left = cur_ref[field, row]
            for q in range(3):
                left = left - products[q] * vec_ref[q, field, row]
            out_ref[field, row] = left * scale


VMEM = pl.BlockSpec(memory_space=pltpu.VMEM)
SMALL = pltpu.CompilerParams(vmem_limit_bytes=8 * 1024 * 1024)
LARGE = pltpu.CompilerParams(vmem_limit_bytes=54500 * 1024)
SMEM = pl.BlockSpec(memory_space=pltpu.SMEM)


def f32(*dims):
    return jax.ShapeDtypeStruct(dims, jnp.float32)


def shards(krylov_basis, base_state, diffusivity):
    span, _, _ = spanwise_tables()
    stream, _, _ = stream_tables()
    sine, sine_slope, wall_slope, wall_eigen = wall_tables()
    stream_columns, span_columns = column_tables()
    eigen = np.broadcast_to(wall_eigen[:, None], (NY, LANES)).astype(np.float32)

    rows = f32(8, NZ, LANES)
    first, second = pl.pallas_call(
        copy_kernel,
        in_specs=[pl.BlockSpec(memory_space=pltpu.HBM)] * 2,
        out_specs=[VMEM] * 2,
        out_shape=[rows, rows],
        scratch_shapes=[pltpu.SemaphoreType.DMA((16,))],
        compiler_params=LARGE,
        name="copy",
    )(krylov_basis, base_state)
    size, walls = lax.axis_size(XS), lax.axis_size(WALL)
    down = [[(size * (i + 1) + s, size * i + s) for i in range(walls - 1)] for s in range(size)]
    up = [[(b, a) for a, b in pairs] for pairs in down]
    inner = lax.ppermute(first, WALL + XS, sum([(down, up)[s % 2][s] for s in range(size)], []))
    outer = lax.ppermute(second, WALL + XS, sum([(up, down)[s % 2][s] for s in range(size)], []))
    low_x, high_x, gain, inverse, slope = pl.pallas_call(
        edges_kernel,
        in_specs=[SMEM] + [VMEM] * 5,
        out_specs=[VMEM] * 5,
        out_shape=[
            f32(NZ, LANES), f32(NZ, LANES), f32(4, NY, LANES), f32(NY, LANES), f32(2, LANES)
        ],
        compiler_params=SMALL,
        name="edges",
    )(diffusivity, first, second, eigen, stream_columns, span_columns)
    right = lax.ppermute(low_x, XS, [((i + 1) % size, i) for i in range(size)])
    left = lax.ppermute(high_x, XS, [(i, (i + 1) % size) for i in range(size)])

    modes, heat = pl.pallas_call(
        advect_kernel,
        in_specs=[VMEM] * 8,
        out_specs=[VMEM] * 2,
        out_shape=[f32(BLOCKS, 6 * LINES, LANES), f32(2, NZ, LANES)],
        compiler_params=SMALL,
        name="advect",
    )(first, second, left, right, inner, outer, *split(span))
    lines = lax.all_to_all(modes, XS, 0, 0, tiled=True)
    spectra = pl.pallas_call(
        stream_kernel,
        in_specs=[VMEM] * 4,
        out_specs=VMEM,
        out_shape=f32(walls * LINES, LANES),
        compiler_params=SMALL,
        name="stream",
    )(lines, heat, *split(stream))
    columns = lax.all_to_all(spectra.reshape(walls, LINES, LANES), WALL, 0, 0, tiled=True)
    solved = pl.pallas_call(
        solve_kernel,
        in_specs=[VMEM] * 12,
        out_specs=VMEM,
        out_shape=f32(walls * LINES, LANES),
        compiler_params=SMALL,
        name="solve",
    )(
        columns.reshape(-1, LANES), *split(sine), *split(sine_slope), *split(sine.T),
        *split(wall_slope), gain, inverse, slope,
    )
    spectra = lax.all_to_all(solved.reshape(walls, LINES, LANES), WALL, 0, 0, tiled=True)
    lines, heat = pl.pallas_call(
        stream_back_kernel,
        in_specs=[VMEM] * 3,
        out_specs=[VMEM] * 2,
        out_shape=[f32(BLOCKS, 6 * LINES, LANES), f32(2, NZ, LANES)],
        compiler_params=SMALL,
        name="stream_back",
    )(spectra.reshape(-1, LANES), *split(stream.transpose(0, 2, 1)))
    modes = lax.all_to_all(lines, XS, 0, 0, tiled=True)
    current, sums = pl.pallas_call(
        cells_kernel,
        in_specs=[VMEM] * 5,
        out_specs=[VMEM] * 2,
        out_shape=[f32(4, 2, NZ, LANES), f32(16, LANES)],
        compiler_params=SMALL,
        name="cells",
    )(modes, heat, krylov_basis, *split(span.T))
    sums = lax.all_to_all(sums, ("wall_0", "xs_1"), 0, 0, tiled=True).sum(axis=0)
    sums = jnp.broadcast_to(sums, (32, LANES))
    sums = lax.all_to_all(sums, ("wall_1", "xs_0"), 0, 0, tiled=True)
    new_vector, hessenberg = pl.pallas_call(
        residual_kernel,
        in_specs=[VMEM] * 3,
        out_specs=[VMEM, SMEM],
        out_shape=[f32(4, 2, NZ, LANES), f32(4)],
        compiler_params=SMALL,
        name="residual",
    )(sums, current, krylov_basis)
    return new_vector, hessenberg


def solution(mesh):
    torus = Mesh(mesh.devices.reshape(8, 8, 4, 2), ("wall_0", "wall_1", "xs_0", "xs_1"))
    return jax.shard_map(
        shards,
        mesh=torus,
        in_specs=(P(None, None, WALL, None, XS), P(None, WALL, None, XS), P()),
        out_specs=(P(None, WALL, None, XS), P()),
        check_vma=False,
    )
```

```python
import math

import jax
import jax.numpy as jnp
import ml_dtypes
import numpy as np
from jax import lax
from jax.experimental import pallas as pl
from jax.experimental.pallas import tpu as pltpu
from jax.sharding import Mesh
from jax.sharding import PartitionSpec as P

WALL = ("wall_0", "wall_1")
XS = ("xs_0", "xs_1")

ADV_STEP = 0.2
BUOYANCY = 0.5
SCREENING = 0.004
EPSILON = 1e-06

NX, NY, NZ = 1024, 128, 64
LINES, LANES, BLOCKS = 8, 128, 8
ROWS = 16
HALF = math.sqrt(0.5)


def split(table):
    high = table.astype(ml_dtypes.bfloat16)
    low = (table - high.astype(np.float64)).astype(ml_dtypes.bfloat16)
    return high, low


def spanwise_tables():
    cells = np.arange(NZ)
    table = np.zeros((NZ, NZ))
    eigen = np.zeros((NZ // 2, 2))
    slope = np.zeros((NZ // 2, 2))
    for pair in range(NZ // 2):
        if pair == 0:
            table[0] = 1.0 / math.sqrt(NZ)
            table[1] = np.cos(math.pi * cells) / math.sqrt(NZ)
            eigen[0] = (0.0, 4.0)
            continue
        angle = 2.0 * math.pi * (cells * pair % NZ) / NZ
        table[2 * pair] = np.cos(angle) * math.sqrt(2.0 / NZ)
        table[2 * pair + 1] = np.sin(angle) * math.sqrt(2.0 / NZ)
        eigen[pair] = 4.0 * math.sin(math.pi * pair / NZ) ** 2
        wave = math.sin(2.0 * math.pi * pair / NZ)
        slope[pair] = (wave, -wave)
    return table, eigen, slope


def stream_tables():
    cells = np.arange(LANES)
    weights = np.zeros((4, 2 * LANES, 2 * LANES))
    eigen = np.zeros((8, 2, 64))
    slope = np.zeros((8, 2, 64))
    for tile in range(8):
        group = tile // 2
        base = (0, 4)[tile] if group == 0 else group
        first = 0 if group == 0 else 64 * (tile % 2)
        for slot in range(64):
            wave = 8 * (first + slot) + base
            at = (tile % 2) * LANES + slot
            angle = 2.0 * math.pi * (cells * wave % NX) / NX
            scale = math.sqrt(2.0 / NX)
            if wave == 0:
                alternate = np.cos(math.pi * cells)
                weights[0, :LANES, at] = 1.0 / math.sqrt(NX)
                weights[0, :LANES, at + 64] = alternate / math.sqrt(NX)
                eigen[tile, :, slot] = (0.0, 4.0)
                continue
            eigen[tile, :, slot] = 4.0 * math.sin(math.pi * wave / NX) ** 2
            rise = math.sin(2.0 * math.pi * wave / NX)
            slope[tile, :, slot] = (rise, -rise)
            cos, sin = scale * np.cos(angle), scale * np.sin(angle)
            if group == 0:
                rows = slice((tile % 2) * LANES, (tile % 2 + 1) * LANES)
                weights[0, rows, at] = cos
                weights[0, rows, at + 64] = sin
            else:
                weights[group, :LANES, at] = cos
                weights[group, LANES:, at] = -sin
                weights[group, :LANES, at + 64] = sin
                weights[group, LANES:, at + 64] = cos
    columns = np.stack([eigen.reshape(8, LANES), slope.reshape(8, LANES)])
    return weights, columns.astype(np.float32)


def block_tables():
    order = np.arange(1, ROWS + 1)
    sine = np.sin(math.pi * np.outer(order, order) / (ROWS + 1))
    sine = sine * math.sqrt(2.0 / (ROWS + 1))
    shift = np.eye(ROWS, k=1)
    slope = 0.5 * (shift - shift.T)
    eigen = 2.0 - 2.0 * np.cos(math.pi * order / (ROWS + 1))
    rows = np.concatenate([np.arange(0, ROWS, 2), np.arange(1, ROWS, 2)])
    marks = np.stack([eigen, sine[:, 0], sine[:, ROWS - 1]])
    marks = np.broadcast_to(marks[:, :, None], (3, ROWS, LANES)).astype(np.float32)
    lift = sine @ slope @ sine
    tables = np.stack([sine[:, rows], (sine @ slope)[:, rows], lift, sine[:, rows].T, lift.T])
    return np.stack(split(tables)), marks


def halves(x):
    high = x.astype(jnp.bfloat16)
    low = (x - high.astype(jnp.float32)).astype(jnp.bfloat16)
    return high, low


def dot(a, b):
    return jnp.dot(a, b, preferred_element_type=jnp.float32)


def times_table(x, high_table, low_table):
    high, low = halves(x)
    return dot(high, high_table) + (dot(low, high_table) + dot(high, low_table))


SINE, SINE_SLOPE, LIFT, SINE_BACK, LIFT_BACK = range(5)


def wall_times(ref, which, x):
    return table_times(ref[0, which], ref[1, which], x)


def table_times(high_table, low_table, x):
    high, low = halves(x)
    return dot(high_table, high) + (dot(high_table, low) + dot(low_table, high))


def lane_ids(rows):
    return lax.broadcasted_iota(jnp.int32, (rows, LANES), 1)


def copy_kernel(vec_ref, base_ref, first_ref, second_ref, sems):
    core = lax.axis_index("xs_1")
    copies = []
    for slot, ref in enumerate((first_ref, second_ref)):
        row = core if slot == 0 else 1 - core
        for field in range(4):
            copies.append((vec_ref.at[2, field, row], ref.at[field]))
            copies.append((base_ref.at[field, row], ref.at[4 + field]))
    copies = [
        pltpu.make_async_copy(source, target, sems.at[at])
        for at, (source, target) in enumerate(copies)
    ]
    for copy in copies:
        copy.start()
    for copy in copies:
        copy.wait()


def edges_kernel(
    diff_ref, first_ref, second_ref, marks_ref, stream_ref, span_ref, wall_ref,
    low_x, high_x, inverse_ref, gain_ref, share_ref, coef_ref, slope_ref, joint_ref,
):
    lanes = lane_ids(NZ)
    low = jnp.zeros((NZ, LANES), jnp.float32)
    high = jnp.zeros((NZ, LANES), jnp.float32)
    for field in range(8):
        for slot, ref in enumerate((first_ref, second_ref)):
            block = ref[field]
            at = 2 * field + slot
            low = jnp.where(lanes == at, pltpu.roll(block, at, 1), low)
            high = jnp.where(lanes == at, pltpu.roll(block, (at + 1) % LANES, 1), high)
    low_x[...] = low
    high_x[...] = high

    slot = lax.axis_index("wall_1") * 8 + lax.axis_index("xs_0") * 2 + lax.axis_index("xs_1")
    span = span_ref[slot]
    column = stream_ref[0] + (span[0:1] + SCREENING)
    slope_ref[...] = jnp.broadcast_to(span[1:2], (LINES, LANES))
    eigen, head, tail = marks_ref[0], marks_ref[1], marks_ref[2]
    shifts = [1.0 / (jnp.zeros((LINES, LANES), jnp.float32) + diff_ref[f]) for f in range(4)]
    gains = []
    for field in range(4):
        shift = jnp.concatenate([shifts[field]] * 2, axis=0)
        share = 1.0 / (eigen + shift)
        gains.append(shift * share)
        share_ref[field] = share
        gain_ref[field] = gains[field]
    head_lift = wall_times(wall_ref, LIFT_BACK, head * gains[1])
    tail_lift = wall_times(wall_ref, LIFT_BACK, tail * gains[1])
    weights = [
        gains[0] * head * head, gains[0] * head * tail,
        gains[2] * head * head, gains[2] * head * tail,
        head_lift * head, head_lift * tail, tail_lift * head, tail_lift * tail,
        head * head, head * tail,
    ]
    for tile in range(BLOCKS):
        inverse = 1.0 / (eigen + column[tile : tile + 1])
        inverse_ref[:, LANES * tile : LANES * (tile + 1)] = inverse
        for at, weight in enumerate(weights):
            coef_ref[at, tile : tile + 1] = jnp.sum(weight * inverse, axis=0, keepdims=True)
    coef_ref[10] = 0.5 * shifts[1]

    shift = jnp.concatenate([column] + shifts, axis=0)
    root = jnp.sqrt(shift * (shift + 4.0))
    decay = 2.0 / (2.0 + shift + root)
    two = decay * decay
    four = two * two
    eight = four * four
    sixteen = eight * eight
    powers = [jnp.ones_like(decay)]
    for _ in range(8):
        powers.append(powers[-1] * (sixteen * sixteen))
    joint_ref[0] = decay
    joint_ref[1] = eight * four * two * decay
    joint_ref[2] = sixteen
    joint_ref[3] = 1.0 / (root * (1.0 - powers[8] * two))
    for b in range(1, 8):
        joint_ref[4 * b] = 1.0 - powers[b]
        joint_ref[4 * b + 1] = 1.0 - powers[b] * two
        joint_ref[4 * b + 2] = 1.0 - powers[8 - b] * two
        joint_ref[4 * b + 3] = 1.0 - powers[8 - b]


def advect_kernel(
    first_ref, second_ref, left_ref, right_ref, inner_ref, outer_ref, table_ref,
    out_ref,
):
    lanes = lane_ids(NZ)
    first, last = lanes == 0, lanes == LANES - 1
    left, right = left_ref[...], right_ref[...]
    core = lax.axis_index("xs_1")
    half = jnp.where(core == 0, 0.5, -0.5)

    def value(field, slot):
        return (first_ref, second_ref)[slot][field]

    def slopes(field, slot):
        x = value(field, slot)
        at = 2 * field + 1 - slot
        up = jnp.where(last, pltpu.roll(right, (LANES - 1 - at) % LANES, 1), pltpu.roll(x, LANES - 1, 1))
        down = jnp.where(first, pltpu.roll(left, (LANES - at) % LANES, 1), pltpu.roll(x, 1, 1))
        along_x = (up - down) * 0.5
        if slot == 0:
            along_y = (value(field, 1) - outer_ref[field]) * half
        else:
            along_y = (inner_ref[field] - value(field, 0)) * half
        along_z = (pltpu.roll(x, NZ - 1, 0) - pltpu.roll(x, 1, 0)) * 0.5
        return along_x, along_y, along_z

    for field in range(4):
        updated = []
        for slot in range(2):
            grad = slopes(field, slot)
            base_grad = slopes(field + 4, slot)
            advect = jnp.zeros((NZ, LANES), jnp.float32)
            for axis in range(3):
                advect += value(4 + axis, slot) * grad[axis]
                advect += value(axis, slot) * base_grad[axis]
            result = value(field, slot) - ADV_STEP * advect
            if field == 1:
                result += BUOYANCY * value(3, slot)
            updated.append(result)
        rows = (
            jnp.where(core == 0, updated[0], updated[1]),
            jnp.where(core == 0, updated[1], updated[0]),
        )
        if field < 3:
            kind = field // 2
            modes = table_times(table_ref[0, kind], table_ref[1, kind], jnp.concatenate(rows, axis=1))
            rows = (modes[:, :LANES], modes[:, LANES:])
        for row in range(2):
            out_ref[pl.ds(2 * field + row, NZ, stride=LINES), :] = rows[row]


def lanes_of(x, tile):
    return x[:, LANES * tile : LANES * (tile + 1)]


def side_by_side(parts):
    return jnp.concatenate(parts, axis=1)


def stream_kernel(
    in_ref, table_ref, wall_ref, marks_ref, stream_ref, inverse_ref, gain_ref, coef_ref, slope_ref,
    waves_ref, pressure_ref, out_ref,
):
    def lines(part, s):
        return in_ref[pl.ds(LINES * s + part, LINES, stride=NZ), :]

    x = [jnp.concatenate([lines(part, s) for part in range(6)], axis=0) for s in range(BLOCKS)]
    s04, d04 = x[0] + x[4], x[0] - x[4]
    s26, d26 = x[2] + x[6], x[2] - x[6]
    s15, d15 = x[1] + x[5], x[1] - x[5]
    s37, d37 = x[3] + x[7], x[3] - x[7]
    even, odd = s04 + s26, s15 + s37
    minus, plus = HALF * (d15 - d37), HALF * (d15 + d37)
    parts = [
        (even + odd, even - odd),
        (d04 + minus, plus + d26),
        (s04 - s26, s15 - s37),
        (d04 - minus, plus - d26),
    ]
    modes = side_by_side(
        [times_table(side_by_side(parts[g]), table_ref[0, g], table_ref[1, g]) for g in range(4)]
    )
    heat = side_by_side(
        [jnp.concatenate([lines(6, s), lines(7, s)], axis=0) for s in range(BLOCKS)]
    )
    fields = [modes[ROWS * f : ROWS * (f + 1)] for f in range(3)] + [heat]
    waves = wall_times(wall_ref, SINE, side_by_side(fields))
    waves_ref[...] = waves
    rise = wall_times(wall_ref, SINE_SLOPE, fields[1])
    head, tail = marks_ref[1], marks_ref[2]
    span = slope_ref[0:1, :]

    def wave(field, tile):
        return lanes_of(waves, BLOCKS * field + tile)

    pressure = []
    for tile in range(BLOCKS):
        slope = stream_ref[1, tile : tile + 1]
        source = slope * pltpu.roll(wave(0, tile), 64, 1) + lanes_of(rise, tile)
        source += span * wave(2, tile)
        pressure.append(-lanes_of(inverse_ref, tile) * source)
    joined = side_by_side(pressure)
    pressure_ref[...] = joined
    lift = wall_times(wall_ref, LIFT, joined)

    def ends(f):
        return (
            jnp.sum(f * tail, axis=0, keepdims=True), jnp.sum(f * head, axis=0, keepdims=True)
        )

    for tile in range(BLOCKS):
        p = pressure[tile]
        last, first = ends(p)
        half = coef_ref[10, tile : tile + 1]
        rows = lanes_of(fields[1], tile)
        values = [(last + 0.5 * rows[ROWS - 1 :], first - 0.5 * rows[:1])]
        slope = stream_ref[1, tile : tile + 1]
        corrected = (
            wave(0, tile) - slope * pltpu.roll(p, 64, 1),
            wave(1, tile) - lanes_of(lift, tile),
            wave(2, tile) + span * p,
            wave(3, tile),
        )
        for field in range(4):
            high, low = ends(gain_ref[field] * corrected[field])
            if field == 1:
                high, low = high + half * last, low - half * first
            values.append((high, low))
        for at, (high, low) in enumerate(values):
            out_ref[0, LINES * at + tile : LINES * at + tile + 1] = high
            out_ref[0, 40 + LINES * at + tile : 40 + LINES * at + tile + 1] = low
    for b in range(1, 8):
        out_ref[b] = out_ref[0]


def joints(joint_ref, rows, highs, lows):
    def coef(at):
        return joint_ref[at, rows]

    decay, fifteen, sixteen, scale = (coef(at) for at in range(4))
    ahead, behind = [None] * 9, [None] * 9
    ahead[1] = jnp.zeros_like(decay)
    for b in range(2, 8):
        ahead[b] = sixteen * (ahead[b - 1] + coef(4 * b - 4) * lows[b - 1])
        ahead[b] += fifteen * (coef(4 * b - 3) * highs[b - 2])
    behind[7] = jnp.zeros_like(decay)
    for b in range(6, 0, -1):
        behind[b] = sixteen * (behind[b + 1] + coef(4 * b + 7) * highs[b])
        behind[b] += fifteen * (coef(4 * b + 6) * lows[b + 1])
    alpha, beta = [jnp.zeros_like(decay)], []
    for b in range(1, 8):
        left_u, right_u, left_w, right_w = (coef(4 * b + at) for at in range(4))
        before = ahead[b] + left_u * lows[b]
        after = behind[b] + right_w * highs[b - 1]
        alpha.append(highs[b - 1] + scale * (left_w * before + left_u * decay * after))
        late = right_w * highs[b - 1] + behind[b]
        beta.append(lows[b] + scale * (decay * right_w * before + right_u * late))
    beta.append(jnp.zeros_like(decay))
    return alpha, beta


def stream_back_kernel(
    in_ref, waves_ref, pressure_ref, table_ref, wall_ref, marks_ref, stream_ref, inverse_ref, gain_ref, share_ref, coef_ref, slope_ref, joint_ref,
    out_ref, alpha_ref, beta_ref,
):
    head, tail = marks_ref[1], marks_ref[2]
    span = slope_ref[0:1, :]
    alpha, beta = joints(
        joint_ref, pl.ds(0, 8), [in_ref[b, :8] for b in range(8)], [in_ref[b, 40:48] for b in range(8)]
    )
    coef = [coef_ref[at] for at in range(11)]
    slope = stream_ref[1]
    highs, lows = [], []
    for b in range(8):
        one, two = alpha[b], beta[b]
        one_x, two_x = slope * pltpu.roll(one, 64, 1), slope * pltpu.roll(two, 64, 1)
        one_z, two_z = span * one, span * two
        high = [
            -(one_x * coef[1] + two_x * coef[0]),
            coef[10] * (one * coef[9] + two * coef[8]) - (one * coef[6] + two * coef[7]),
            one_z * coef[3] + two_z * coef[2],
            jnp.zeros_like(one),
        ]
        low = [
            -(one_x * coef[0] + two_x * coef[1]),
            -coef[10] * (one * coef[8] + two * coef[9]) - (one * coef[4] + two * coef[5]),
            one_z * coef[2] + two_z * coef[3],
            jnp.zeros_like(one),
        ]
        highs.append(in_ref[b, 8:40] + jnp.concatenate(high, axis=0))
        lows.append(in_ref[b, 48:80] + jnp.concatenate(low, axis=0))
    alphas, betas = joints(joint_ref, pl.ds(8, 32), highs, lows)
    for b in range(8):
        alpha_ref[b, :8] = alpha[b]
        beta_ref[b, :8] = beta[b]
        alpha_ref[b, 8:] = alphas[b]
        beta_ref[b, 8:] = betas[b]
    own = lax.axis_index("wall_0")

    def outside(field, tile):
        at = LINES * field + tile
        return alpha_ref[own, at : at + 1] * head + beta_ref[own, at : at + 1] * tail

    def wave(field, tile):
        return lanes_of(waves_ref, BLOCKS * field + tile)

    pressure = [
        lanes_of(pressure_ref, tile) + lanes_of(inverse_ref, tile) * outside(0, tile)
        for tile in range(BLOCKS)
    ]
    lift = wall_times(wall_ref, LIFT, side_by_side(pressure))
    solved = [[], [], [], []]
    for tile in range(BLOCKS):
        p = pressure[tile]
        corrected = (
            wave(0, tile) - stream_ref[1, tile : tile + 1] * pltpu.roll(p, 64, 1),
            wave(1, tile) - lanes_of(lift, tile),
            wave(2, tile) + span * p,
            wave(3, tile),
        )
        for field in range(4):
            value = gain_ref[field] * corrected[field]
            solved[field].append(value + share_ref[field] * outside(field + 1, tile))
    rows = wall_times(wall_ref, SINE_BACK, side_by_side(sum(solved, [])))
    fields = [rows[:, NX * f : NX * (f + 1)] for f in range(4)]
    modes = jnp.concatenate(fields[:3], axis=0)
    parts = []
    for group in range(4):
        cells = times_table(
            modes[:, 2 * LANES * group : 2 * LANES * (group + 1)],
            table_ref[0, group], table_ref[1, group],
        )
        parts.append((cells[:, :LANES], cells[:, LANES:]))
    (c0, c4), (c1, s1), (c2, s2), (c3, s3) = parts
    sum04, dif04 = c0 + c4, c0 - c4
    sum13, dif13 = c1 + c3, HALF * (c1 - c3)
    plus13, minus13 = HALF * (s1 + s3), s1 - s3
    outer_a, outer_b = sum04 + c2, sum04 - c2
    inner_a, inner_b = dif04 + s2, dif04 - s2
    cells = [
        outer_a + sum13,
        inner_a + (dif13 + plus13),
        outer_b + minus13,
        inner_b + (plus13 - dif13),
        outer_a - sum13,
        inner_a - (dif13 + plus13),
        outer_b - minus13,
        inner_b - (plus13 - dif13),
    ]
    for s in range(BLOCKS):
        for part in range(8):
            if part < 6:
                value = cells[s][LINES * part : LINES * (part + 1)]
            else:
                value = lanes_of(fields[3], s)[LINES * (part - 6) : LINES * (part - 5)]
            out_ref[pl.ds(LINES * s + part, LINES, stride=NZ), :] = value


PAIRS = ((0, 0), (0, 1), (0, 2), (1, 1), (1, 2), (2, 2))


def folded(x):
    total = x[:LINES]
    for part in range(1, NZ // LINES):
        total += x[LINES * part : LINES * (part + 1)]
    return total


def cells_kernel(in_ref, vec_ref, table_ref, cur_ref, sums_ref):
    sums = [jnp.zeros((LINES, LANES), jnp.float32) for _ in range(10)]
    for field in range(4):
        for row in range(2):
            part = 2 * field + row
            cells = in_ref[pl.ds(part, NZ, stride=LINES), :]
            if field < 3:
                cells = table_times(table_ref[0, field // 2], table_ref[1, field // 2], cells)
            cur_ref[field, row] = cells
            vectors = [vec_ref[q, field, row] for q in range(3)]
            for q in range(3):
                sums[q] += folded(vectors[q] * cells)
            sums[3] += folded(cells * cells)
            for at, (q, p) in enumerate(PAIRS):
                sums[4 + at] += folded(vectors[q] * vectors[p])
    lanes = lane_ids(16)
    packed = jnp.zeros((16, LANES), jnp.float32)
    for at in range(10):
        packed = jnp.where(lanes == at, jnp.sum(sums[at]), packed)
    sums_ref[...] = packed


def residual_kernel(sums_ref, cur_ref, vec_ref, out_ref, hess_ref):
    entries = float(4 * NX * NY * NZ)
    totals = jnp.sum(sums_ref[...], axis=0, keepdims=True) * (1.0 / entries)
    lanes = lane_ids(1)

    def pick(at):
        return jnp.sum(jnp.where(lanes == at, totals, 0.0), axis=1, keepdims=True)

    values = [pick(at) for at in range(10)]
    products = values[:3]
    square = values[3]
    for q in range(3):
        square = square - 2.0 * products[q] * products[q]
    for at, (q, p) in enumerate(PAIRS):
        twice = 1.0 if q == p else 2.0
        square = square + twice * products[q] * products[p] * values[4 + at]
    norm = jnp.sqrt(square + EPSILON)
    for q in range(3):
        hess_ref[q] = jnp.sum(products[q])
    hess_ref[3] = jnp.sum(norm)
    scale = 1.0 / norm
    for field in range(4):
        for row in range(2):
            left = cur_ref[field, row]
            for q in range(3):
                left = left - products[q] * vec_ref[q, field, row]
            out_ref[field, row] = left * scale


VMEM = pl.BlockSpec(memory_space=pltpu.VMEM)
SMALL = pltpu.CompilerParams(vmem_limit_bytes=8 * 1024 * 1024)
LARGE = pltpu.CompilerParams(vmem_limit_bytes=54500 * 1024)
SMEM = pl.BlockSpec(memory_space=pltpu.SMEM)


def f32(*dims):
    return jax.ShapeDtypeStruct(dims, jnp.float32)


def shards(krylov_basis, base_state, diffusivity):
    span, span_eigen, span_slope = spanwise_tables()
    span = np.stack([span, span[np.arange(NZ) ^ 1]])
    span_columns = np.stack([span_eigen.reshape(-1), span_slope.reshape(-1)], axis=1)
    span_columns = np.broadcast_to(span_columns[:, :, None], (NZ, 2, LANES)).astype(np.float32)
    stream, stream_columns = stream_tables()
    wall, marks = block_tables()
    span, stream = np.stack(split(span)), np.stack(split(stream))

    rows = f32(8, NZ, LANES)
    first, second = pl.pallas_call(
        copy_kernel,
        in_specs=[pl.BlockSpec(memory_space=pltpu.HBM)] * 2,
        out_specs=[VMEM] * 2,
        out_shape=[rows, rows],
        scratch_shapes=[pltpu.SemaphoreType.DMA((16,))],
        compiler_params=LARGE,
        name="copy",
    )(krylov_basis, base_state)
    size, walls = lax.axis_size(XS), lax.axis_size(WALL)
    down = [[(size * (i + 1) + s, size * i + s) for i in range(walls - 1)] for s in range(size)]
    up = [[(b, a) for a, b in pairs] for pairs in down]
    inner = lax.ppermute(first, WALL + XS, sum([(down, up)[s % 2][s] for s in range(size)], []))
    outer = lax.ppermute(second, WALL + XS, sum([(up, down)[s % 2][s] for s in range(size)], []))
    low_x, high_x, inverse, gain, share, coef, slope, joint = pl.pallas_call(
        edges_kernel,
        in_specs=[SMEM] + [VMEM] * 6,
        out_specs=[VMEM] * 8,
        out_shape=[
            f32(NZ, LANES), f32(NZ, LANES), f32(ROWS, NX), f32(4, ROWS, LANES),
            f32(4, ROWS, LANES), f32(11, LINES, LANES), f32(LINES, LANES), f32(32, 40, LANES),
        ],
        compiler_params=SMALL,
        name="edges",
    )(
        diffusivity, first, second, marks, stream_columns, span_columns, wall
    )
    right = lax.ppermute(low_x, XS, [((i + 1) % size, i) for i in range(size)])
    left = lax.ppermute(high_x, XS, [(i, (i + 1) % size) for i in range(size)])

    plane = ("wall_1",) + XS
    modes = pl.pallas_call(
        advect_kernel,
        in_specs=[VMEM] * 7,
        out_specs=VMEM,
        out_shape=f32(NZ * LINES, LANES),
        compiler_params=SMALL,
        name="advect",
    )(first, second, left, right, inner, outer, span)
    lines = lax.all_to_all(modes.reshape(NZ, LINES, LANES), plane, 0, 0, tiled=True)
    waves, pressure, ends = pl.pallas_call(
        stream_kernel,
        in_specs=[VMEM] * 9,
        out_specs=[VMEM] * 3,
        out_shape=[f32(ROWS, 4 * NX), f32(ROWS, NX), f32(8, 80, LANES)],
        compiler_params=SMALL,
        name="stream",
    )(
        lines.reshape(-1, LANES), stream, wall, marks, stream_columns, inverse, gain, coef, slope
    )
    ends = lax.all_to_all(ends, "wall_0", 0, 0, tiled=True)
    lines = pl.pallas_call(
        stream_back_kernel,
        in_specs=[VMEM] * 13,
        out_specs=VMEM,
        out_shape=f32(NZ * LINES, LANES),
        scratch_shapes=[pltpu.VMEM((8, 40, LANES), jnp.float32)] * 2,
        compiler_params=SMALL,
        name="stream_back",
    )(
        ends, waves, pressure, stream.transpose(0, 1, 3, 2), wall, marks, stream_columns,
        inverse, gain, share, coef, slope, joint,
    )
    modes = lax.all_to_all(lines.reshape(NZ, LINES, LANES), plane, 0, 0, tiled=True)
    current, sums = pl.pallas_call(
        cells_kernel,
        in_specs=[VMEM] * 3,
        out_specs=[VMEM] * 2,
        out_shape=[f32(4, 2, NZ, LANES), f32(16, LANES)],
        compiler_params=SMALL,
        name="cells",
    )(modes.reshape(-1, LANES), krylov_basis, span.transpose(0, 1, 3, 2))
    sums = lax.all_to_all(sums, ("wall_0", "xs_1"), 0, 0, tiled=True).sum(axis=0)
    sums = jnp.broadcast_to(sums, (32, LANES))
    sums = lax.all_to_all(sums, ("wall_1", "xs_0"), 0, 0, tiled=True)
    new_vector, hessenberg = pl.pallas_call(
        residual_kernel,
        in_specs=[VMEM] * 3,
        out_specs=[VMEM, SMEM],
        out_shape=[f32(4, 2, NZ, LANES), f32(4)],
        compiler_params=SMALL,
        name="residual",
    )(sums, current, krylov_basis)
    return new_vector, hessenberg


def solution(mesh):
    torus = Mesh(mesh.devices.reshape(8, 8, 4, 2), ("wall_0", "wall_1", "xs_0", "xs_1"))
    return jax.shard_map(
        shards,
        mesh=torus,
        in_specs=(P(None, None, WALL, None, XS), P(None, WALL, None, XS), P()),
        out_specs=(P(None, WALL, None, XS), P()),
        check_vma=False,
    )
```

```python
import math

import jax
import jax.numpy as jnp
import ml_dtypes
import numpy as np
from jax import lax
from jax.experimental import pallas as pl
from jax.experimental.pallas import tpu as pltpu
from jax.sharding import Mesh
from jax.sharding import PartitionSpec as P

WALL = ("wall_0", "wall_1")
XS = ("xs_0", "xs_1")

ADV_STEP = 0.2
BUOYANCY = 0.5
SCREENING = 0.004
EPSILON = 1e-06

NX, NY, NZ = 1024, 128, 64
LINES, LANES, BLOCKS = 8, 128, 8
ROWS = 16
HALF = math.sqrt(0.5)


def split(table):
    high = table.astype(ml_dtypes.bfloat16)
    low = (table - high.astype(np.float64)).astype(ml_dtypes.bfloat16)
    return high, low


def spanwise_tables():
    cells = np.arange(NZ)
    table = np.zeros((NZ, NZ))
    eigen = np.zeros((NZ // 2, 2))
    slope = np.zeros((NZ // 2, 2))
    for pair in range(NZ // 2):
        if pair == 0:
            table[0] = 1.0 / math.sqrt(NZ)
            table[1] = np.cos(math.pi * cells) / math.sqrt(NZ)
            eigen[0] = (0.0, 4.0)
            continue
        angle = 2.0 * math.pi * (cells * pair % NZ) / NZ
        table[2 * pair] = np.cos(angle) * math.sqrt(2.0 / NZ)
        table[2 * pair + 1] = np.sin(angle) * math.sqrt(2.0 / NZ)
        eigen[pair] = 4.0 * math.sin(math.pi * pair / NZ) ** 2
        wave = math.sin(2.0 * math.pi * pair / NZ)
        slope[pair] = (wave, -wave)
    return table, eigen, slope


def stream_tables():
    cells = np.arange(LANES)
    weights = np.zeros((4, 2 * LANES, 2 * LANES))
    eigen = np.zeros((8, 2, 64))
    slope = np.zeros((8, 2, 64))
    for tile in range(8):
        group = tile // 2
        base = (0, 4)[tile] if group == 0 else group
        first = 0 if group == 0 else 64 * (tile % 2)
        for slot in range(64):
            wave = 8 * (first + slot) + base
            at = (tile % 2) * LANES + slot
            angle = 2.0 * math.pi * (cells * wave % NX) / NX
            scale = math.sqrt(2.0 / NX)
            if wave == 0:
                alternate = np.cos(math.pi * cells)
                weights[0, :LANES, at] = 1.0 / math.sqrt(NX)
                weights[0, :LANES, at + 64] = alternate / math.sqrt(NX)
                eigen[tile, :, slot] = (0.0, 4.0)
                continue
            eigen[tile, :, slot] = 4.0 * math.sin(math.pi * wave / NX) ** 2
            rise = math.sin(2.0 * math.pi * wave / NX)
            slope[tile, :, slot] = (rise, -rise)
            cos, sin = scale * np.cos(angle), scale * np.sin(angle)
            if group == 0:
                rows = slice((tile % 2) * LANES, (tile % 2 + 1) * LANES)
                weights[0, rows, at] = cos
                weights[0, rows, at + 64] = sin
            else:
                weights[group, :LANES, at] = cos
                weights[group, LANES:, at] = -sin
                weights[group, :LANES, at + 64] = sin
                weights[group, LANES:, at + 64] = cos
    columns = np.stack([eigen.reshape(8, LANES), slope.reshape(8, LANES)])
    return weights, columns.astype(np.float32)


def block_tables():
    order = np.arange(1, ROWS + 1)
    sine = np.sin(math.pi * np.outer(order, order) / (ROWS + 1))
    sine = sine * math.sqrt(2.0 / (ROWS + 1))
    shift = np.eye(ROWS, k=1)
    slope = 0.5 * (shift - shift.T)
    eigen = 2.0 - 2.0 * np.cos(math.pi * order / (ROWS + 1))
    rows = np.concatenate([np.arange(0, ROWS, 2), np.arange(1, ROWS, 2)])
    marks = np.stack([eigen, sine[:, 0], sine[:, ROWS - 1]])
    marks = np.broadcast_to(marks[:, :, None], (3, ROWS, LANES)).astype(np.float32)
    lift = sine @ slope @ sine
    tables = np.stack([sine[:, rows], (sine @ slope)[:, rows], lift, sine[:, rows].T, lift.T])
    return np.stack(split(tables)), marks


def halves(x):
    high = x.astype(jnp.bfloat16)
    low = (x - high.astype(jnp.float32)).astype(jnp.bfloat16)
    return high, low


def dot(a, b):
    return jnp.dot(a, b, preferred_element_type=jnp.float32)


def times_table(x, high_table, low_table):
    high, low = halves(x)
    return dot(high, high_table) + (dot(low, high_table) + dot(high, low_table))


SINE, SINE_SLOPE, LIFT, SINE_BACK, LIFT_BACK = range(5)


def wall_times(ref, which, x):
    return table_times(ref[0, which], ref[1, which], x)


def table_times(high_table, low_table, x):
    high, low = halves(x)
    return dot(high_table, high) + (dot(high_table, low) + dot(low_table, high))


def lane_ids(rows):
    return lax.broadcasted_iota(jnp.int32, (rows, LANES), 1)


def copy_kernel(vec_ref, base_ref, first_ref, second_ref, sems):
    core = lax.axis_index("xs_1")
    copies = []
    for slot, ref in enumerate((first_ref, second_ref)):
        row = core if slot == 0 else 1 - core
        for field in range(4):
            copies.append((vec_ref.at[2, field, row], ref.at[field]))
            copies.append((base_ref.at[field, row], ref.at[4 + field]))
    copies = [
        pltpu.make_async_copy(source, target, sems.at[at])
        for at, (source, target) in enumerate(copies)
    ]
    for copy in copies:
        copy.start()
    for copy in copies:
        copy.wait()


def edges_kernel(
    diff_ref, first_ref, second_ref, marks_ref, stream_ref, span_ref, wall_ref,
    low_x, high_x, inverse_ref, gain_ref, share_ref, coef_ref, slope_ref, joint_ref,
):
    lanes = lane_ids(NZ)
    low = jnp.zeros((NZ, LANES), jnp.float32)
    high = jnp.zeros((NZ, LANES), jnp.float32)
    for field in range(8):
        for slot, ref in enumerate((first_ref, second_ref)):
            block = ref[field]
            at = 2 * field + slot
            low = jnp.where(lanes == at, pltpu.roll(block, at, 1), low)
            high = jnp.where(lanes == at, pltpu.roll(block, (at + 1) % LANES, 1), high)
    low_x[...] = low
    high_x[...] = high

    slot = lax.axis_index("wall_1") * 8 + lax.axis_index("xs_0") * 2 + lax.axis_index("xs_1")
    span = span_ref[slot]
    column = stream_ref[0] + (span[0:1] + SCREENING)
    slope_ref[...] = jnp.broadcast_to(span[1:2], (LINES, LANES))
    eigen, head, tail = marks_ref[0], marks_ref[1], marks_ref[2]
    shifts = [1.0 / (jnp.zeros((LINES, LANES), jnp.float32) + diff_ref[f]) for f in range(4)]
    gains = []
    for field in range(4):
        shift = jnp.concatenate([shifts[field]] * 2, axis=0)
        share = 1.0 / (eigen + shift)
        gains.append(shift * share)
        share_ref[field] = share
        gain_ref[field] = gains[field]
    head_lift = wall_times(wall_ref, LIFT_BACK, head * gains[1])
    tail_lift = wall_times(wall_ref, LIFT_BACK, tail * gains[1])
    weights = [
        gains[0] * head * head, gains[0] * head * tail,
        gains[2] * head * head, gains[2] * head * tail,
        head_lift * head, head_lift * tail, tail_lift * head, tail_lift * tail,
        head * head, head * tail,
    ]
    for tile in range(BLOCKS):
        inverse = 1.0 / (eigen + column[tile : tile + 1])
        inverse_ref[:, LANES * tile : LANES * (tile + 1)] = inverse
        for at, weight in enumerate(weights):
            coef_ref[at, tile : tile + 1] = jnp.sum(weight * inverse, axis=0, keepdims=True)
    coef_ref[10] = 0.5 * shifts[1]

    shift = jnp.concatenate([column] + [part[:2] for part in shifts], axis=0)
    root = jnp.sqrt(shift * (shift + 4.0))
    decay = 2.0 / (2.0 + shift + root)
    two = decay * decay
    four = two * two
    eight = four * four
    sixteen = eight * eight
    powers = [jnp.ones_like(decay)]
    for _ in range(8):
        powers.append(powers[-1] * (sixteen * sixteen))
    scale = 1.0 / (root * (1.0 - powers[8] * two))
    none = jnp.zeros_like(decay)
    left_u, right_u = [none] * 9, [none] * 9
    left_w, right_w = [none] * 9, [none] * 9
    for b in range(1, 8):
        left_u[b], right_u[b] = 1.0 - powers[b], 1.0 - powers[b] * two
        left_w[b], right_w[b] = 1.0 - powers[8 - b] * two, 1.0 - powers[8 - b]
    for b in range(8):
        above = b + 1 if b < 7 else 8
        if b > 0:
            over_u, over_w = 1.0 / right_u[b], 1.0 / left_w[b]
            if b < 7:
                joint_ref[b + 1, 0] = sixteen * left_w[b + 1] * over_w
            if b > 1:
                joint_ref[b - 1, 1] = sixteen * right_u[b - 1] * over_u
            joint_ref[b, 2] = decay * left_u[b] * over_u
            joint_ref[b, 3] = decay * right_w[b] * over_w
        joint_ref[b, 4] = 1.0 + scale * decay * left_u[above] * right_w[above]
        joint_ref[b, 5] = scale * sixteen * left_u[b] * left_w[above]
        joint_ref[b, 6] = 1.0 + scale * decay * left_u[b] * right_w[b]
        joint_ref[b, 7] = scale * sixteen * right_u[b] * right_w[above]


def advect_kernel(
    first_ref, second_ref, left_ref, right_ref, inner_ref, outer_ref, table_ref,
    out_ref,
):
    lanes = lane_ids(NZ)
    first, last = lanes == 0, lanes == LANES - 1
    left, right = left_ref[...], right_ref[...]
    core = lax.axis_index("xs_1")
    half = jnp.where(core == 0, 0.5, -0.5)

    def value(field, slot):
        return (first_ref, second_ref)[slot][field]

    def slopes(field, slot):
        x = value(field, slot)
        at = 2 * field + 1 - slot
        up = jnp.where(last, pltpu.roll(right, (LANES - 1 - at) % LANES, 1), pltpu.roll(x, LANES - 1, 1))
        down = jnp.where(first, pltpu.roll(left, (LANES - at) % LANES, 1), pltpu.roll(x, 1, 1))
        along_x = (up - down) * 0.5
        if slot == 0:
            along_y = (value(field, 1) - outer_ref[field]) * half
        else:
            along_y = (inner_ref[field] - value(field, 0)) * half
        along_z = (pltpu.roll(x, NZ - 1, 0) - pltpu.roll(x, 1, 0)) * 0.5
        return along_x, along_y, along_z

    for field in range(4):
        updated = []
        for slot in range(2):
            grad = slopes(field, slot)
            base_grad = slopes(field + 4, slot)
            advect = jnp.zeros((NZ, LANES), jnp.float32)
            for axis in range(3):
                advect += value(4 + axis, slot) * grad[axis]
                advect += value(axis, slot) * base_grad[axis]
            result = value(field, slot) - ADV_STEP * advect
            if field == 1:
                result += BUOYANCY * value(3, slot)
            updated.append(result)
        rows = (
            jnp.where(core == 0, updated[0], updated[1]),
            jnp.where(core == 0, updated[1], updated[0]),
        )
        if field < 3:
            kind = field // 2
            modes = table_times(table_ref[0, kind], table_ref[1, kind], jnp.concatenate(rows, axis=1))
            rows = (modes[:, :LANES], modes[:, LANES:])
        for row in range(2):
            out_ref[pl.ds(2 * field + row, NZ, stride=LINES), :] = rows[row]


def lanes_of(x, tile):
    return x[:, LANES * tile : LANES * (tile + 1)]


def side_by_side(parts):
    return jnp.concatenate(parts, axis=1)


def stream_kernel(
    in_ref, table_ref, wall_ref, marks_ref, stream_ref, inverse_ref, gain_ref, coef_ref, slope_ref, joint_ref,
    waves_ref, pressure_ref, out_ref, local_ref, ends_ref,
):
    def lines(part, s):
        return in_ref[pl.ds(LINES * s + part, LINES, stride=NZ), :]

    x = [jnp.concatenate([lines(part, s) for part in range(6)], axis=0) for s in range(BLOCKS)]
    s04, d04 = x[0] + x[4], x[0] - x[4]
    s26, d26 = x[2] + x[6], x[2] - x[6]
    s15, d15 = x[1] + x[5], x[1] - x[5]
    s37, d37 = x[3] + x[7], x[3] - x[7]
    even, odd = s04 + s26, s15 + s37
    minus, plus = HALF * (d15 - d37), HALF * (d15 + d37)
    parts = [
        (even + odd, even - odd),
        (d04 + minus, plus + d26),
        (s04 - s26, s15 - s37),
        (d04 - minus, plus - d26),
    ]
    modes = side_by_side(
        [times_table(side_by_side(parts[g]), table_ref[0, g], table_ref[1, g]) for g in range(4)]
    )
    heat = side_by_side(
        [jnp.concatenate([lines(6, s), lines(7, s)], axis=0) for s in range(BLOCKS)]
    )
    fields = [modes[ROWS * f : ROWS * (f + 1)] for f in range(3)] + [heat]
    waves = wall_times(wall_ref, SINE, side_by_side(fields))
    waves_ref[...] = waves
    rise = wall_times(wall_ref, SINE_SLOPE, fields[1])
    head, tail = marks_ref[1], marks_ref[2]
    span = slope_ref[0:1, :]

    def wave(field, tile):
        return lanes_of(waves, BLOCKS * field + tile)

    pressure = []
    for tile in range(BLOCKS):
        slope = stream_ref[1, tile : tile + 1]
        source = slope * pltpu.roll(wave(0, tile), 64, 1) + lanes_of(rise, tile)
        source += span * wave(2, tile)
        pressure.append(-lanes_of(inverse_ref, tile) * source)
    joined = side_by_side(pressure)
    pressure_ref[...] = joined
    lift = wall_times(wall_ref, LIFT, joined)

    def ends(f):
        return (
            jnp.sum(f * tail, axis=0, keepdims=True), jnp.sum(f * head, axis=0, keepdims=True)
        )

    for tile in range(BLOCKS):
        p = pressure[tile]
        last, first = ends(p)
        half = coef_ref[10, tile : tile + 1]
        rows = lanes_of(fields[1], tile)
        values = [(last + 0.5 * rows[ROWS - 1 :], first - 0.5 * rows[:1])]
        slope = stream_ref[1, tile : tile + 1]
        corrected = (
            wave(0, tile) - slope * pltpu.roll(p, 64, 1),
            wave(1, tile) - lanes_of(lift, tile),
            wave(2, tile) + span * p,
            wave(3, tile),
        )
        for field in range(4):
            high, low = ends(gain_ref[field] * corrected[field])
            if field == 1:
                high, low = high + half * last, low - half * first
            values.append((high, low))
        for at, (high, low) in enumerate(values):
            ends_ref[0, LINES * at + tile : LINES * at + tile + 1] = high
            ends_ref[1, LINES * at + tile : LINES * at + tile + 1] = low
    own = lax.axis_index("wall_0")
    high, low = ends_ref[0], ends_ref[1]
    coefs = [joint_ref[own, at] for at in range(4, 8)]
    for system in range(5):
        part = slice(LINES * system, LINES * (system + 1))
        rows = slice(0, LINES) if system == 0 else slice(2 * system + 6, 2 * system + 7)
        up, down = high[part], low[part]
        upward = coefs[0][rows] * up + coefs[1][rows] * down
        downward = coefs[2][rows] * down + coefs[3][rows] * up
        if system > 0:
            local_ref[0, system - 1] = upward
            local_ref[1, system - 1] = downward
        for b in range(8):
            if system == 0:
                out_ref[b, 0] = upward
                out_ref[b, 1] = downward
            else:
                out_ref[b, system + 1] = jnp.where(own < b, upward, downward)


def joints(joint_ref, rows, upward, downward):
    rise, fall = [None, upward[0]], [None] * 7 + [downward[7]]
    for b in range(2, 8):
        rise.append(upward[b - 1] + joint_ref[b, 0, rows] * rise[b - 1])
    for b in range(6, 0, -1):
        fall[b] = downward[b] + joint_ref[b, 1, rows] * fall[b + 1]
    none = jnp.zeros_like(upward[0])
    alpha = [none] + [rise[b] + joint_ref[b, 2, rows] * fall[b] for b in range(1, 8)]
    beta = [fall[b] + joint_ref[b, 3, rows] * rise[b] for b in range(1, 8)] + [none]
    return alpha, beta


def stream_back_kernel(
    in_ref, local_ref, waves_ref, pressure_ref, table_ref, wall_ref, marks_ref, stream_ref, inverse_ref, gain_ref, share_ref, coef_ref, slope_ref, joint_ref,
    out_ref, alpha_ref, beta_ref,
):
    head, tail = marks_ref[1], marks_ref[2]
    span = slope_ref[0:1, :]
    alpha, beta = joints(
        joint_ref, pl.ds(0, 8), [in_ref[b, 0] for b in range(8)], [in_ref[b, 1] for b in range(8)]
    )
    own = lax.axis_index("wall_0")
    coef = [coef_ref[at] for at in range(11)]
    slope = stream_ref[1]
    upward, downward = [[], [], [], []], [[], [], [], []]
    for b in range(8):
        one, two = alpha[b], beta[b]
        one_x, two_x = slope * pltpu.roll(one, 64, 1), slope * pltpu.roll(two, 64, 1)
        one_z, two_z = span * one, span * two
        high = [
            -(one_x * coef[1] + two_x * coef[0]),
            coef[10] * (one * coef[9] + two * coef[8]) - (one * coef[6] + two * coef[7]),
            one_z * coef[3] + two_z * coef[2],
        ]
        low = [
            -(one_x * coef[0] + two_x * coef[1]),
            -coef[10] * (one * coef[8] + two * coef[9]) - (one * coef[4] + two * coef[5]),
            one_z * coef[2] + two_z * coef[3],
        ]
        for field in range(4):
            up, down = local_ref[0, field], local_ref[1, field]
            up = jnp.where(own == b, up, in_ref[b, field + 2])
            down = jnp.where(own == b, down, in_ref[b, field + 2])
            if field < 3:
                coefs = [joint_ref[b, at, pl.ds(8 + 2 * field, 1)] for at in range(4, 8)]
                up += coefs[0] * high[field] + coefs[1] * low[field]
                down += coefs[2] * low[field] + coefs[3] * high[field]
            upward[field].append(up)
            downward[field].append(down)
    pairs = [
        joints(joint_ref, pl.ds(8 + 2 * field, 1), upward[field], downward[field])
        for field in range(4)
    ]
    for b in range(8):
        for field in range(4):
            rows = slice(LINES * (field + 1), LINES * (field + 2))
            alpha_ref[b, rows] = pairs[field][0][b]
            beta_ref[b, rows] = pairs[field][1][b]
    for b in range(8):
        alpha_ref[b, :8] = alpha[b]
        beta_ref[b, :8] = beta[b]

    def outside(field, tile):
        at = LINES * field + tile
        return alpha_ref[own, at : at + 1] * head + beta_ref[own, at : at + 1] * tail

    def wave(field, tile):
        return lanes_of(waves_ref, BLOCKS * field + tile)

    pressure = [
        lanes_of(pressure_ref, tile) + lanes_of(inverse_ref, tile) * outside(0, tile)
        for tile in range(BLOCKS)
    ]
    lift = wall_times(wall_ref, LIFT, side_by_side(pressure))
    solved = [[], [], [], []]
    for tile in range(BLOCKS):
        p = pressure[tile]
        corrected = (
            wave(0, tile) - stream_ref[1, tile : tile + 1] * pltpu.roll(p, 64, 1),
            wave(1, tile) - lanes_of(lift, tile),
            wave(2, tile) + span * p,
            wave(3, tile),
        )
        for field in range(4):
            value = gain_ref[field] * corrected[field]
            solved[field].append(value + share_ref[field] * outside(field + 1, tile))
    rows = wall_times(wall_ref, SINE_BACK, side_by_side(sum(solved, [])))
    fields = [rows[:, NX * f : NX * (f + 1)] for f in range(4)]
    modes = jnp.concatenate(fields[:3], axis=0)
    parts = []
    for group in range(4):
        cells = times_table(
            modes[:, 2 * LANES * group : 2 * LANES * (group + 1)],
            table_ref[0, group], table_ref[1, group],
        )
        parts.append((cells[:, :LANES], cells[:, LANES:]))
    (c0, c4), (c1, s1), (c2, s2), (c3, s3) = parts
    sum04, dif04 = c0 + c4, c0 - c4
    sum13, dif13 = c1 + c3, HALF * (c1 - c3)
    plus13, minus13 = HALF * (s1 + s3), s1 - s3
    outer_a, outer_b = sum04 + c2, sum04 - c2
    inner_a, inner_b = dif04 + s2, dif04 - s2
    cells = [
        outer_a + sum13,
        inner_a + (dif13 + plus13),
        outer_b + minus13,
        inner_b + (plus13 - dif13),
        outer_a - sum13,
        inner_a - (dif13 + plus13),
        outer_b - minus13,
        inner_b - (plus13 - dif13),
    ]
    for s in range(BLOCKS):
        for part in range(8):
            if part < 6:
                value = cells[s][LINES * part : LINES * (part + 1)]
            else:
                value = lanes_of(fields[3], s)[LINES * (part - 6) : LINES * (part - 5)]
            out_ref[pl.ds(LINES * s + part, LINES, stride=NZ), :] = value


PAIRS = ((0, 0), (0, 1), (0, 2), (1, 1), (1, 2), (2, 2))


def folded(x):
    total = x[:LINES]
    for part in range(1, NZ // LINES):
        total += x[LINES * part : LINES * (part + 1)]
    return total


def cells_kernel(in_ref, vec_ref, table_ref, cur_ref, sums_ref):
    sums = [jnp.zeros((LINES, LANES), jnp.float32) for _ in range(10)]
    for field in range(4):
        for row in range(2):
            part = 2 * field + row
            cells = in_ref[pl.ds(part, NZ, stride=LINES), :]
            if field < 3:
                cells = table_times(table_ref[0, field // 2], table_ref[1, field // 2], cells)
            cur_ref[field, row] = cells
            vectors = [vec_ref[q, field, row] for q in range(3)]
            for q in range(3):
                sums[q] += folded(vectors[q] * cells)
            sums[3] += folded(cells * cells)
            for at, (q, p) in enumerate(PAIRS):
                sums[4 + at] += folded(vectors[q] * vectors[p])
    lanes = lane_ids(16)
    packed = jnp.zeros((16, LANES), jnp.float32)
    for at in range(10):
        packed = jnp.where(lanes == at, jnp.sum(sums[at]), packed)
    sums_ref[...] = packed


def residual_kernel(sums_ref, cur_ref, vec_ref, out_ref, hess_ref):
    entries = float(4 * NX * NY * NZ)
    totals = jnp.sum(sums_ref[...], axis=0, keepdims=True) * (1.0 / entries)
    lanes = lane_ids(1)

    def pick(at):
        return jnp.sum(jnp.where(lanes == at, totals, 0.0), axis=1, keepdims=True)

    values = [pick(at) for at in range(10)]
    products = values[:3]
    square = values[3]
    for q in range(3):
        square = square - 2.0 * products[q] * products[q]
    for at, (q, p) in enumerate(PAIRS):
        twice = 1.0 if q == p else 2.0
        square = square + twice * products[q] * products[p] * values[4 + at]
    norm = jnp.sqrt(square + EPSILON)
    for q in range(3):
        hess_ref[q] = jnp.sum(products[q])
    hess_ref[3] = jnp.sum(norm)
    scale = 1.0 / norm
    for field in range(4):
        for row in range(2):
            left = cur_ref[field, row]
            for q in range(3):
                left = left - products[q] * vec_ref[q, field, row]
            out_ref[field, row] = left * scale


VMEM = pl.BlockSpec(memory_space=pltpu.VMEM)
SMALL = pltpu.CompilerParams(vmem_limit_bytes=8 * 1024 * 1024)
LARGE = pltpu.CompilerParams(vmem_limit_bytes=54500 * 1024)
SMEM = pl.BlockSpec(memory_space=pltpu.SMEM)


def f32(*dims):
    return jax.ShapeDtypeStruct(dims, jnp.float32)


def shards(krylov_basis, base_state, diffusivity):
    span, span_eigen, span_slope = spanwise_tables()
    span = np.stack([span, span[np.arange(NZ) ^ 1]])
    span_columns = np.stack([span_eigen.reshape(-1), span_slope.reshape(-1)], axis=1)
    span_columns = np.broadcast_to(span_columns[:, :, None], (NZ, 2, LANES)).astype(np.float32)
    stream, stream_columns = stream_tables()
    wall, marks = block_tables()
    span, stream = np.stack(split(span)), np.stack(split(stream))

    rows = f32(8, NZ, LANES)
    first, second = pl.pallas_call(
        copy_kernel,
        in_specs=[pl.BlockSpec(memory_space=pltpu.HBM)] * 2,
        out_specs=[VMEM] * 2,
        out_shape=[rows, rows],
        scratch_shapes=[pltpu.SemaphoreType.DMA((16,))],
        compiler_params=LARGE,
        name="copy",
    )(krylov_basis, base_state)
    size, walls = lax.axis_size(XS), lax.axis_size(WALL)
    down = [[(size * (i + 1) + s, size * i + s) for i in range(walls - 1)] for s in range(size)]
    up = [[(b, a) for a, b in pairs] for pairs in down]
    inner = lax.ppermute(first, WALL + XS, sum([(down, up)[s % 2][s] for s in range(size)], []))
    outer = lax.ppermute(second, WALL + XS, sum([(up, down)[s % 2][s] for s in range(size)], []))
    low_x, high_x, inverse, gain, share, coef, slope, joint = pl.pallas_call(
        edges_kernel,
        in_specs=[SMEM] + [VMEM] * 6,
        out_specs=[VMEM] * 8,
        out_shape=[
            f32(NZ, LANES), f32(NZ, LANES), f32(ROWS, NX), f32(4, ROWS, LANES),
            f32(4, ROWS, LANES), f32(11, LINES, LANES), f32(LINES, LANES), f32(8, 8, ROWS, LANES),
        ],
        compiler_params=SMALL,
        name="edges",
    )(
        diffusivity, first, second, marks, stream_columns, span_columns, wall
    )
    right = lax.ppermute(low_x, XS, [((i + 1) % size, i) for i in range(size)])
    left = lax.ppermute(high_x, XS, [(i, (i + 1) % size) for i in range(size)])

    plane = ("wall_1",) + XS
    modes = pl.pallas_call(
        advect_kernel,
        in_specs=[VMEM] * 7,
        out_specs=VMEM,
        out_shape=f32(NZ * LINES, LANES),
        compiler_params=SMALL,
        name="advect",
    )(first, second, left, right, inner, outer, span)
    lines = lax.all_to_all(modes.reshape(NZ, LINES, LANES), plane, 0, 0, tiled=True)
    waves, pressure, ends, local = pl.pallas_call(
        stream_kernel,
        in_specs=[VMEM] * 10,
        out_specs=[VMEM] * 4,
        out_shape=[
            f32(ROWS, 4 * NX), f32(ROWS, NX), f32(8, 6, LINES, LANES), f32(2, 4, LINES, LANES)
        ],
        scratch_shapes=[pltpu.VMEM((2, 40, LANES), jnp.float32)],
        compiler_params=SMALL,
        name="stream",
    )(
        lines.reshape(-1, LANES), stream, wall, marks, stream_columns, inverse, gain, coef, slope,
        joint,
    )
    ends = lax.all_to_all(ends, "wall_0", 0, 0, tiled=True)
    lines = pl.pallas_call(
        stream_back_kernel,
        in_specs=[VMEM] * 14,
        out_specs=VMEM,
        out_shape=f32(NZ * LINES, LANES),
        scratch_shapes=[pltpu.VMEM((8, 40, LANES), jnp.float32)] * 2,
        compiler_params=SMALL,
        name="stream_back",
    )(
        ends, local, waves, pressure, stream.transpose(0, 1, 3, 2), wall, marks, stream_columns,
        inverse, gain, share, coef, slope, joint,
    )
    modes = lax.all_to_all(lines.reshape(NZ, LINES, LANES), plane, 0, 0, tiled=True)
    current, sums = pl.pallas_call(
        cells_kernel,
        in_specs=[VMEM] * 3,
        out_specs=[VMEM] * 2,
        out_shape=[f32(4, 2, NZ, LANES), f32(16, LANES)],
        compiler_params=SMALL,
        name="cells",
    )(modes.reshape(-1, LANES), krylov_basis, span.transpose(0, 1, 3, 2))
    sums = lax.all_to_all(sums, ("wall_0", "xs_1"), 0, 0, tiled=True).sum(axis=0)
    sums = jnp.broadcast_to(sums, (32, LANES))
    sums = lax.all_to_all(sums, ("wall_1", "xs_0"), 0, 0, tiled=True)
    new_vector, hessenberg = pl.pallas_call(
        residual_kernel,
        in_specs=[VMEM] * 3,
        out_specs=[VMEM, SMEM],
        out_shape=[f32(4, 2, NZ, LANES), f32(4)],
        compiler_params=SMALL,
        name="residual",
    )(sums, current, krylov_basis)
    return new_vector, hessenberg


def solution(mesh):
    torus = Mesh(mesh.devices.reshape(8, 8, 4, 2), ("wall_0", "wall_1", "xs_0", "xs_1"))
    return jax.shard_map(
        shards,
        mesh=torus,
        in_specs=(P(None, None, WALL, None, XS), P(None, WALL, None, XS), P()),
        out_specs=(P(None, WALL, None, XS), P()),
        check_vma=False,
    )
```

```python
import math

import jax
import jax.numpy as jnp
import ml_dtypes
import numpy as np
from jax import lax
from jax.experimental import pallas as pl
from jax.experimental.pallas import tpu as pltpu
from jax.sharding import Mesh
from jax.sharding import PartitionSpec as P

WALL = ("wall_0", "wall_1")
XS = ("xs_0", "xs_1")

ADV_STEP = 0.2
BUOYANCY = 0.5
SCREENING = 0.004
EPSILON = 1e-06

NX, NY, NZ = 1024, 128, 64
LINES, LANES, BLOCKS = 8, 128, 8
ROWS = 16
HALF = math.sqrt(0.5)


def split(table):
    high = table.astype(ml_dtypes.bfloat16)
    low = (table - high.astype(np.float64)).astype(ml_dtypes.bfloat16)
    return high, low


def spanwise_tables():
    cells = np.arange(NZ)
    table = np.zeros((NZ, NZ))
    eigen = np.zeros((NZ // 2, 2))
    slope = np.zeros((NZ // 2, 2))
    for pair in range(NZ // 2):
        if pair == 0:
            table[0] = 1.0 / math.sqrt(NZ)
            table[1] = np.cos(math.pi * cells) / math.sqrt(NZ)
            eigen[0] = (0.0, 4.0)
            continue
        angle = 2.0 * math.pi * (cells * pair % NZ) / NZ
        table[2 * pair] = np.cos(angle) * math.sqrt(2.0 / NZ)
        table[2 * pair + 1] = np.sin(angle) * math.sqrt(2.0 / NZ)
        eigen[pair] = 4.0 * math.sin(math.pi * pair / NZ) ** 2
        wave = math.sin(2.0 * math.pi * pair / NZ)
        slope[pair] = (wave, -wave)
    return table, eigen, slope


def stream_tables():
    cells = np.arange(LANES)
    weights = np.zeros((4, 2 * LANES, 2 * LANES))
    eigen = np.zeros((8, 2, 64))
    slope = np.zeros((8, 2, 64))
    for tile in range(8):
        group = tile // 2
        base = (0, 4)[tile] if group == 0 else group
        first = 0 if group == 0 else 64 * (tile % 2)
        for slot in range(64):
            wave = 8 * (first + slot) + base
            at = (tile % 2) * LANES + slot
            angle = 2.0 * math.pi * (cells * wave % NX) / NX
            scale = math.sqrt(2.0 / NX)
            if wave == 0:
                alternate = np.cos(math.pi * cells)
                weights[0, :LANES, at] = 1.0 / math.sqrt(NX)
                weights[0, :LANES, at + 64] = alternate / math.sqrt(NX)
                eigen[tile, :, slot] = (0.0, 4.0)
                continue
            eigen[tile, :, slot] = 4.0 * math.sin(math.pi * wave / NX) ** 2
            rise = math.sin(2.0 * math.pi * wave / NX)
            slope[tile, :, slot] = (rise, -rise)
            cos, sin = scale * np.cos(angle), scale * np.sin(angle)
            if group == 0:
                rows = slice((tile % 2) * LANES, (tile % 2 + 1) * LANES)
                weights[0, rows, at] = cos
                weights[0, rows, at + 64] = sin
            else:
                weights[group, :LANES, at] = cos
                weights[group, LANES:, at] = -sin
                weights[group, :LANES, at + 64] = sin
                weights[group, LANES:, at + 64] = cos
    columns = np.stack([eigen.reshape(8, LANES), slope.reshape(8, LANES)])
    return weights, columns.astype(np.float32)


def block_tables():
    order = np.arange(1, ROWS + 1)
    sine = np.sin(math.pi * np.outer(order, order) / (ROWS + 1))
    sine = sine * math.sqrt(2.0 / (ROWS + 1))
    shift = np.eye(ROWS, k=1)
    slope = 0.5 * (shift - shift.T)
    eigen = 2.0 - 2.0 * np.cos(math.pi * order / (ROWS + 1))
    rows = np.concatenate([np.arange(0, ROWS, 2), np.arange(1, ROWS, 2)])
    marks = np.stack([eigen, sine[:, 0], sine[:, ROWS - 1]])
    marks = np.broadcast_to(marks[:, :, None], (3, ROWS, LANES)).astype(np.float32)
    lift = sine @ slope @ sine
    tables = np.stack([sine[:, rows], (sine @ slope)[:, rows], lift, sine[:, rows].T, lift.T])
    return np.stack(split(tables)), marks


def halves(x):
    high = x.astype(jnp.bfloat16)
    low = (x - high.astype(jnp.float32)).astype(jnp.bfloat16)
    return high, low


def dot(a, b):
    return jnp.dot(a, b, preferred_element_type=jnp.float32)


def times_table(x, high_table, low_table):
    high, low = halves(x)
    return dot(high, high_table) + (dot(low, high_table) + dot(high, low_table))


SINE, SINE_SLOPE, LIFT, SINE_BACK, LIFT_BACK = range(5)


def wall_times(ref, which, x):
    return table_times(ref[0, which], ref[1, which], x)


def table_times(high_table, low_table, x):
    high, low = halves(x)
    return dot(high_table, high) + (dot(high_table, low) + dot(low_table, high))


def lane_ids(rows):
    return lax.broadcasted_iota(jnp.int32, (rows, LANES), 1)


def copy_kernel(vec_ref, base_ref, first_ref, second_ref, sems):
    core = lax.axis_index("xs_1")
    copies = []
    for slot, ref in enumerate((first_ref, second_ref)):
        row = core if slot == 0 else 1 - core
        for field in range(4):
            copies.append((vec_ref.at[2, field, row], ref.at[field]))
            copies.append((base_ref.at[field, row], ref.at[4 + field]))
    copies = [
        pltpu.make_async_copy(source, target, sems.at[at])
        for at, (source, target) in enumerate(copies)
    ]
    for copy in copies:
        copy.start()
    for copy in copies:
        copy.wait()


def edges_kernel(
    diff_ref, first_ref, second_ref, marks_ref, stream_ref, span_ref, wall_ref,
    low_x, high_x, inverse_ref, gain_ref, share_ref, coef_ref, slope_ref, joint_ref,
):
    lanes = lane_ids(NZ)
    low = jnp.zeros((NZ, LANES), jnp.float32)
    high = jnp.zeros((NZ, LANES), jnp.float32)
    for field in range(8):
        for slot, ref in enumerate((first_ref, second_ref)):
            block = ref[field]
            at = 2 * field + slot
            low = jnp.where(lanes == at, pltpu.roll(block, at, 1), low)
            high = jnp.where(lanes == at, pltpu.roll(block, (at + 1) % LANES, 1), high)
    low_x[...] = low
    high_x[...] = high

    slot = lax.axis_index("wall_1") * 8 + lax.axis_index("xs_0") * 2 + lax.axis_index("xs_1")
    span = span_ref[slot]
    column = stream_ref[0] + (span[0:1] + SCREENING)
    slope_ref[...] = jnp.broadcast_to(span[1:2], (LINES, LANES))
    eigen, head, tail = marks_ref[0], marks_ref[1], marks_ref[2]
    shifts = [1.0 / (jnp.zeros((LINES, LANES), jnp.float32) + diff_ref[f]) for f in range(4)]
    gains = []
    for field in range(4):
        shift = jnp.concatenate([shifts[field]] * 2, axis=0)
        share = 1.0 / (eigen + shift)
        gains.append(shift * share)
        share_ref[field] = share
        gain_ref[field] = gains[field]
    head_lift = wall_times(wall_ref, LIFT_BACK, head * gains[1])
    tail_lift = wall_times(wall_ref, LIFT_BACK, tail * gains[1])
    weights = [
        gains[0] * head * head, gains[0] * head * tail,
        gains[2] * head * head, gains[2] * head * tail,
        head_lift * head, head_lift * tail, tail_lift * head, tail_lift * tail,
        head * head, head * tail,
    ]
    for tile in range(BLOCKS):
        inverse = 1.0 / (eigen + column[tile : tile + 1])
        inverse_ref[:, LANES * tile : LANES * (tile + 1)] = inverse
        for at, weight in enumerate(weights):
            coef_ref[at, tile : tile + 1] = jnp.sum(weight * inverse, axis=0, keepdims=True)
    coef_ref[10] = 0.5 * shifts[1]

    shift = jnp.concatenate([column] + [part[:2] for part in shifts], axis=0)
    root = jnp.sqrt(shift * (shift + 4.0))
    decay = 2.0 / (2.0 + shift + root)
    two = decay * decay
    four = two * two
    eight = four * four
    sixteen = eight * eight
    powers = [jnp.ones_like(decay)]
    for _ in range(8):
        powers.append(powers[-1] * (sixteen * sixteen))
    scale = 1.0 / (root * (1.0 - powers[8] * two))
    none = jnp.zeros_like(decay)
    left_u, right_u = [none] * 9, [none] * 9
    left_w, right_w = [none] * 9, [none] * 9
    for b in range(1, 8):
        left_u[b], right_u[b] = 1.0 - powers[b], 1.0 - powers[b] * two
        left_w[b], right_w[b] = 1.0 - powers[8 - b] * two, 1.0 - powers[8 - b]
    for b in range(8):
        above = b + 1 if b < 7 else 8
        if b > 0:
            over_u, over_w = 1.0 / right_u[b], 1.0 / left_w[b]
            if b < 7:
                joint_ref[b + 1, 0] = sixteen * left_w[b + 1] * over_w
            if b > 1:
                joint_ref[b - 1, 1] = sixteen * right_u[b - 1] * over_u
            joint_ref[b, 2] = decay * left_u[b] * over_u
            joint_ref[b, 3] = decay * right_w[b] * over_w
        joint_ref[b, 4] = 1.0 + scale * decay * left_u[above] * right_w[above]
        joint_ref[b, 5] = scale * sixteen * left_u[b] * left_w[above]
        joint_ref[b, 6] = 1.0 + scale * decay * left_u[b] * right_w[b]
        joint_ref[b, 7] = scale * sixteen * right_u[b] * right_w[above]


def advect_kernel(first_ref, second_ref, left_ref, right_ref, out_ref):
    lanes = lane_ids(NZ)
    first, last = lanes == 0, lanes == LANES - 1
    left, right = left_ref[...], right_ref[...]
    half = jnp.where(lax.axis_index("xs_1") == 0, 0.5, -0.5)

    def value(field, slot):
        return (first_ref, second_ref)[slot][field]

    def slopes(field, slot):
        x = value(field, slot)
        at = 2 * field + 1 - slot
        up = jnp.where(last, pltpu.roll(right, (LANES - 1 - at) % LANES, 1), pltpu.roll(x, LANES - 1, 1))
        down = jnp.where(first, pltpu.roll(left, (LANES - at) % LANES, 1), pltpu.roll(x, 1, 1))
        along_x = (up - down) * 0.5
        along_y = value(field, 1) * half if slot == 0 else value(field, 0) * -half
        along_z = (pltpu.roll(x, NZ - 1, 0) - pltpu.roll(x, 1, 0)) * 0.5
        return along_x, along_y, along_z

    for field in range(4):
        for slot in range(2):
            grad = slopes(field, slot)
            base_grad = slopes(field + 4, slot)
            advect = jnp.zeros((NZ, LANES), jnp.float32)
            for axis in range(3):
                advect += value(4 + axis, slot) * grad[axis]
                advect += value(axis, slot) * base_grad[axis]
            result = value(field, slot) - ADV_STEP * advect
            if field == 1:
                result += BUOYANCY * value(3, slot)
            out_ref[field, slot] = result


def update_kernel(part_ref, first_ref, second_ref, inner_ref, outer_ref, table_ref, out_ref):
    core = lax.axis_index("xs_1")
    step = ADV_STEP * jnp.where(core == 0, 0.5, -0.5)
    sides = ((first_ref, outer_ref, step), (second_ref, inner_ref, -step))
    for field in range(4):
        updated = []
        for slot, (own_ref, far_ref, weight) in enumerate(sides):
            far = own_ref[5] * far_ref[field] + own_ref[1] * far_ref[field + 4]
            updated.append(part_ref[field, slot] + weight * far)
        rows = (
            jnp.where(core == 0, updated[0], updated[1]),
            jnp.where(core == 0, updated[1], updated[0]),
        )
        if field < 3:
            kind = field // 2
            modes = table_times(table_ref[0, kind], table_ref[1, kind], jnp.concatenate(rows, axis=1))
            rows = (modes[:, :LANES], modes[:, LANES:])
        for row in range(2):
            out_ref[pl.ds(2 * field + row, NZ, stride=LINES), :] = rows[row]


def lanes_of(x, tile):
    return x[:, LANES * tile : LANES * (tile + 1)]


def side_by_side(parts):
    return jnp.concatenate(parts, axis=1)


def stream_kernel(
    in_ref, table_ref, wall_ref, marks_ref, stream_ref, inverse_ref, gain_ref, coef_ref, slope_ref, joint_ref,
    waves_ref, pressure_ref, out_ref, local_ref, ends_ref,
):
    def lines(part, s):
        return in_ref[pl.ds(LINES * s + part, LINES, stride=NZ), :]

    x = [jnp.concatenate([lines(part, s) for part in range(6)], axis=0) for s in range(BLOCKS)]
    s04, d04 = x[0] + x[4], x[0] - x[4]
    s26, d26 = x[2] + x[6], x[2] - x[6]
    s15, d15 = x[1] + x[5], x[1] - x[5]
    s37, d37 = x[3] + x[7], x[3] - x[7]
    even, odd = s04 + s26, s15 + s37
    minus, plus = HALF * (d15 - d37), HALF * (d15 + d37)
    parts = [
        (even + odd, even - odd),
        (d04 + minus, plus + d26),
        (s04 - s26, s15 - s37),
        (d04 - minus, plus - d26),
    ]
    modes = side_by_side(
        [times_table(side_by_side(parts[g]), table_ref[0, g], table_ref[1, g]) for g in range(4)]
    )
    heat = side_by_side(
        [jnp.concatenate([lines(6, s), lines(7, s)], axis=0) for s in range(BLOCKS)]
    )
    fields = [modes[ROWS * f : ROWS * (f + 1)] for f in range(3)] + [heat]
    waves = wall_times(wall_ref, SINE, side_by_side(fields))
    waves_ref[...] = waves
    rise = wall_times(wall_ref, SINE_SLOPE, fields[1])
    head, tail = marks_ref[1], marks_ref[2]
    span = slope_ref[0:1, :]

    def wave(field, tile):
        return lanes_of(waves, BLOCKS * field + tile)

    pressure = []
    for tile in range(BLOCKS):
        slope = stream_ref[1, tile : tile + 1]
        source = slope * pltpu.roll(wave(0, tile), 64, 1) + lanes_of(rise, tile)
        source += span * wave(2, tile)
        pressure.append(-lanes_of(inverse_ref, tile) * source)
    joined = side_by_side(pressure)
    pressure_ref[...] = joined
    lift = wall_times(wall_ref, LIFT, joined)

    def ends(f):
        return (
            jnp.sum(f * tail, axis=0, keepdims=True), jnp.sum(f * head, axis=0, keepdims=True)
        )

    for tile in range(BLOCKS):
        p = pressure[tile]
        last, first = ends(p)
        half = coef_ref[10, tile : tile + 1]
        rows = lanes_of(fields[1], tile)
        values = [(last + 0.5 * rows[ROWS - 1 :], first - 0.5 * rows[:1])]
        slope = stream_ref[1, tile : tile + 1]
        corrected = (
            wave(0, tile) - slope * pltpu.roll(p, 64, 1),
            wave(1, tile) - lanes_of(lift, tile),
            wave(2, tile) + span * p,
            wave(3, tile),
        )
        for field in range(4):
            high, low = ends(gain_ref[field] * corrected[field])
            if field == 1:
                high, low = high + half * last, low - half * first
            values.append((high, low))
        for at, (high, low) in enumerate(values):
            ends_ref[0, LINES * at + tile : LINES * at + tile + 1] = high
            ends_ref[1, LINES * at + tile : LINES * at + tile + 1] = low
    own = lax.axis_index("wall_0")
    high, low = ends_ref[0], ends_ref[1]
    coefs = [joint_ref[own, at] for at in range(4, 8)]
    for system in range(5):
        part = slice(LINES * system, LINES * (system + 1))
        rows = slice(0, LINES) if system == 0 else slice(2 * system + 6, 2 * system + 7)
        up, down = high[part], low[part]
        upward = coefs[0][rows] * up + coefs[1][rows] * down
        downward = coefs[2][rows] * down + coefs[3][rows] * up
        if system > 0:
            local_ref[0, system - 1] = upward
            local_ref[1, system - 1] = downward
        for b in range(8):
            if system == 0:
                out_ref[b, 0] = upward
                out_ref[b, 1] = downward
            else:
                out_ref[b, system + 1] = jnp.where(own < b, upward, downward)


def joints(joint_ref, rows, upward, downward):
    rise, fall = [None, upward[0]], [None] * 7 + [downward[7]]
    for b in range(2, 8):
        rise.append(upward[b - 1] + joint_ref[b, 0, rows] * rise[b - 1])
    for b in range(6, 0, -1):
        fall[b] = downward[b] + joint_ref[b, 1, rows] * fall[b + 1]
    none = jnp.zeros_like(upward[0])
    alpha = [none] + [rise[b] + joint_ref[b, 2, rows] * fall[b] for b in range(1, 8)]
    beta = [fall[b] + joint_ref[b, 3, rows] * rise[b] for b in range(1, 8)] + [none]
    return alpha, beta


def stream_back_kernel(
    in_ref, local_ref, waves_ref, pressure_ref, table_ref, wall_ref, marks_ref, stream_ref, inverse_ref, gain_ref, share_ref, coef_ref, slope_ref, joint_ref,
    out_ref, alpha_ref, beta_ref,
):
    head, tail = marks_ref[1], marks_ref[2]
    span = slope_ref[0:1, :]
    alpha, beta = joints(
        joint_ref, pl.ds(0, 8), [in_ref[b, 0] for b in range(8)], [in_ref[b, 1] for b in range(8)]
    )
    own = lax.axis_index("wall_0")
    coef = [coef_ref[at] for at in range(11)]
    slope = stream_ref[1]
    upward, downward = [[], [], [], []], [[], [], [], []]
    for b in range(8):
        one, two = alpha[b], beta[b]
        one_x, two_x = slope * pltpu.roll(one, 64, 1), slope * pltpu.roll(two, 64, 1)
        one_z, two_z = span * one, span * two
        high = [
            -(one_x * coef[1] + two_x * coef[0]),
            coef[10] * (one * coef[9] + two * coef[8]) - (one * coef[6] + two * coef[7]),
            one_z * coef[3] + two_z * coef[2],
        ]
        low = [
            -(one_x * coef[0] + two_x * coef[1]),
            -coef[10] * (one * coef[8] + two * coef[9]) - (one * coef[4] + two * coef[5]),
            one_z * coef[2] + two_z * coef[3],
        ]
        for field in range(4):
            up, down = local_ref[0, field], local_ref[1, field]
            up = jnp.where(own == b, up, in_ref[b, field + 2])
            down = jnp.where(own == b, down, in_ref[b, field + 2])
            if field < 3:
                coefs = [joint_ref[b, at, pl.ds(8 + 2 * field, 1)] for at in range(4, 8)]
                up += coefs[0] * high[field] + coefs[1] * low[field]
                down += coefs[2] * low[field] + coefs[3] * high[field]
            upward[field].append(up)
            downward[field].append(down)
    pairs = [
        joints(joint_ref, pl.ds(8 + 2 * field, 1), upward[field], downward[field])
        for field in range(4)
    ]
    for b in range(8):
        for field in range(4):
            rows = slice(LINES * (field + 1), LINES * (field + 2))
            alpha_ref[b, rows] = pairs[field][0][b]
            beta_ref[b, rows] = pairs[field][1][b]
    for b in range(8):
        alpha_ref[b, :8] = alpha[b]
        beta_ref[b, :8] = beta[b]

    def outside(field, tile):
        at = LINES * field + tile
        return alpha_ref[own, at : at + 1] * head + beta_ref[own, at : at + 1] * tail

    def wave(field, tile):
        return lanes_of(waves_ref, BLOCKS * field + tile)

    pressure = [
        lanes_of(pressure_ref, tile) + lanes_of(inverse_ref, tile) * outside(0, tile)
        for tile in range(BLOCKS)
    ]
    lift = wall_times(wall_ref, LIFT, side_by_side(pressure))
    solved = [[], [], [], []]
    for tile in range(BLOCKS):
        p = pressure[tile]
        corrected = (
            wave(0, tile) - stream_ref[1, tile : tile + 1] * pltpu.roll(p, 64, 1),
            wave(1, tile) - lanes_of(lift, tile),
            wave(2, tile) + span * p,
            wave(3, tile),
        )
        for field in range(4):
            value = gain_ref[field] * corrected[field]
            solved[field].append(value + share_ref[field] * outside(field + 1, tile))
    rows = wall_times(wall_ref, SINE_BACK, side_by_side(sum(solved, [])))
    fields = [rows[:, NX * f : NX * (f + 1)] for f in range(4)]
    modes = jnp.concatenate(fields[:3], axis=0)
    parts = []
    for group in range(4):
        cells = times_table(
            modes[:, 2 * LANES * group : 2 * LANES * (group + 1)],
            table_ref[0, group], table_ref[1, group],
        )
        parts.append((cells[:, :LANES], cells[:, LANES:]))
    (c0, c4), (c1, s1), (c2, s2), (c3, s3) = parts
    sum04, dif04 = c0 + c4, c0 - c4
    sum13, dif13 = c1 + c3, HALF * (c1 - c3)
    plus13, minus13 = HALF * (s1 + s3), s1 - s3
    outer_a, outer_b = sum04 + c2, sum04 - c2
    inner_a, inner_b = dif04 + s2, dif04 - s2
    cells = [
        outer_a + sum13,
        inner_a + (dif13 + plus13),
        outer_b + minus13,
        inner_b + (plus13 - dif13),
        outer_a - sum13,
        inner_a - (dif13 + plus13),
        outer_b - minus13,
        inner_b - (plus13 - dif13),
    ]
    for s in range(BLOCKS):
        for part in range(8):
            if part < 6:
                value = cells[s][LINES * part : LINES * (part + 1)]
            else:
                value = lanes_of(fields[3], s)[LINES * (part - 6) : LINES * (part - 5)]
            out_ref[pl.ds(LINES * s + part, LINES, stride=NZ), :] = value


PAIRS = ((0, 0), (0, 1), (0, 2), (1, 1), (1, 2), (2, 2))


def folded(x):
    total = x[:LINES]
    for part in range(1, NZ // LINES):
        total += x[LINES * part : LINES * (part + 1)]
    return total


def cells_kernel(in_ref, vec_ref, table_ref, cur_ref, sums_ref):
    sums = [jnp.zeros((LINES, LANES), jnp.float32) for _ in range(10)]
    for field in range(4):
        for row in range(2):
            part = 2 * field + row
            cells = in_ref[pl.ds(part, NZ, stride=LINES), :]
            if field < 3:
                cells = table_times(table_ref[0, field // 2], table_ref[1, field // 2], cells)
            cur_ref[field, row] = cells
            vectors = [vec_ref[q, field, row] for q in range(3)]
            for q in range(3):
                sums[q] += folded(vectors[q] * cells)
            sums[3] += folded(cells * cells)
            for at, (q, p) in enumerate(PAIRS):
                sums[4 + at] += folded(vectors[q] * vectors[p])
    lanes = lane_ids(16)
    packed = jnp.zeros((16, LANES), jnp.float32)
    for at in range(10):
        packed = jnp.where(lanes == at, jnp.sum(sums[at]), packed)
    sums_ref[...] = packed


def residual_kernel(sums_ref, cur_ref, vec_ref, out_ref, hess_ref):
    entries = float(4 * NX * NY * NZ)
    totals = jnp.sum(sums_ref[...], axis=0, keepdims=True) * (1.0 / entries)
    lanes = lane_ids(1)

    def pick(at):
        return jnp.sum(jnp.where(lanes == at, totals, 0.0), axis=1, keepdims=True)

    values = [pick(at) for at in range(10)]
    products = values[:3]
    square = values[3]
    for q in range(3):
        square = square - 2.0 * products[q] * products[q]
    for at, (q, p) in enumerate(PAIRS):
        twice = 1.0 if q == p else 2.0
        square = square + twice * products[q] * products[p] * values[4 + at]
    norm = jnp.sqrt(square + EPSILON)
    for q in range(3):
        hess_ref[q] = jnp.sum(products[q])
    hess_ref[3] = jnp.sum(norm)
    scale = 1.0 / norm
    for field in range(4):
        for row in range(2):
            left = cur_ref[field, row]
            for q in range(3):
                left = left - products[q] * vec_ref[q, field, row]
            out_ref[field, row] = left * scale


VMEM = pl.BlockSpec(memory_space=pltpu.VMEM)
SMALL = pltpu.CompilerParams(vmem_limit_bytes=8 * 1024 * 1024)
LARGE = pltpu.CompilerParams(vmem_limit_bytes=54500 * 1024)
SMEM = pl.BlockSpec(memory_space=pltpu.SMEM)


def f32(*dims):
    return jax.ShapeDtypeStruct(dims, jnp.float32)


def shards(krylov_basis, base_state, diffusivity):
    span, span_eigen, span_slope = spanwise_tables()
    span = np.stack([span, span[np.arange(NZ) ^ 1]])
    span_columns = np.stack([span_eigen.reshape(-1), span_slope.reshape(-1)], axis=1)
    span_columns = np.broadcast_to(span_columns[:, :, None], (NZ, 2, LANES)).astype(np.float32)
    stream, stream_columns = stream_tables()
    wall, marks = block_tables()
    span, stream = np.stack(split(span)), np.stack(split(stream))

    rows = f32(8, NZ, LANES)
    first, second = pl.pallas_call(
        copy_kernel,
        in_specs=[pl.BlockSpec(memory_space=pltpu.HBM)] * 2,
        out_specs=[VMEM] * 2,
        out_shape=[rows, rows],
        scratch_shapes=[pltpu.SemaphoreType.DMA((16,))],
        compiler_params=LARGE,
        name="copy",
    )(krylov_basis, base_state)
    size, walls = lax.axis_size(XS), lax.axis_size(WALL)
    down = [[(size * (i + 1) + s, size * i + s) for i in range(walls - 1)] for s in range(size)]
    up = [[(b, a) for a, b in pairs] for pairs in down]
    inner = lax.ppermute(first, WALL + XS, sum([(down, up)[s % 2][s] for s in range(size)], []))
    outer = lax.ppermute(second, WALL + XS, sum([(up, down)[s % 2][s] for s in range(size)], []))
    low_x, high_x, inverse, gain, share, coef, slope, joint = pl.pallas_call(
        edges_kernel,
        in_specs=[SMEM] + [VMEM] * 6,
        out_specs=[VMEM] * 8,
        out_shape=[
            f32(NZ, LANES), f32(NZ, LANES), f32(ROWS, NX), f32(4, ROWS, LANES),
            f32(4, ROWS, LANES), f32(11, LINES, LANES), f32(LINES, LANES), f32(8, 8, ROWS, LANES),
        ],
        compiler_params=SMALL,
        name="edges",
    )(
        diffusivity, first, second, marks, stream_columns, span_columns, wall
    )
    right = lax.ppermute(low_x, XS, [((i + 1) % size, i) for i in range(size)])
    left = lax.ppermute(high_x, XS, [(i, (i + 1) % size) for i in range(size)])

    plane = ("wall_1",) + XS
    part = pl.pallas_call(
        advect_kernel,
        in_specs=[VMEM] * 4,
        out_specs=VMEM,
        out_shape=f32(4, 2, NZ, LANES),
        compiler_params=SMALL,
        name="advect",
    )(first, second, left, right)
    modes = pl.pallas_call(
        update_kernel,
        in_specs=[VMEM] * 6,
        out_specs=VMEM,
        out_shape=f32(NZ * LINES, LANES),
        compiler_params=SMALL,
        name="update",
    )(part, first, second, inner, outer, span)
    lines = lax.all_to_all(modes.reshape(NZ, LINES, LANES), plane, 0, 0, tiled=True)
    waves, pressure, ends, local = pl.pallas_call(
        stream_kernel,
        in_specs=[VMEM] * 10,
        out_specs=[VMEM] * 4,
        out_shape=[
            f32(ROWS, 4 * NX), f32(ROWS, NX), f32(8, 6, LINES, LANES), f32(2, 4, LINES, LANES)
        ],
        scratch_shapes=[pltpu.VMEM((2, 40, LANES), jnp.float32)],
        compiler_params=SMALL,
        name="stream",
    )(
        lines.reshape(-1, LANES), stream, wall, marks, stream_columns, inverse, gain, coef, slope,
        joint,
    )
    ends = lax.all_to_all(ends, "wall_0", 0, 0, tiled=True)
    lines = pl.pallas_call(
        stream_back_kernel,
        in_specs=[VMEM] * 14,
        out_specs=VMEM,
        out_shape=f32(NZ * LINES, LANES),
        scratch_shapes=[pltpu.VMEM((8, 40, LANES), jnp.float32)] * 2,
        compiler_params=SMALL,
        name="stream_back",
    )(
        ends, local, waves, pressure, stream.transpose(0, 1, 3, 2), wall, marks, stream_columns,
        inverse, gain, share, coef, slope, joint,
    )
    modes = lax.all_to_all(lines.reshape(NZ, LINES, LANES), plane, 0, 0, tiled=True)
    current, sums = pl.pallas_call(
        cells_kernel,
        in_specs=[VMEM] * 3,
        out_specs=[VMEM] * 2,
        out_shape=[f32(4, 2, NZ, LANES), f32(16, LANES)],
        compiler_params=SMALL,
        name="cells",
    )(modes.reshape(-1, LANES), krylov_basis, span.transpose(0, 1, 3, 2))
    sums = lax.all_to_all(sums, ("wall_0", "xs_1"), 0, 0, tiled=True).sum(axis=0)
    sums = jnp.broadcast_to(sums, (32, LANES))
    sums = lax.all_to_all(sums, ("wall_1", "xs_0"), 0, 0, tiled=True)
    new_vector, hessenberg = pl.pallas_call(
        residual_kernel,
        in_specs=[VMEM] * 3,
        out_specs=[VMEM, SMEM],
        out_shape=[f32(4, 2, NZ, LANES), f32(4)],
        compiler_params=SMALL,
        name="residual",
    )(sums, current, krylov_basis)
    return new_vector, hessenberg


def solution(mesh):
    torus = Mesh(mesh.devices.reshape(8, 8, 4, 2), ("wall_0", "wall_1", "xs_0", "xs_1"))
    return jax.shard_map(
        shards,
        mesh=torus,
        in_specs=(P(None, None, WALL, None, XS), P(None, WALL, None, XS), P()),
        out_specs=(P(None, WALL, None, XS), P()),
        check_vma=False,
    )
```

```python
import math

import jax
import jax.numpy as jnp
import ml_dtypes
import numpy as np
from jax import lax
from jax.experimental import pallas as pl
from jax.experimental.pallas import tpu as pltpu
from jax.sharding import Mesh
from jax.sharding import PartitionSpec as P

WALL = ("wall_0", "wall_1")
XS = ("xs_0", "xs_1")

ADV_STEP = 0.2
BUOYANCY = 0.5
SCREENING = 0.004
EPSILON = 1e-06

NX, NY, NZ = 1024, 128, 64
LINES, LANES, BLOCKS = 8, 128, 8
ROWS = 16
HALF = math.sqrt(0.5)


def split(table):
    high = table.astype(ml_dtypes.bfloat16)
    low = (table - high.astype(np.float64)).astype(ml_dtypes.bfloat16)
    return high, low


def spanwise_tables():
    cells = np.arange(NZ)
    table = np.zeros((NZ, NZ))
    eigen = np.zeros((NZ // 2, 2))
    slope = np.zeros((NZ // 2, 2))
    for pair in range(NZ // 2):
        if pair == 0:
            table[0] = 1.0 / math.sqrt(NZ)
            table[1] = np.cos(math.pi * cells) / math.sqrt(NZ)
            eigen[0] = (0.0, 4.0)
            continue
        angle = 2.0 * math.pi * (cells * pair % NZ) / NZ
        table[2 * pair] = np.cos(angle) * math.sqrt(2.0 / NZ)
        table[2 * pair + 1] = np.sin(angle) * math.sqrt(2.0 / NZ)
        eigen[pair] = 4.0 * math.sin(math.pi * pair / NZ) ** 2
        wave = math.sin(2.0 * math.pi * pair / NZ)
        slope[pair] = (wave, -wave)
    return table, eigen, slope


def stream_tables():
    cells = np.arange(LANES)
    weights = np.zeros((4, 2 * LANES, 2 * LANES))
    eigen = np.zeros((8, 2, 64))
    slope = np.zeros((8, 2, 64))
    for tile in range(8):
        group = tile // 2
        base = (0, 4)[tile] if group == 0 else group
        first = 0 if group == 0 else 64 * (tile % 2)
        for slot in range(64):
            wave = 8 * (first + slot) + base
            at = (tile % 2) * LANES + slot
            angle = 2.0 * math.pi * (cells * wave % NX) / NX
            scale = math.sqrt(2.0 / NX)
            if wave == 0:
                alternate = np.cos(math.pi * cells)
                weights[0, :LANES, at] = 1.0 / math.sqrt(NX)
                weights[0, :LANES, at + 64] = alternate / math.sqrt(NX)
                eigen[tile, :, slot] = (0.0, 4.0)
                continue
            eigen[tile, :, slot] = 4.0 * math.sin(math.pi * wave / NX) ** 2
            rise = math.sin(2.0 * math.pi * wave / NX)
            slope[tile, :, slot] = (rise, -rise)
            cos, sin = scale * np.cos(angle), scale * np.sin(angle)
            if group == 0:
                rows = slice((tile % 2) * LANES, (tile % 2 + 1) * LANES)
                weights[0, rows, at] = cos
                weights[0, rows, at + 64] = sin
            else:
                weights[group, :LANES, at] = cos
                weights[group, LANES:, at] = -sin
                weights[group, :LANES, at + 64] = sin
                weights[group, LANES:, at + 64] = cos
    columns = np.stack([eigen.reshape(8, LANES), slope.reshape(8, LANES)])
    return weights, columns.astype(np.float32)


def block_tables():
    order = np.arange(1, ROWS + 1)
    sine = np.sin(math.pi * np.outer(order, order) / (ROWS + 1))
    sine = sine * math.sqrt(2.0 / (ROWS + 1))
    shift = np.eye(ROWS, k=1)
    slope = 0.5 * (shift - shift.T)
    eigen = 2.0 - 2.0 * np.cos(math.pi * order / (ROWS + 1))
    rows = np.concatenate([np.arange(0, ROWS, 2), np.arange(1, ROWS, 2)])
    marks = np.stack([eigen, sine[:, 0], sine[:, ROWS - 1]])
    marks = np.broadcast_to(marks[:, :, None], (3, ROWS, LANES)).astype(np.float32)
    lift = sine @ slope @ sine
    tables = np.stack([sine[:, rows], (sine @ slope)[:, rows], lift, sine[:, rows].T, lift.T])
    return np.stack(split(tables)), marks


def halves(x):
    high = x.astype(jnp.bfloat16)
    low = (x - high.astype(jnp.float32)).astype(jnp.bfloat16)
    return high, low


def dot(a, b):
    return jnp.dot(a, b, preferred_element_type=jnp.float32)


def times_table(x, high_table, low_table):
    high, low = halves(x)
    return dot(high, high_table) + (dot(low, high_table) + dot(high, low_table))


SINE, SINE_SLOPE, LIFT, SINE_BACK, LIFT_BACK = range(5)


def wall_times(ref, which, x):
    return table_times(ref[0, which], ref[1, which], x)


def table_times(high_table, low_table, x):
    high, low = halves(x)
    return dot(high_table, high) + (dot(high_table, low) + dot(low_table, high))


def lane_ids(rows):
    return lax.broadcasted_iota(jnp.int32, (rows, LANES), 1)


def copy_kernel(vec_ref, base_ref, first_ref, second_ref, sems):
    core = lax.axis_index("xs_1")
    copies = []
    for slot, ref in enumerate((first_ref, second_ref)):
        row = core if slot == 0 else 1 - core
        for field in range(4):
            copies.append((vec_ref.at[2, field, row], ref.at[field]))
            copies.append((base_ref.at[field, row], ref.at[4 + field]))
    copies = [
        pltpu.make_async_copy(source, target, sems.at[at])
        for at, (source, target) in enumerate(copies)
    ]
    for copy in copies:
        copy.start()
    for copy in copies:
        copy.wait()


def edges_kernel(
    diff_ref, first_ref, second_ref, marks_ref, stream_ref, span_ref, wall_ref,
    low_x, high_x, inverse_ref, gain_ref, share_ref, coef_ref, slope_ref, joint_ref,
):
    lanes = lane_ids(NZ)
    low = jnp.zeros((NZ, LANES), jnp.float32)
    high = jnp.zeros((NZ, LANES), jnp.float32)
    for field in range(8):
        for slot, ref in enumerate((first_ref, second_ref)):
            block = ref[field]
            at = 2 * field + slot
            low = jnp.where(lanes == at, pltpu.roll(block, at, 1), low)
            high = jnp.where(lanes == at, pltpu.roll(block, (at + 1) % LANES, 1), high)
    low_x[...] = low
    high_x[...] = high

    slot = lax.axis_index("wall_1") * 8 + lax.axis_index("xs_0") * 2 + lax.axis_index("xs_1")
    span = span_ref[slot]
    column = stream_ref[0] + (span[0:1] + SCREENING)
    slope_ref[...] = jnp.broadcast_to(span[1:2], (LINES, LANES))
    eigen, head, tail = marks_ref[0], marks_ref[1], marks_ref[2]
    shifts = [1.0 / (jnp.zeros((LINES, LANES), jnp.float32) + diff_ref[f]) for f in range(4)]
    gains = []
    for field in range(4):
        shift = jnp.concatenate([shifts[field]] * 2, axis=0)
        share = 1.0 / (eigen + shift)
        gains.append(shift * share)
        share_ref[field] = share
        gain_ref[field] = gains[field]
    head_lift = wall_times(wall_ref, LIFT_BACK, head * gains[1])
    tail_lift = wall_times(wall_ref, LIFT_BACK, tail * gains[1])
    weights = [
        gains[0] * head * head, gains[0] * head * tail,
        gains[2] * head * head, gains[2] * head * tail,
        head_lift * head, head_lift * tail, tail_lift * head, tail_lift * tail,
        head * head, head * tail,
    ]
    for tile in range(BLOCKS):
        inverse = 1.0 / (eigen + column[tile : tile + 1])
        inverse_ref[:, LANES * tile : LANES * (tile + 1)] = inverse
        for at, weight in enumerate(weights):
            coef_ref[at, tile : tile + 1] = jnp.sum(weight * inverse, axis=0, keepdims=True)
    coef_ref[10] = 0.5 * shifts[1]

    shift = jnp.concatenate([column] + [part[:2] for part in shifts], axis=0)
    root = jnp.sqrt(shift * (shift + 4.0))
    decay = 2.0 / (2.0 + shift + root)
    two = decay * decay
    four = two * two
    eight = four * four
    sixteen = eight * eight
    powers = [jnp.ones_like(decay)]
    for _ in range(8):
        powers.append(powers[-1] * (sixteen * sixteen))
    scale = 1.0 / (root * (1.0 - powers[8] * two))
    none = jnp.zeros_like(decay)
    left_u, right_u = [none] * 9, [none] * 9
    left_w, right_w = [none] * 9, [none] * 9
    for b in range(1, 8):
        left_u[b], right_u[b] = 1.0 - powers[b], 1.0 - powers[b] * two
        left_w[b], right_w[b] = 1.0 - powers[8 - b] * two, 1.0 - powers[8 - b]
    for b in range(8):
        above = b + 1 if b < 7 else 8
        if b > 0:
            over_u, over_w = 1.0 / right_u[b], 1.0 / left_w[b]
            if b < 7:
                joint_ref[b + 1, 0] = sixteen * left_w[b + 1] * over_w
            if b > 1:
                joint_ref[b - 1, 1] = sixteen * right_u[b - 1] * over_u
            joint_ref[b, 2] = decay * left_u[b] * over_u
            joint_ref[b, 3] = decay * right_w[b] * over_w
        joint_ref[b, 4] = 1.0 + scale * decay * left_u[above] * right_w[above]
        joint_ref[b, 5] = scale * sixteen * left_u[b] * left_w[above]
        joint_ref[b, 6] = 1.0 + scale * decay * left_u[b] * right_w[b]
        joint_ref[b, 7] = scale * sixteen * right_u[b] * right_w[above]


def advect_kernel(first_ref, second_ref, left_ref, right_ref, out_ref):
    lanes = lane_ids(NZ)
    first, last = lanes == 0, lanes == LANES - 1
    left, right = left_ref[...], right_ref[...]
    half = jnp.where(lax.axis_index("xs_1") == 0, 0.5, -0.5)

    def value(field, slot):
        return (first_ref, second_ref)[slot][field]

    def slopes(field, slot):
        x = value(field, slot)
        at = 2 * field + 1 - slot
        up = jnp.where(last, pltpu.roll(right, (LANES - 1 - at) % LANES, 1), pltpu.roll(x, LANES - 1, 1))
        down = jnp.where(first, pltpu.roll(left, (LANES - at) % LANES, 1), pltpu.roll(x, 1, 1))
        along_x = (up - down) * 0.5
        along_y = value(field, 1) * half if slot == 0 else value(field, 0) * -half
        along_z = (pltpu.roll(x, NZ - 1, 0) - pltpu.roll(x, 1, 0)) * 0.5
        return along_x, along_y, along_z

    for field in range(4):
        for slot in range(2):
            grad = slopes(field, slot)
            base_grad = slopes(field + 4, slot)
            advect = jnp.zeros((NZ, LANES), jnp.float32)
            for axis in range(3):
                advect += value(4 + axis, slot) * grad[axis]
                advect += value(axis, slot) * base_grad[axis]
            result = value(field, slot) - ADV_STEP * advect
            if field == 1:
                result += BUOYANCY * value(3, slot)
            out_ref[field, slot] = result


def update_kernel(part_ref, first_ref, second_ref, inner_ref, outer_ref, table_ref, out_ref):
    core = lax.axis_index("xs_1")
    step = ADV_STEP * jnp.where(core == 0, 0.5, -0.5)
    sides = ((first_ref, outer_ref, step), (second_ref, inner_ref, -step))
    for field in range(4):
        updated = []
        for slot, (own_ref, far_ref, weight) in enumerate(sides):
            far = own_ref[5] * far_ref[field] + own_ref[1] * far_ref[field + 4]
            updated.append(part_ref[field, slot] + weight * far)
        rows = (
            jnp.where(core == 0, updated[0], updated[1]),
            jnp.where(core == 0, updated[1], updated[0]),
        )
        if field < 3:
            kind = field // 2
            modes = table_times(table_ref[0, kind], table_ref[1, kind], jnp.concatenate(rows, axis=1))
            rows = (modes[:, :LANES], modes[:, LANES:])
        for row in range(2):
            out_ref[pl.ds(2 * field + row, NZ, stride=LINES), :] = rows[row]


def lanes_of(x, tile):
    return x[:, LANES * tile : LANES * (tile + 1)]


def side_by_side(parts):
    return jnp.concatenate(parts, axis=1)


def stream_kernel(
    in_ref, table_ref, wall_ref, marks_ref, stream_ref, inverse_ref, gain_ref, coef_ref, slope_ref, joint_ref,
    waves_ref, pressure_ref, out_ref, local_ref, ends_ref,
):
    def lines(part, s):
        return in_ref[pl.ds(LINES * s + part, LINES, stride=NZ), :]

    x = [jnp.concatenate([lines(part, s) for part in range(6)], axis=0) for s in range(BLOCKS)]
    s04, d04 = x[0] + x[4], x[0] - x[4]
    s26, d26 = x[2] + x[6], x[2] - x[6]
    s15, d15 = x[1] + x[5], x[1] - x[5]
    s37, d37 = x[3] + x[7], x[3] - x[7]
    even, odd = s04 + s26, s15 + s37
    minus, plus = HALF * (d15 - d37), HALF * (d15 + d37)
    parts = [
        (even + odd, even - odd),
        (d04 + minus, plus + d26),
        (s04 - s26, s15 - s37),
        (d04 - minus, plus - d26),
    ]
    modes = side_by_side(
        [times_table(side_by_side(parts[g]), table_ref[0, g], table_ref[1, g]) for g in range(4)]
    )
    heat = side_by_side(
        [jnp.concatenate([lines(6, s), lines(7, s)], axis=0) for s in range(BLOCKS)]
    )
    fields = [modes[ROWS * f : ROWS * (f + 1)] for f in range(3)] + [heat]
    waves = wall_times(wall_ref, SINE, side_by_side(fields))
    waves_ref[...] = waves
    rise = wall_times(wall_ref, SINE_SLOPE, fields[1])
    head = marks_ref[1]
    span = slope_ref[0:1, :]

    def wave(field, tile):
        return lanes_of(waves, BLOCKS * field + tile)

    pressure = []
    for tile in range(BLOCKS):
        slope = stream_ref[1, tile : tile + 1]
        source = slope * pltpu.roll(wave(0, tile), 64, 1) + lanes_of(rise, tile)
        source += span * wave(2, tile)
        pressure.append(-lanes_of(inverse_ref, tile) * source)
    joined = side_by_side(pressure)
    pressure_ref[...] = joined
    lift = wall_times(wall_ref, LIFT, joined)

    def ends(f):
        weighted = f * head
        total = weighted[:LINES] + weighted[LINES:]
        total = total + pltpu.roll(total, 4, 0)
        total = total + pltpu.roll(total, 2, 0)
        even, odd = total[:1], total[1:2]
        return even - odd, even + odd

    for tile in range(BLOCKS):
        p = pressure[tile]
        last, first = ends(p)
        half = coef_ref[10, tile : tile + 1]
        rows = lanes_of(fields[1], tile)
        values = [(last + 0.5 * rows[ROWS - 1 :], first - 0.5 * rows[:1])]
        slope = stream_ref[1, tile : tile + 1]
        corrected = (
            wave(0, tile) - slope * pltpu.roll(p, 64, 1),
            wave(1, tile) - lanes_of(lift, tile),
            wave(2, tile) + span * p,
            wave(3, tile),
        )
        for field in range(4):
            high, low = ends(gain_ref[field] * corrected[field])
            if field == 1:
                high, low = high + half * last, low - half * first
            values.append((high, low))
        for at, (high, low) in enumerate(values):
            ends_ref[0, LINES * at + tile : LINES * at + tile + 1] = high
            ends_ref[1, LINES * at + tile : LINES * at + tile + 1] = low
    own = lax.axis_index("wall_0")
    high, low = ends_ref[0], ends_ref[1]
    coefs = [joint_ref[own, at] for at in range(4, 8)]
    for system in range(5):
        part = slice(LINES * system, LINES * (system + 1))
        rows = slice(0, LINES) if system == 0 else slice(2 * system + 6, 2 * system + 7)
        up, down = high[part], low[part]
        upward = coefs[0][rows] * up + coefs[1][rows] * down
        downward = coefs[2][rows] * down + coefs[3][rows] * up
        if system > 0:
            local_ref[0, system - 1] = upward
            local_ref[1, system - 1] = downward
        for b in range(8):
            if system == 0:
                out_ref[b, 0] = upward
                out_ref[b, 1] = downward
            else:
                out_ref[b, system + 1] = jnp.where(own < b, upward, downward)


def joints(joint_ref, rows, upward, downward):
    rise, fall = [None, upward[0]], [None] * 7 + [downward[7]]
    for b in range(2, 8):
        rise.append(upward[b - 1] + joint_ref[b, 0, rows] * rise[b - 1])
    for b in range(6, 0, -1):
        fall[b] = downward[b] + joint_ref[b, 1, rows] * fall[b + 1]
    none = jnp.zeros_like(upward[0])
    alpha = [none] + [rise[b] + joint_ref[b, 2, rows] * fall[b] for b in range(1, 8)]
    beta = [fall[b] + joint_ref[b, 3, rows] * rise[b] for b in range(1, 8)] + [none]
    return alpha, beta


def stream_back_kernel(
    in_ref, local_ref, waves_ref, pressure_ref, table_ref, wall_ref, marks_ref, stream_ref, inverse_ref, gain_ref, share_ref, coef_ref, slope_ref, joint_ref,
    out_ref, alpha_ref, beta_ref,
):
    head, tail = marks_ref[1], marks_ref[2]
    span = slope_ref[0:1, :]
    alpha, beta = joints(
        joint_ref, pl.ds(0, 8), [in_ref[b, 0] for b in range(8)], [in_ref[b, 1] for b in range(8)]
    )
    own = lax.axis_index("wall_0")
    coef = [coef_ref[at] for at in range(11)]
    slope = stream_ref[1]
    upward, downward = [[], [], [], []], [[], [], [], []]
    for b in range(8):
        one, two = alpha[b], beta[b]
        one_x, two_x = slope * pltpu.roll(one, 64, 1), slope * pltpu.roll(two, 64, 1)
        one_z, two_z = span * one, span * two
        high = [
            -(one_x * coef[1] + two_x * coef[0]),
            coef[10] * (one * coef[9] + two * coef[8]) - (one * coef[6] + two * coef[7]),
            one_z * coef[3] + two_z * coef[2],
        ]
        low = [
            -(one_x * coef[0] + two_x * coef[1]),
            -coef[10] * (one * coef[8] + two * coef[9]) - (one * coef[4] + two * coef[5]),
            one_z * coef[2] + two_z * coef[3],
        ]
        for field in range(4):
            up, down = local_ref[0, field], local_ref[1, field]
            up = jnp.where(own == b, up, in_ref[b, field + 2])
            down = jnp.where(own == b, down, in_ref[b, field + 2])
            if field < 3:
                coefs = [joint_ref[b, at, pl.ds(8 + 2 * field, 1)] for at in range(4, 8)]
                up += coefs[0] * high[field] + coefs[1] * low[field]
                down += coefs[2] * low[field] + coefs[3] * high[field]
            upward[field].append(up)
            downward[field].append(down)
    pairs = [
        joints(joint_ref, pl.ds(8 + 2 * field, 1), upward[field], downward[field])
        for field in range(4)
    ]
    for b in range(8):
        for field in range(4):
            rows = slice(LINES * (field + 1), LINES * (field + 2))
            alpha_ref[b, rows] = pairs[field][0][b]
            beta_ref[b, rows] = pairs[field][1][b]
    for b in range(8):
        alpha_ref[b, :8] = alpha[b]
        beta_ref[b, :8] = beta[b]

    def outside(field, tile):
        at = LINES * field + tile
        return alpha_ref[own, at : at + 1] * head + beta_ref[own, at : at + 1] * tail

    def wave(field, tile):
        return lanes_of(waves_ref, BLOCKS * field + tile)

    pressure = [
        lanes_of(pressure_ref, tile) + lanes_of(inverse_ref, tile) * outside(0, tile)
        for tile in range(BLOCKS)
    ]
    lift = wall_times(wall_ref, LIFT, side_by_side(pressure))
    solved = [[], [], [], []]
    for tile in range(BLOCKS):
        p = pressure[tile]
        corrected = (
            wave(0, tile) - stream_ref[1, tile : tile + 1] * pltpu.roll(p, 64, 1),
            wave(1, tile) - lanes_of(lift, tile),
            wave(2, tile) + span * p,
            wave(3, tile),
        )
        for field in range(4):
            value = gain_ref[field] * corrected[field]
            solved[field].append(value + share_ref[field] * outside(field + 1, tile))
    rows = wall_times(wall_ref, SINE_BACK, side_by_side(sum(solved, [])))
    fields = [rows[:, NX * f : NX * (f + 1)] for f in range(4)]
    modes = jnp.concatenate(fields[:3], axis=0)
    parts = []
    for group in range(4):
        cells = times_table(
            modes[:, 2 * LANES * group : 2 * LANES * (group + 1)],
            table_ref[0, group], table_ref[1, group],
        )
        parts.append((cells[:, :LANES], cells[:, LANES:]))
    (c0, c4), (c1, s1), (c2, s2), (c3, s3) = parts
    sum04, dif04 = c0 + c4, c0 - c4
    sum13, dif13 = c1 + c3, HALF * (c1 - c3)
    plus13, minus13 = HALF * (s1 + s3), s1 - s3
    outer_a, outer_b = sum04 + c2, sum04 - c2
    inner_a, inner_b = dif04 + s2, dif04 - s2
    cells = [
        outer_a + sum13,
        inner_a + (dif13 + plus13),
        outer_b + minus13,
        inner_b + (plus13 - dif13),
        outer_a - sum13,
        inner_a - (dif13 + plus13),
        outer_b - minus13,
        inner_b - (plus13 - dif13),
    ]
    for s in range(BLOCKS):
        for part in range(8):
            if part < 6:
                value = cells[s][LINES * part : LINES * (part + 1)]
            else:
                value = lanes_of(fields[3], s)[LINES * (part - 6) : LINES * (part - 5)]
            out_ref[pl.ds(LINES * s + part, LINES, stride=NZ), :] = value


PAIRS = ((0, 0), (0, 1), (0, 2), (1, 1), (1, 2), (2, 2))


def folded(x):
    total = x[:LINES]
    for part in range(1, NZ // LINES):
        total += x[LINES * part : LINES * (part + 1)]
    return total


def cells_kernel(in_ref, vec_ref, table_ref, cur_ref, sums_ref):
    sums = [jnp.zeros((LINES, LANES), jnp.float32) for _ in range(10)]
    for field in range(4):
        for row in range(2):
            part = 2 * field + row
            cells = in_ref[pl.ds(part, NZ, stride=LINES), :]
            if field < 3:
                cells = table_times(table_ref[0, field // 2], table_ref[1, field // 2], cells)
            cur_ref[field, row] = cells
            vectors = [vec_ref[q, field, row] for q in range(3)]
            for q in range(3):
                sums[q] += folded(vectors[q] * cells)
            sums[3] += folded(cells * cells)
            for at, (q, p) in enumerate(PAIRS):
                sums[4 + at] += folded(vectors[q] * vectors[p])
    lanes = lane_ids(16)
    packed = jnp.zeros((16, LANES), jnp.float32)
    for at in range(10):
        total = jnp.sum(jnp.sum(sums[at], axis=0, keepdims=True), axis=1, keepdims=True)
        packed = jnp.where(lanes == at, total, packed)
    sums_ref[...] = packed


def residual_kernel(sums_ref, cur_ref, vec_ref, out_ref, hess_ref):
    entries = float(4 * NX * NY * NZ)
    totals = jnp.sum(sums_ref[...], axis=0, keepdims=True) * (1.0 / entries)
    lanes = lane_ids(1)

    def pick(at):
        return jnp.sum(jnp.where(lanes == at, totals, 0.0), axis=1, keepdims=True)

    values = [pick(at) for at in range(10)]
    products = values[:3]
    square = values[3]
    for q in range(3):
        square = square - 2.0 * products[q] * products[q]
    for at, (q, p) in enumerate(PAIRS):
        twice = 1.0 if q == p else 2.0
        square = square + twice * products[q] * products[p] * values[4 + at]
    norm = jnp.sqrt(square + EPSILON)
    for q in range(3):
        hess_ref[q] = jnp.sum(products[q])
    hess_ref[3] = jnp.sum(norm)
    scale = 1.0 / norm
    for field in range(4):
        for row in range(2):
            left = cur_ref[field, row]
            for q in range(3):
                left = left - products[q] * vec_ref[q, field, row]
            out_ref[field, row] = left * scale


VMEM = pl.BlockSpec(memory_space=pltpu.VMEM)
SMALL = pltpu.CompilerParams(vmem_limit_bytes=8 * 1024 * 1024)
LARGE = pltpu.CompilerParams(vmem_limit_bytes=54500 * 1024)
SMEM = pl.BlockSpec(memory_space=pltpu.SMEM)


def f32(*dims):
    return jax.ShapeDtypeStruct(dims, jnp.float32)


def shards(krylov_basis, base_state, diffusivity):
    span, span_eigen, span_slope = spanwise_tables()
    span = np.stack([span, span[np.arange(NZ) ^ 1]])
    span_columns = np.stack([span_eigen.reshape(-1), span_slope.reshape(-1)], axis=1)
    span_columns = np.broadcast_to(span_columns[:, :, None], (NZ, 2, LANES)).astype(np.float32)
    stream, stream_columns = stream_tables()
    wall, marks = block_tables()
    span, stream = np.stack(split(span)), np.stack(split(stream))

    rows = f32(8, NZ, LANES)
    first, second = pl.pallas_call(
        copy_kernel,
        in_specs=[pl.BlockSpec(memory_space=pltpu.HBM)] * 2,
        out_specs=[VMEM] * 2,
        out_shape=[rows, rows],
        scratch_shapes=[pltpu.SemaphoreType.DMA((16,))],
        compiler_params=LARGE,
        name="copy",
    )(krylov_basis, base_state)
    size, walls = lax.axis_size(XS), lax.axis_size(WALL)
    down = [[(size * (i + 1) + s, size * i + s) for i in range(walls - 1)] for s in range(size)]
    up = [[(b, a) for a, b in pairs] for pairs in down]
    inner = lax.ppermute(first, WALL + XS, sum([(down, up)[s % 2][s] for s in range(size)], []))
    outer = lax.ppermute(second, WALL + XS, sum([(up, down)[s % 2][s] for s in range(size)], []))
    low_x, high_x, inverse, gain, share, coef, slope, joint = pl.pallas_call(
        edges_kernel,
        in_specs=[SMEM] + [VMEM] * 6,
        out_specs=[VMEM] * 8,
        out_shape=[
            f32(NZ, LANES), f32(NZ, LANES), f32(ROWS, NX), f32(4, ROWS, LANES),
            f32(4, ROWS, LANES), f32(11, LINES, LANES), f32(LINES, LANES), f32(8, 8, ROWS, LANES),
        ],
        compiler_params=SMALL,
        name="edges",
    )(
        diffusivity, first, second, marks, stream_columns, span_columns, wall
    )
    right = lax.ppermute(low_x, XS, [((i + 1) % size, i) for i in range(size)])
    left = lax.ppermute(high_x, XS, [(i, (i + 1) % size) for i in range(size)])

    plane = ("wall_1",) + XS
    part = pl.pallas_call(
        advect_kernel,
        in_specs=[VMEM] * 4,
        out_specs=VMEM,
        out_shape=f32(4, 2, NZ, LANES),
        compiler_params=SMALL,
        name="advect",
    )(first, second, left, right)
    modes = pl.pallas_call(
        update_kernel,
        in_specs=[VMEM] * 6,
        out_specs=VMEM,
        out_shape=f32(NZ * LINES, LANES),
        compiler_params=SMALL,
        name="update",
    )(part, first, second, inner, outer, span)
    lines = lax.all_to_all(modes.reshape(NZ, LINES, LANES), plane, 0, 0, tiled=True)
    waves, pressure, ends, local = pl.pallas_call(
        stream_kernel,
        in_specs=[VMEM] * 10,
        out_specs=[VMEM] * 4,
        out_shape=[
            f32(ROWS, 4 * NX), f32(ROWS, NX), f32(8, 6, LINES, LANES), f32(2, 4, LINES, LANES)
        ],
        scratch_shapes=[pltpu.VMEM((2, 40, LANES), jnp.float32)],
        compiler_params=SMALL,
        name="stream",
    )(
        lines.reshape(-1, LANES), stream, wall, marks, stream_columns, inverse, gain, coef, slope,
        joint,
    )
    ends = lax.all_to_all(ends, "wall_0", 0, 0, tiled=True)
    lines = pl.pallas_call(
        stream_back_kernel,
        in_specs=[VMEM] * 14,
        out_specs=VMEM,
        out_shape=f32(NZ * LINES, LANES),
        scratch_shapes=[pltpu.VMEM((8, 40, LANES), jnp.float32)] * 2,
        compiler_params=SMALL,
        name="stream_back",
    )(
        ends, local, waves, pressure, stream.transpose(0, 1, 3, 2), wall, marks, stream_columns,
        inverse, gain, share, coef, slope, joint,
    )
    modes = lax.all_to_all(lines.reshape(NZ, LINES, LANES), plane, 0, 0, tiled=True)
    current, sums = pl.pallas_call(
        cells_kernel,
        in_specs=[VMEM] * 3,
        out_specs=[VMEM] * 2,
        out_shape=[f32(4, 2, NZ, LANES), f32(16, LANES)],
        compiler_params=SMALL,
        name="cells",
    )(modes.reshape(-1, LANES), krylov_basis, span.transpose(0, 1, 3, 2))
    sums = lax.all_to_all(sums, ("wall_0", "xs_1"), 0, 0, tiled=True).sum(axis=0)
    sums = jnp.broadcast_to(sums, (32, LANES))
    sums = lax.all_to_all(sums, ("wall_1", "xs_0"), 0, 0, tiled=True)
    new_vector, hessenberg = pl.pallas_call(
        residual_kernel,
        in_specs=[VMEM] * 3,
        out_specs=[VMEM, SMEM],
        out_shape=[f32(4, 2, NZ, LANES), f32(4)],
        compiler_params=SMALL,
        name="residual",
    )(sums, current, krylov_basis)
    return new_vector, hessenberg


def solution(mesh):
    torus = Mesh(mesh.devices.reshape(8, 8, 4, 2), ("wall_0", "wall_1", "xs_0", "xs_1"))
    return jax.shard_map(
        shards,
        mesh=torus,
        in_specs=(P(None, None, WALL, None, XS), P(None, WALL, None, XS), P()),
        out_specs=(P(None, WALL, None, XS), P()),
        check_vma=False,
    )
```

```python
import math

import jax
import jax.numpy as jnp
import ml_dtypes
import numpy as np
from jax import lax
from jax.experimental import pallas as pl
from jax.experimental.pallas import tpu as pltpu
from jax.sharding import Mesh
from jax.sharding import PartitionSpec as P

WALL = ("wall_0", "wall_1")
XS = ("xs_0", "xs_1")

ADV_STEP = 0.2
BUOYANCY = 0.5
SCREENING = 0.004
EPSILON = 1e-06

NX, NY, NZ = 1024, 128, 64
LINES, LANES, BLOCKS = 8, 128, 8
ROWS = 16
HALF = math.sqrt(0.5)


def split(table):
    high = table.astype(ml_dtypes.bfloat16)
    low = (table - high.astype(np.float64)).astype(ml_dtypes.bfloat16)
    return high, low


def joined(table):
    high, low = split(table)
    return np.concatenate([high, high, low], axis=-1)


def spanwise_tables():
    cells = np.arange(NZ)
    table = np.zeros((NZ, NZ))
    eigen = np.zeros((NZ // 2, 2))
    slope = np.zeros((NZ // 2, 2))
    for pair in range(NZ // 2):
        if pair == 0:
            table[0] = 1.0 / math.sqrt(NZ)
            table[1] = np.cos(math.pi * cells) / math.sqrt(NZ)
            eigen[0] = (0.0, 4.0)
            continue
        angle = 2.0 * math.pi * (cells * pair % NZ) / NZ
        table[2 * pair] = np.cos(angle) * math.sqrt(2.0 / NZ)
        table[2 * pair + 1] = np.sin(angle) * math.sqrt(2.0 / NZ)
        eigen[pair] = 4.0 * math.sin(math.pi * pair / NZ) ** 2
        wave = math.sin(2.0 * math.pi * pair / NZ)
        slope[pair] = (wave, -wave)
    return table, eigen, slope


def stream_tables():
    cells = np.arange(LANES)
    weights = np.zeros((4, 2 * LANES, 2 * LANES))
    eigen = np.zeros((8, 2, 64))
    slope = np.zeros((8, 2, 64))
    for tile in range(8):
        group = tile // 2
        base = (0, 4)[tile] if group == 0 else group
        first = 0 if group == 0 else 64 * (tile % 2)
        for slot in range(64):
            wave = 8 * (first + slot) + base
            at = (tile % 2) * LANES + slot
            angle = 2.0 * math.pi * (cells * wave % NX) / NX
            scale = math.sqrt(2.0 / NX)
            if wave == 0:
                alternate = np.cos(math.pi * cells)
                weights[0, :LANES, at] = 1.0 / math.sqrt(NX)
                weights[0, :LANES, at + 64] = alternate / math.sqrt(NX)
                eigen[tile, :, slot] = (0.0, 4.0)
                continue
            eigen[tile, :, slot] = 4.0 * math.sin(math.pi * wave / NX) ** 2
            rise = math.sin(2.0 * math.pi * wave / NX)
            slope[tile, :, slot] = (rise, -rise)
            cos, sin = scale * np.cos(angle), scale * np.sin(angle)
            if group == 0:
                rows = slice((tile % 2) * LANES, (tile % 2 + 1) * LANES)
                weights[0, rows, at] = cos
                weights[0, rows, at + 64] = sin
            else:
                weights[group, :LANES, at] = cos
                weights[group, LANES:, at] = -sin
                weights[group, :LANES, at + 64] = sin
                weights[group, LANES:, at + 64] = cos
    columns = np.stack([eigen.reshape(8, LANES), slope.reshape(8, LANES)])
    return weights, columns.astype(np.float32)


def block_tables():
    order = np.arange(1, ROWS + 1)
    sine = np.sin(math.pi * np.outer(order, order) / (ROWS + 1))
    sine = sine * math.sqrt(2.0 / (ROWS + 1))
    shift = np.eye(ROWS, k=1)
    slope = 0.5 * (shift - shift.T)
    eigen = 2.0 - 2.0 * np.cos(math.pi * order / (ROWS + 1))
    rows = np.concatenate([np.arange(0, ROWS, 2), np.arange(1, ROWS, 2)])
    marks = np.stack([eigen, sine[:, 0], sine[:, ROWS - 1]])
    marks = np.broadcast_to(marks[:, :, None], (3, ROWS, LANES)).astype(np.float32)
    lift = sine @ slope @ sine
    tables = np.stack([sine[:, rows], (sine @ slope)[:, rows], lift, sine[:, rows].T, lift.T])
    return joined(tables), marks


def halves(x):
    high = x.astype(jnp.bfloat16)
    low = (x - high.astype(jnp.float32)).astype(jnp.bfloat16)
    return high, low


def dot(a, b):
    return jnp.dot(a, b, preferred_element_type=jnp.float32)


def times_table(x, high_table, low_table):
    high, low = halves(x)
    return dot(high, high_table) + (dot(low, high_table) + dot(high, low_table))


SINE, SINE_SLOPE, LIFT, SINE_BACK, LIFT_BACK = range(5)


def wall_times(ref, which, x):
    return table_times(ref[which], x)


def table_times(table, x):
    high, low = halves(x)
    return dot(table, jnp.concatenate([high, low, high], axis=0))


def lane_ids(rows):
    return lax.broadcasted_iota(jnp.int32, (rows, LANES), 1)


def copy_kernel(vec_ref, base_ref, first_ref, second_ref, sems):
    core = lax.axis_index("xs_1")
    copies = []
    for slot, ref in enumerate((first_ref, second_ref)):
        row = core if slot == 0 else 1 - core
        for field in range(4):
            copies.append((vec_ref.at[2, field, row], ref.at[field]))
            copies.append((base_ref.at[field, row], ref.at[4 + field]))
    copies = [
        pltpu.make_async_copy(source, target, sems.at[at])
        for at, (source, target) in enumerate(copies)
    ]
    for copy in copies:
        copy.start()
    for copy in copies:
        copy.wait()


def edges_kernel(
    diff_ref, first_ref, second_ref, marks_ref, stream_ref, span_ref, wall_ref,
    low_x, high_x, inverse_ref, gain_ref, share_ref, coef_ref, slope_ref, joint_ref,
):
    lanes = lane_ids(NZ)
    low = jnp.zeros((NZ, LANES), jnp.float32)
    high = jnp.zeros((NZ, LANES), jnp.float32)
    for field in range(8):
        for slot, ref in enumerate((first_ref, second_ref)):
            block = ref[field]
            at = 2 * field + slot
            low = jnp.where(lanes == at, pltpu.roll(block, at, 1), low)
            high = jnp.where(lanes == at, pltpu.roll(block, (at + 1) % LANES, 1), high)
    low_x[...] = low
    high_x[...] = high

    slot = lax.axis_index("wall_1") * 8 + lax.axis_index("xs_0") * 2 + lax.axis_index("xs_1")
    span = span_ref[slot]
    column = stream_ref[0] + (span[0:1] + SCREENING)
    slope_ref[...] = jnp.broadcast_to(span[1:2], (LINES, LANES))
    eigen, head, tail = marks_ref[0], marks_ref[1], marks_ref[2]
    shifts = [1.0 / (jnp.zeros((LINES, LANES), jnp.float32) + diff_ref[f]) for f in range(4)]
    gains = []
    for field in range(4):
        shift = jnp.concatenate([shifts[field]] * 2, axis=0)
        share = 1.0 / (eigen + shift)
        gains.append(shift * share)
        share_ref[field] = share
        gain_ref[field] = gains[field]
    head_lift = wall_times(wall_ref, LIFT_BACK, head * gains[1])
    tail_lift = wall_times(wall_ref, LIFT_BACK, tail * gains[1])
    weights = [
        gains[0] * head * head, gains[0] * head * tail,
        gains[2] * head * head, gains[2] * head * tail,
        head_lift * head, head_lift * tail, tail_lift * head, tail_lift * tail,
        head * head, head * tail,
    ]
    for tile in range(BLOCKS):
        inverse = 1.0 / (eigen + column[tile : tile + 1])
        inverse_ref[:, LANES * tile : LANES * (tile + 1)] = inverse
        for at, weight in enumerate(weights):
            coef_ref[at, tile : tile + 1] = jnp.sum(weight * inverse, axis=0, keepdims=True)
    coef_ref[10] = 0.5 * shifts[1]

    shift = jnp.concatenate([column] + [part[:2] for part in shifts], axis=0)
    root = jnp.sqrt(shift * (shift + 4.0))
    decay = 2.0 / (2.0 + shift + root)
    two = decay * decay
    four = two * two
    eight = four * four
    sixteen = eight * eight
    powers = [jnp.ones_like(decay)]
    for _ in range(8):
        powers.append(powers[-1] * (sixteen * sixteen))
    scale = 1.0 / (root * (1.0 - powers[8] * two))
    none = jnp.zeros_like(decay)
    left_u, right_u = [none] * 9, [none] * 9
    left_w, right_w = [none] * 9, [none] * 9
    for b in range(1, 8):
        left_u[b], right_u[b] = 1.0 - powers[b], 1.0 - powers[b] * two
        left_w[b], right_w[b] = 1.0 - powers[8 - b] * two, 1.0 - powers[8 - b]
    for b in range(8):
        above = b + 1 if b < 7 else 8
        if b > 0:
            over_u, over_w = 1.0 / right_u[b], 1.0 / left_w[b]
            if b < 7:
                joint_ref[b + 1, 0] = sixteen * left_w[b + 1] * over_w
            if b > 1:
                joint_ref[b - 1, 1] = sixteen * right_u[b - 1] * over_u
            joint_ref[b, 2] = decay * left_u[b] * over_u
            joint_ref[b, 3] = decay * right_w[b] * over_w
        joint_ref[b, 4] = 1.0 + scale * decay * left_u[above] * right_w[above]
        joint_ref[b, 5] = scale * sixteen * left_u[b] * left_w[above]
        joint_ref[b, 6] = 1.0 + scale * decay * left_u[b] * right_w[b]
        joint_ref[b, 7] = scale * sixteen * right_u[b] * right_w[above]


def advect_kernel(first_ref, second_ref, left_ref, right_ref, out_ref):
    lanes = lane_ids(NZ)
    first, last = lanes == 0, lanes == LANES - 1
    left, right = left_ref[...], right_ref[...]
    half = jnp.where(lax.axis_index("xs_1") == 0, 0.5, -0.5)

    def value(field, slot):
        return (first_ref, second_ref)[slot][field]

    def slopes(field, slot):
        x = value(field, slot)
        at = 2 * field + 1 - slot
        up = jnp.where(last, pltpu.roll(right, (LANES - 1 - at) % LANES, 1), pltpu.roll(x, LANES - 1, 1))
        down = jnp.where(first, pltpu.roll(left, (LANES - at) % LANES, 1), pltpu.roll(x, 1, 1))
        along_x = (up - down) * 0.5
        along_y = value(field, 1) * half if slot == 0 else value(field, 0) * -half
        along_z = (pltpu.roll(x, NZ - 1, 0) - pltpu.roll(x, 1, 0)) * 0.5
        return along_x, along_y, along_z

    for field in range(4):
        for slot in range(2):
            grad = slopes(field, slot)
            base_grad = slopes(field + 4, slot)
            advect = jnp.zeros((NZ, LANES), jnp.float32)
            for axis in range(3):
                advect += value(4 + axis, slot) * grad[axis]
                advect += value(axis, slot) * base_grad[axis]
            result = value(field, slot) - ADV_STEP * advect
            if field == 1:
                result += BUOYANCY * value(3, slot)
            out_ref[field, slot] = result


def update_kernel(part_ref, first_ref, second_ref, inner_ref, outer_ref, table_ref, out_ref):
    core = lax.axis_index("xs_1")
    step = ADV_STEP * jnp.where(core == 0, 0.5, -0.5)
    sides = ((first_ref, outer_ref, step), (second_ref, inner_ref, -step))
    for field in range(4):
        updated = []
        for slot, (own_ref, far_ref, weight) in enumerate(sides):
            far = own_ref[5] * far_ref[field] + own_ref[1] * far_ref[field + 4]
            updated.append(part_ref[field, slot] + weight * far)
        rows = (
            jnp.where(core == 0, updated[0], updated[1]),
            jnp.where(core == 0, updated[1], updated[0]),
        )
        if field < 3:
            kind = field // 2
            modes = table_times(table_ref[kind], jnp.concatenate(rows, axis=1))
            rows = (modes[:, :LANES], modes[:, LANES:])
        for row in range(2):
            out_ref[pl.ds(2 * field + row, NZ, stride=LINES), :] = rows[row]


def lanes_of(x, tile):
    return x[:, LANES * tile : LANES * (tile + 1)]


def side_by_side(parts):
    return jnp.concatenate(parts, axis=1)


def stream_kernel(
    in_ref, table_ref, wall_ref, marks_ref, stream_ref, inverse_ref, gain_ref, coef_ref, slope_ref, joint_ref,
    waves_ref, pressure_ref, out_ref, local_ref, ends_ref,
):
    def lines(part, s):
        return in_ref[pl.ds(LINES * s + part, LINES, stride=NZ), :]

    x = [jnp.concatenate([lines(part, s) for part in range(6)], axis=0) for s in range(BLOCKS)]
    s04, d04 = x[0] + x[4], x[0] - x[4]
    s26, d26 = x[2] + x[6], x[2] - x[6]
    s15, d15 = x[1] + x[5], x[1] - x[5]
    s37, d37 = x[3] + x[7], x[3] - x[7]
    even, odd = s04 + s26, s15 + s37
    minus, plus = HALF * (d15 - d37), HALF * (d15 + d37)
    parts = [
        (even + odd, even - odd),
        (d04 + minus, plus + d26),
        (s04 - s26, s15 - s37),
        (d04 - minus, plus - d26),
    ]
    modes = side_by_side(
        [times_table(side_by_side(parts[g]), table_ref[0, g], table_ref[1, g]) for g in range(4)]
    )
    heat = side_by_side(
        [jnp.concatenate([lines(6, s), lines(7, s)], axis=0) for s in range(BLOCKS)]
    )
    fields = [modes[ROWS * f : ROWS * (f + 1)] for f in range(3)] + [heat]
    waves = wall_times(wall_ref, SINE, side_by_side(fields))
    waves_ref[...] = waves
    rise = wall_times(wall_ref, SINE_SLOPE, fields[1])
    head = marks_ref[1]
    span = slope_ref[0:1, :]

    def wave(field, tile):
        return lanes_of(waves, BLOCKS * field + tile)

    pressure = []
    for tile in range(BLOCKS):
        slope = stream_ref[1, tile : tile + 1]
        source = slope * pltpu.roll(wave(0, tile), 64, 1) + lanes_of(rise, tile)
        source += span * wave(2, tile)
        pressure.append(-lanes_of(inverse_ref, tile) * source)
    joined = side_by_side(pressure)
    pressure_ref[...] = joined
    lift = wall_times(wall_ref, LIFT, joined)

    def ends(f):
        weighted = f * head
        total = weighted[:LINES] + weighted[LINES:]
        total = total + pltpu.roll(total, 4, 0)
        total = total + pltpu.roll(total, 2, 0)
        even, odd = total[:1], total[1:2]
        return even - odd, even + odd

    for tile in range(BLOCKS):
        p = pressure[tile]
        last, first = ends(p)
        half = coef_ref[10, tile : tile + 1]
        rows = lanes_of(fields[1], tile)
        values = [(last + 0.5 * rows[ROWS - 1 :], first - 0.5 * rows[:1])]
        slope = stream_ref[1, tile : tile + 1]
        corrected = (
            wave(0, tile) - slope * pltpu.roll(p, 64, 1),
            wave(1, tile) - lanes_of(lift, tile),
            wave(2, tile) + span * p,
            wave(3, tile),
        )
        for field in range(4):
            high, low = ends(gain_ref[field] * corrected[field])
            if field == 1:
                high, low = high + half * last, low - half * first
            values.append((high, low))
        for at, (high, low) in enumerate(values):
            ends_ref[0, LINES * at + tile : LINES * at + tile + 1] = high
            ends_ref[1, LINES * at + tile : LINES * at + tile + 1] = low
    own = lax.axis_index("wall_0")
    high, low = ends_ref[0], ends_ref[1]
    coefs = [joint_ref[own, at] for at in range(4, 8)]
    for system in range(5):
        part = slice(LINES * system, LINES * (system + 1))
        rows = slice(0, LINES) if system == 0 else slice(2 * system + 6, 2 * system + 7)
        up, down = high[part], low[part]
        upward = coefs[0][rows] * up + coefs[1][rows] * down
        downward = coefs[2][rows] * down + coefs[3][rows] * up
        if system > 0:
            local_ref[0, system - 1] = upward
            local_ref[1, system - 1] = downward
        for b in range(8):
            if system == 0:
                out_ref[b, 0] = upward
                out_ref[b, 1] = downward
            else:
                out_ref[b, system + 1] = jnp.where(own < b, upward, downward)


def joints(joint_ref, rows, upward, downward):
    rise, fall = [None, upward[0]], [None] * 7 + [downward[7]]
    for b in range(2, 8):
        rise.append(upward[b - 1] + joint_ref[b, 0, rows] * rise[b - 1])
    for b in range(6, 0, -1):
        fall[b] = downward[b] + joint_ref[b, 1, rows] * fall[b + 1]
    none = jnp.zeros_like(upward[0])
    alpha = [none] + [rise[b] + joint_ref[b, 2, rows] * fall[b] for b in range(1, 8)]
    beta = [fall[b] + joint_ref[b, 3, rows] * rise[b] for b in range(1, 8)] + [none]
    return alpha, beta


def stream_back_kernel(
    in_ref, local_ref, waves_ref, pressure_ref, table_ref, wall_ref, marks_ref, stream_ref, inverse_ref, gain_ref, share_ref, coef_ref, slope_ref, joint_ref,
    out_ref, alpha_ref, beta_ref,
):
    head, tail = marks_ref[1], marks_ref[2]
    span = slope_ref[0:1, :]
    alpha, beta = joints(
        joint_ref, pl.ds(0, 8), [in_ref[b, 0] for b in range(8)], [in_ref[b, 1] for b in range(8)]
    )
    own = lax.axis_index("wall_0")
    coef = [coef_ref[at] for at in range(11)]
    slope = stream_ref[1]
    upward, downward = [[], [], [], []], [[], [], [], []]
    for b in range(8):
        one, two = alpha[b], beta[b]
        one_x, two_x = slope * pltpu.roll(one, 64, 1), slope * pltpu.roll(two, 64, 1)
        one_z, two_z = span * one, span * two
        high = [
            -(one_x * coef[1] + two_x * coef[0]),
            coef[10] * (one * coef[9] + two * coef[8]) - (one * coef[6] + two * coef[7]),
            one_z * coef[3] + two_z * coef[2],
        ]
        low = [
            -(one_x * coef[0] + two_x * coef[1]),
            -coef[10] * (one * coef[8] + two * coef[9]) - (one * coef[4] + two * coef[5]),
            one_z * coef[2] + two_z * coef[3],
        ]
        for field in range(4):
            up, down = local_ref[0, field], local_ref[1, field]
            up = jnp.where(own == b, up, in_ref[b, field + 2])
            down = jnp.where(own == b, down, in_ref[b, field + 2])
            if field < 3:
                coefs = [joint_ref[b, at, pl.ds(8 + 2 * field, 1)] for at in range(4, 8)]
                up += coefs[0] * high[field] + coefs[1] * low[field]
                down += coefs[2] * low[field] + coefs[3] * high[field]
            upward[field].append(up)
            downward[field].append(down)
    pairs = [
        joints(joint_ref, pl.ds(8 + 2 * field, 1), upward[field], downward[field])
        for field in range(4)
    ]
    for b in range(8):
        for field in range(4):
            rows = slice(LINES * (field + 1), LINES * (field + 2))
            alpha_ref[b, rows] = pairs[field][0][b]
            beta_ref[b, rows] = pairs[field][1][b]
    for b in range(8):
        alpha_ref[b, :8] = alpha[b]
        beta_ref[b, :8] = beta[b]

    def outside(field, tile):
        at = LINES * field + tile
        return alpha_ref[own, at : at + 1] * head + beta_ref[own, at : at + 1] * tail

    def wave(field, tile):
        return lanes_of(waves_ref, BLOCKS * field + tile)

    pressure = [
        lanes_of(pressure_ref, tile) + lanes_of(inverse_ref, tile) * outside(0, tile)
        for tile in range(BLOCKS)
    ]
    lift = wall_times(wall_ref, LIFT, side_by_side(pressure))
    solved = [[], [], [], []]
    for tile in range(BLOCKS):
        p = pressure[tile]
        corrected = (
            wave(0, tile) - stream_ref[1, tile : tile + 1] * pltpu.roll(p, 64, 1),
            wave(1, tile) - lanes_of(lift, tile),
            wave(2, tile) + span * p,
            wave(3, tile),
        )
        for field in range(4):
            value = gain_ref[field] * corrected[field]
            solved[field].append(value + share_ref[field] * outside(field + 1, tile))
    rows = wall_times(wall_ref, SINE_BACK, side_by_side(sum(solved, [])))
    fields = [rows[:, NX * f : NX * (f + 1)] for f in range(4)]
    modes = jnp.concatenate(fields[:3], axis=0)
    parts = []
    for group in range(4):
        cells = times_table(
            modes[:, 2 * LANES * group : 2 * LANES * (group + 1)],
            table_ref[0, group], table_ref[1, group],
        )
        parts.append((cells[:, :LANES], cells[:, LANES:]))
    (c0, c4), (c1, s1), (c2, s2), (c3, s3) = parts
    sum04, dif04 = c0 + c4, c0 - c4
    sum13, dif13 = c1 + c3, HALF * (c1 - c3)
    plus13, minus13 = HALF * (s1 + s3), s1 - s3
    outer_a, outer_b = sum04 + c2, sum04 - c2
    inner_a, inner_b = dif04 + s2, dif04 - s2
    cells = [
        outer_a + sum13,
        inner_a + (dif13 + plus13),
        outer_b + minus13,
        inner_b + (plus13 - dif13),
        outer_a - sum13,
        inner_a - (dif13 + plus13),
        outer_b - minus13,
        inner_b - (plus13 - dif13),
    ]
    for s in range(BLOCKS):
        for part in range(8):
            if part < 6:
                value = cells[s][LINES * part : LINES * (part + 1)]
            else:
                value = lanes_of(fields[3], s)[LINES * (part - 6) : LINES * (part - 5)]
            out_ref[pl.ds(LINES * s + part, LINES, stride=NZ), :] = value


PAIRS = ((0, 0), (0, 1), (0, 2), (1, 1), (1, 2), (2, 2))


def folded(x):
    total = x[:LINES]
    for part in range(1, NZ // LINES):
        total += x[LINES * part : LINES * (part + 1)]
    return total


def cells_kernel(in_ref, vec_ref, table_ref, cur_ref, sums_ref):
    sums = [jnp.zeros((LINES, LANES), jnp.float32) for _ in range(10)]
    for field in range(4):
        for row in range(2):
            part = 2 * field + row
            cells = in_ref[pl.ds(part, NZ, stride=LINES), :]
            if field < 3:
                cells = table_times(table_ref[field // 2], cells)
            cur_ref[field, row] = cells
            vectors = [vec_ref[q, field, row] for q in range(3)]
            for q in range(3):
                sums[q] += folded(vectors[q] * cells)
            sums[3] += folded(cells * cells)
            for at, (q, p) in enumerate(PAIRS):
                sums[4 + at] += folded(vectors[q] * vectors[p])
    lanes = lane_ids(16)
    packed = jnp.zeros((16, LANES), jnp.float32)
    for at in range(10):
        total = jnp.sum(jnp.sum(sums[at], axis=0, keepdims=True), axis=1, keepdims=True)
        packed = jnp.where(lanes == at, total, packed)
    sums_ref[...] = packed


def residual_kernel(sums_ref, cur_ref, vec_ref, out_ref, hess_ref):
    entries = float(4 * NX * NY * NZ)
    totals = jnp.sum(sums_ref[...], axis=0, keepdims=True) * (1.0 / entries)
    lanes = lane_ids(1)

    def pick(at):
        return jnp.sum(jnp.where(lanes == at, totals, 0.0), axis=1, keepdims=True)

    values = [pick(at) for at in range(10)]
    products = values[:3]
    square = values[3]
    for q in range(3):
        square = square - 2.0 * products[q] * products[q]
    for at, (q, p) in enumerate(PAIRS):
        twice = 1.0 if q == p else 2.0
        square = square + twice * products[q] * products[p] * values[4 + at]
    norm = jnp.sqrt(square + EPSILON)
    for q in range(3):
        hess_ref[q] = jnp.sum(products[q])
    hess_ref[3] = jnp.sum(norm)
    scale = 1.0 / norm
    for field in range(4):
        for row in range(2):
            left = cur_ref[field, row]
            for q in range(3):
                left = left - products[q] * vec_ref[q, field, row]
            out_ref[field, row] = left * scale


VMEM = pl.BlockSpec(memory_space=pltpu.VMEM)
SMALL = pltpu.CompilerParams(vmem_limit_bytes=8 * 1024 * 1024)
LARGE = pltpu.CompilerParams(vmem_limit_bytes=54500 * 1024)
SMEM = pl.BlockSpec(memory_space=pltpu.SMEM)


def f32(*dims):
    return jax.ShapeDtypeStruct(dims, jnp.float32)


def shards(krylov_basis, base_state, diffusivity):
    span, span_eigen, span_slope = spanwise_tables()
    span = np.stack([span, span[np.arange(NZ) ^ 1]])
    span_columns = np.stack([span_eigen.reshape(-1), span_slope.reshape(-1)], axis=1)
    span_columns = np.broadcast_to(span_columns[:, :, None], (NZ, 2, LANES)).astype(np.float32)
    stream, stream_columns = stream_tables()
    wall, marks = block_tables()
    stream = np.stack(split(stream))
    span, span_back = joined(span), joined(span.transpose(0, 2, 1))

    rows = f32(8, NZ, LANES)
    first, second = pl.pallas_call(
        copy_kernel,
        in_specs=[pl.BlockSpec(memory_space=pltpu.HBM)] * 2,
        out_specs=[VMEM] * 2,
        out_shape=[rows, rows],
        scratch_shapes=[pltpu.SemaphoreType.DMA((16,))],
        compiler_params=LARGE,
        name="copy",
    )(krylov_basis, base_state)
    size, walls = lax.axis_size(XS), lax.axis_size(WALL)
    down = [[(size * (i + 1) + s, size * i + s) for i in range(walls - 1)] for s in range(size)]
    up = [[(b, a) for a, b in pairs] for pairs in down]
    inner = lax.ppermute(first, WALL + XS, sum([(down, up)[s % 2][s] for s in range(size)], []))
    outer = lax.ppermute(second, WALL + XS, sum([(up, down)[s % 2][s] for s in range(size)], []))
    low_x, high_x, inverse, gain, share, coef, slope, joint = pl.pallas_call(
        edges_kernel,
        in_specs=[SMEM] + [VMEM] * 6,
        out_specs=[VMEM] * 8,
        out_shape=[
            f32(NZ, LANES), f32(NZ, LANES), f32(ROWS, NX), f32(4, ROWS, LANES),
            f32(4, ROWS, LANES), f32(11, LINES, LANES), f32(LINES, LANES), f32(8, 8, ROWS, LANES),
        ],
        compiler_params=SMALL,
        name="edges",
    )(
        diffusivity, first, second, marks, stream_columns, span_columns, wall
    )
    right = lax.ppermute(low_x, XS, [((i + 1) % size, i) for i in range(size)])
    left = lax.ppermute(high_x, XS, [(i, (i + 1) % size) for i in range(size)])

    plane = ("wall_1",) + XS
    part = pl.pallas_call(
        advect_kernel,
        in_specs=[VMEM] * 4,
        out_specs=VMEM,
        out_shape=f32(4, 2, NZ, LANES),
        compiler_params=SMALL,
        name="advect",
    )(first, second, left, right)
    modes = pl.pallas_call(
        update_kernel,
        in_specs=[VMEM] * 6,
        out_specs=VMEM,
        out_shape=f32(NZ * LINES, LANES),
        compiler_params=SMALL,
        name="update",
    )(part, first, second, inner, outer, span)
    lines = lax.all_to_all(modes.reshape(NZ, LINES, LANES), plane, 0, 0, tiled=True)
    waves, pressure, ends, local = pl.pallas_call(
        stream_kernel,
        in_specs=[VMEM] * 10,
        out_specs=[VMEM] * 4,
        out_shape=[
            f32(ROWS, 4 * NX), f32(ROWS, NX), f32(8, 6, LINES, LANES), f32(2, 4, LINES, LANES)
        ],
        scratch_shapes=[pltpu.VMEM((2, 40, LANES), jnp.float32)],
        compiler_params=SMALL,
        name="stream",
    )(
        lines.reshape(-1, LANES), stream, wall, marks, stream_columns, inverse, gain, coef, slope,
        joint,
    )
    ends = lax.all_to_all(ends, "wall_0", 0, 0, tiled=True)
    lines = pl.pallas_call(
        stream_back_kernel,
        in_specs=[VMEM] * 14,
        out_specs=VMEM,
        out_shape=f32(NZ * LINES, LANES),
        scratch_shapes=[pltpu.VMEM((8, 40, LANES), jnp.float32)] * 2,
        compiler_params=SMALL,
        name="stream_back",
    )(
        ends, local, waves, pressure, stream.transpose(0, 1, 3, 2), wall, marks, stream_columns,
        inverse, gain, share, coef, slope, joint,
    )
    modes = lax.all_to_all(lines.reshape(NZ, LINES, LANES), plane, 0, 0, tiled=True)
    current, sums = pl.pallas_call(
        cells_kernel,
        in_specs=[VMEM] * 3,
        out_specs=[VMEM] * 2,
        out_shape=[f32(4, 2, NZ, LANES), f32(16, LANES)],
        compiler_params=SMALL,
        name="cells",
    )(modes.reshape(-1, LANES), krylov_basis, span_back)
    sums = lax.all_to_all(sums, ("wall_0", "xs_1"), 0, 0, tiled=True).sum(axis=0)
    sums = jnp.broadcast_to(sums, (32, LANES))
    sums = lax.all_to_all(sums, ("wall_1", "xs_0"), 0, 0, tiled=True)
    new_vector, hessenberg = pl.pallas_call(
        residual_kernel,
        in_specs=[VMEM] * 3,
        out_specs=[VMEM, SMEM],
        out_shape=[f32(4, 2, NZ, LANES), f32(4)],
        compiler_params=SMALL,
        name="residual",
    )(sums, current, krylov_basis)
    return new_vector, hessenberg


def solution(mesh):
    torus = Mesh(mesh.devices.reshape(8, 8, 4, 2), ("wall_0", "wall_1", "xs_0", "xs_1"))
    return jax.shard_map(
        shards,
        mesh=torus,
        in_specs=(P(None, None, WALL, None, XS), P(None, WALL, None, XS), P()),
        out_specs=(P(None, WALL, None, XS), P()),
        check_vma=False,
    )
```

```python
import math

import jax
import jax.numpy as jnp
import ml_dtypes
import numpy as np
from jax import lax
from jax.experimental import pallas as pl
from jax.experimental.pallas import tpu as pltpu
from jax.sharding import Mesh
from jax.sharding import PartitionSpec as P

WALL = ("wall_0", "wall_1")
XS = ("xs_0", "xs_1")

ADV_STEP = 0.2
BUOYANCY = 0.5
SCREENING = 0.004
EPSILON = 1e-06

NX, NY, NZ = 1024, 128, 64
LINES, LANES, BLOCKS = 8, 128, 8
ROWS = 16
HALF = math.sqrt(0.5)


def split(table):
    high = table.astype(ml_dtypes.bfloat16)
    low = (table - high.astype(np.float64)).astype(ml_dtypes.bfloat16)
    return high, low


def joined(table):
    high, low = split(table)
    return np.concatenate([high, high, low], axis=-1)


def spanwise_tables():
    cells = np.arange(NZ)
    table = np.zeros((NZ, NZ))
    eigen = np.zeros((NZ // 2, 2))
    slope = np.zeros((NZ // 2, 2))
    for pair in range(NZ // 2):
        if pair == 0:
            table[0] = 1.0 / math.sqrt(NZ)
            table[1] = np.cos(math.pi * cells) / math.sqrt(NZ)
            eigen[0] = (0.0, 4.0)
            continue
        angle = 2.0 * math.pi * (cells * pair % NZ) / NZ
        table[2 * pair] = np.cos(angle) * math.sqrt(2.0 / NZ)
        table[2 * pair + 1] = np.sin(angle) * math.sqrt(2.0 / NZ)
        eigen[pair] = 4.0 * math.sin(math.pi * pair / NZ) ** 2
        wave = math.sin(2.0 * math.pi * pair / NZ)
        slope[pair] = (wave, -wave)
    return table, eigen, slope


def stream_tables():
    cells = np.arange(LANES)
    weights = np.zeros((4, 2 * LANES, 2 * LANES))
    eigen = np.zeros((8, 2, 64))
    slope = np.zeros((8, 2, 64))
    for tile in range(8):
        group = tile // 2
        base = (0, 4)[tile] if group == 0 else group
        first = 0 if group == 0 else 64 * (tile % 2)
        for slot in range(64):
            wave = 8 * (first + slot) + base
            at = (tile % 2) * LANES + slot
            angle = 2.0 * math.pi * (cells * wave % NX) / NX
            scale = math.sqrt(2.0 / NX)
            if wave == 0:
                alternate = np.cos(math.pi * cells)
                weights[0, :LANES, at] = 1.0 / math.sqrt(NX)
                weights[0, :LANES, at + 64] = alternate / math.sqrt(NX)
                eigen[tile, :, slot] = (0.0, 4.0)
                continue
            eigen[tile, :, slot] = 4.0 * math.sin(math.pi * wave / NX) ** 2
            rise = math.sin(2.0 * math.pi * wave / NX)
            slope[tile, :, slot] = (rise, -rise)
            cos, sin = scale * np.cos(angle), scale * np.sin(angle)
            if group == 0:
                rows = slice((tile % 2) * LANES, (tile % 2 + 1) * LANES)
                weights[0, rows, at] = cos
                weights[0, rows, at + 64] = sin
            else:
                weights[group, :LANES, at] = cos
                weights[group, LANES:, at] = -sin
                weights[group, :LANES, at + 64] = sin
                weights[group, LANES:, at + 64] = cos
    columns = np.stack([eigen.reshape(8, LANES), slope.reshape(8, LANES)])
    return weights, columns.astype(np.float32)


def block_tables():
    order = np.arange(1, ROWS + 1)
    sine = np.sin(math.pi * np.outer(order, order) / (ROWS + 1))
    sine = sine * math.sqrt(2.0 / (ROWS + 1))
    shift = np.eye(ROWS, k=1)
    slope = 0.5 * (shift - shift.T)
    eigen = 2.0 - 2.0 * np.cos(math.pi * order / (ROWS + 1))
    rows = np.concatenate([np.arange(0, ROWS, 2), np.arange(1, ROWS, 2)])
    marks = np.stack([eigen, sine[:, 0], sine[:, ROWS - 1]])
    marks = np.broadcast_to(marks[:, :, None], (3, ROWS, LANES)).astype(np.float32)
    lift = sine @ slope @ sine
    tables = np.stack([sine[:, rows], (sine @ slope)[:, rows], lift, sine[:, rows].T, lift.T])
    return joined(tables), marks


def halves(x):
    high = x.astype(jnp.bfloat16)
    low = (x - high.astype(jnp.float32)).astype(jnp.bfloat16)
    return high, low


def dot(a, b):
    return jnp.dot(a, b, preferred_element_type=jnp.float32)


def times_table(x, high_table, low_table):
    high, low = halves(x)
    both = dot(jnp.concatenate([high, low], axis=0), high_table)
    rows = x.shape[0]
    return both[:rows] + (both[rows:] + dot(high, low_table))


SINE, SINE_SLOPE, LIFT, SINE_BACK, LIFT_BACK = range(5)


def wall_times(ref, which, x):
    return table_times(ref[which], x)


def table_times(table, x):
    high, low = halves(x)
    return dot(table, jnp.concatenate([high, low, high], axis=0))


def lane_ids(rows):
    return lax.broadcasted_iota(jnp.int32, (rows, LANES), 1)


def copy_kernel(vec_ref, base_ref, first_ref, second_ref, sems):
    core = lax.axis_index("xs_1")
    copies = []
    for slot, ref in enumerate((first_ref, second_ref)):
        row = core if slot == 0 else 1 - core
        for field in range(4):
            copies.append((vec_ref.at[2, field, row], ref.at[field]))
            copies.append((base_ref.at[field, row], ref.at[4 + field]))
    copies = [
        pltpu.make_async_copy(source, target, sems.at[at])
        for at, (source, target) in enumerate(copies)
    ]
    for copy in copies:
        copy.start()
    for copy in copies:
        copy.wait()


def edges_kernel(
    diff_ref, first_ref, second_ref, marks_ref, stream_ref, span_ref, wall_ref,
    low_x, high_x, inverse_ref, gain_ref, share_ref, coef_ref, slope_ref, joint_ref,
):
    lanes = lane_ids(NZ)
    low = jnp.zeros((NZ, LANES), jnp.float32)
    high = jnp.zeros((NZ, LANES), jnp.float32)
    for field in range(8):
        for slot, ref in enumerate((first_ref, second_ref)):
            block = ref[field]
            at = 2 * field + slot
            low = jnp.where(lanes == at, pltpu.roll(block, at, 1), low)
            high = jnp.where(lanes == at, pltpu.roll(block, (at + 1) % LANES, 1), high)
    low_x[...] = low
    high_x[...] = high

    slot = lax.axis_index("wall_1") * 8 + lax.axis_index("xs_0") * 2 + lax.axis_index("xs_1")
    span = span_ref[slot]
    column = stream_ref[0] + (span[0:1] + SCREENING)
    slope_ref[...] = jnp.broadcast_to(span[1:2], (LINES, LANES))
    eigen, head, tail = marks_ref[0], marks_ref[1], marks_ref[2]
    shifts = [1.0 / (jnp.zeros((LINES, LANES), jnp.float32) + diff_ref[f]) for f in range(4)]
    gains = []
    for field in range(4):
        shift = jnp.concatenate([shifts[field]] * 2, axis=0)
        share = 1.0 / (eigen + shift)
        gains.append(shift * share)
        share_ref[field] = share
        gain_ref[field] = gains[field]
    head_lift = wall_times(wall_ref, LIFT_BACK, head * gains[1])
    tail_lift = wall_times(wall_ref, LIFT_BACK, tail * gains[1])
    weights = [
        gains[0] * head * head, gains[0] * head * tail,
        gains[2] * head * head, gains[2] * head * tail,
        head_lift * head, head_lift * tail, tail_lift * head, tail_lift * tail,
        head * head, head * tail,
    ]
    for tile in range(BLOCKS):
        inverse = 1.0 / (eigen + column[tile : tile + 1])
        inverse_ref[:, LANES * tile : LANES * (tile + 1)] = inverse
        for at, weight in enumerate(weights):
            coef_ref[at, tile : tile + 1] = jnp.sum(weight * inverse, axis=0, keepdims=True)
    coef_ref[10] = 0.5 * shifts[1]

    shift = jnp.concatenate([column] + [part[:2] for part in shifts], axis=0)
    root = jnp.sqrt(shift * (shift + 4.0))
    decay = 2.0 / (2.0 + shift + root)
    two = decay * decay
    four = two * two
    eight = four * four
    sixteen = eight * eight
    powers = [jnp.ones_like(decay)]
    for _ in range(8):
        powers.append(powers[-1] * (sixteen * sixteen))
    scale = 1.0 / (root * (1.0 - powers[8] * two))
    none = jnp.zeros_like(decay)
    left_u, right_u = [none] * 9, [none] * 9
    left_w, right_w = [none] * 9, [none] * 9
    for b in range(1, 8):
        left_u[b], right_u[b] = 1.0 - powers[b], 1.0 - powers[b] * two
        left_w[b], right_w[b] = 1.0 - powers[8 - b] * two, 1.0 - powers[8 - b]
    for b in range(8):
        above = b + 1 if b < 7 else 8
        if b > 0:
            over_u, over_w = 1.0 / right_u[b], 1.0 / left_w[b]
            if b < 7:
                joint_ref[b + 1, 0] = sixteen * left_w[b + 1] * over_w
            if b > 1:
                joint_ref[b - 1, 1] = sixteen * right_u[b - 1] * over_u
            joint_ref[b, 2] = decay * left_u[b] * over_u
            joint_ref[b, 3] = decay * right_w[b] * over_w
        joint_ref[b, 4] = 1.0 + scale * decay * left_u[above] * right_w[above]
        joint_ref[b, 5] = scale * sixteen * left_u[b] * left_w[above]
        joint_ref[b, 6] = 1.0 + scale * decay * left_u[b] * right_w[b]
        joint_ref[b, 7] = scale * sixteen * right_u[b] * right_w[above]


def advect_kernel(first_ref, second_ref, left_ref, right_ref, out_ref):
    lanes = lane_ids(NZ)
    first, last = lanes == 0, lanes == LANES - 1
    left, right = left_ref[...], right_ref[...]
    half = jnp.where(lax.axis_index("xs_1") == 0, 0.5, -0.5)

    def value(field, slot):
        return (first_ref, second_ref)[slot][field]

    def slopes(field, slot):
        x = value(field, slot)
        at = 2 * field + 1 - slot
        up = jnp.where(last, pltpu.roll(right, (LANES - 1 - at) % LANES, 1), pltpu.roll(x, LANES - 1, 1))
        down = jnp.where(first, pltpu.roll(left, (LANES - at) % LANES, 1), pltpu.roll(x, 1, 1))
        along_x = (up - down) * 0.5
        along_y = value(field, 1) * half if slot == 0 else value(field, 0) * -half
        along_z = (pltpu.roll(x, NZ - 1, 0) - pltpu.roll(x, 1, 0)) * 0.5
        return along_x, along_y, along_z

    for field in range(4):
        for slot in range(2):
            grad = slopes(field, slot)
            base_grad = slopes(field + 4, slot)
            advect = jnp.zeros((NZ, LANES), jnp.float32)
            for axis in range(3):
                advect += value(4 + axis, slot) * grad[axis]
                advect += value(axis, slot) * base_grad[axis]
            result = value(field, slot) - ADV_STEP * advect
            if field == 1:
                result += BUOYANCY * value(3, slot)
            out_ref[field, slot] = result


def update_kernel(part_ref, first_ref, second_ref, inner_ref, outer_ref, table_ref, out_ref):
    core = lax.axis_index("xs_1")
    step = ADV_STEP * jnp.where(core == 0, 0.5, -0.5)
    sides = ((first_ref, outer_ref, step), (second_ref, inner_ref, -step))
    for field in range(4):
        updated = []
        for slot, (own_ref, far_ref, weight) in enumerate(sides):
            far = own_ref[5] * far_ref[field] + own_ref[1] * far_ref[field + 4]
            updated.append(part_ref[field, slot] + weight * far)
        rows = (
            jnp.where(core == 0, updated[0], updated[1]),
            jnp.where(core == 0, updated[1], updated[0]),
        )
        if field < 3:
            kind = field // 2
            modes = table_times(table_ref[kind], jnp.concatenate(rows, axis=1))
            rows = (modes[:, :LANES], modes[:, LANES:])
        for row in range(2):
            out_ref[pl.ds(2 * field + row, NZ, stride=LINES), :] = rows[row]


def lanes_of(x, tile):
    return x[:, LANES * tile : LANES * (tile + 1)]


def side_by_side(parts):
    return jnp.concatenate(parts, axis=1)


def stream_kernel(
    in_ref, table_ref, wall_ref, marks_ref, stream_ref, inverse_ref, gain_ref, coef_ref, slope_ref, joint_ref,
    waves_ref, pressure_ref, out_ref, local_ref, ends_ref,
):
    def lines(part, s):
        return in_ref[pl.ds(LINES * s + part, LINES, stride=NZ), :]

    x = [jnp.concatenate([lines(part, s) for part in range(6)], axis=0) for s in range(BLOCKS)]
    s04, d04 = x[0] + x[4], x[0] - x[4]
    s26, d26 = x[2] + x[6], x[2] - x[6]
    s15, d15 = x[1] + x[5], x[1] - x[5]
    s37, d37 = x[3] + x[7], x[3] - x[7]
    even, odd = s04 + s26, s15 + s37
    minus, plus = HALF * (d15 - d37), HALF * (d15 + d37)
    parts = [
        (even + odd, even - odd),
        (d04 + minus, plus + d26),
        (s04 - s26, s15 - s37),
        (d04 - minus, plus - d26),
    ]
    modes = side_by_side(
        [times_table(side_by_side(parts[g]), table_ref[0, g], table_ref[1, g]) for g in range(4)]
    )
    heat = side_by_side(
        [jnp.concatenate([lines(6, s), lines(7, s)], axis=0) for s in range(BLOCKS)]
    )
    fields = [modes[ROWS * f : ROWS * (f + 1)] for f in range(3)] + [heat]
    waves = wall_times(wall_ref, SINE, side_by_side(fields))
    waves_ref[...] = waves
    rise = wall_times(wall_ref, SINE_SLOPE, fields[1])
    head = marks_ref[1]
    span = slope_ref[0:1, :]

    def wave(field, tile):
        return lanes_of(waves, BLOCKS * field + tile)

    pressure = []
    for tile in range(BLOCKS):
        slope = stream_ref[1, tile : tile + 1]
        source = slope * pltpu.roll(wave(0, tile), 64, 1) + lanes_of(rise, tile)
        source += span * wave(2, tile)
        pressure.append(-lanes_of(inverse_ref, tile) * source)
    joined = side_by_side(pressure)
    pressure_ref[...] = joined
    lift = wall_times(wall_ref, LIFT, joined)

    def ends(f):
        weighted = f * head
        total = weighted[:LINES] + weighted[LINES:]
        total = total + pltpu.roll(total, 4, 0)
        total = total + pltpu.roll(total, 2, 0)
        even, odd = total[:1], total[1:2]
        return even - odd, even + odd

    for tile in range(BLOCKS):
        p = pressure[tile]
        last, first = ends(p)
        half = coef_ref[10, tile : tile + 1]
        rows = lanes_of(fields[1], tile)
        values = [(last + 0.5 * rows[ROWS - 1 :], first - 0.5 * rows[:1])]
        slope = stream_ref[1, tile : tile + 1]
        corrected = (
            wave(0, tile) - slope * pltpu.roll(p, 64, 1),
            wave(1, tile) - lanes_of(lift, tile),
            wave(2, tile) + span * p,
            wave(3, tile),
        )
        for field in range(4):
            high, low = ends(gain_ref[field] * corrected[field])
            if field == 1:
                high, low = high + half * last, low - half * first
            values.append((high, low))
        for at, (high, low) in enumerate(values):
            ends_ref[0, LINES * at + tile : LINES * at + tile + 1] = high
            ends_ref[1, LINES * at + tile : LINES * at + tile + 1] = low
    own = lax.axis_index("wall_0")
    high, low = ends_ref[0], ends_ref[1]
    coefs = [joint_ref[own, at] for at in range(4, 8)]
    for system in range(5):
        part = slice(LINES * system, LINES * (system + 1))
        rows = slice(0, LINES) if system == 0 else slice(2 * system + 6, 2 * system + 7)
        up, down = high[part], low[part]
        upward = coefs[0][rows] * up + coefs[1][rows] * down
        downward = coefs[2][rows] * down + coefs[3][rows] * up
        if system > 0:
            local_ref[0, system - 1] = upward
            local_ref[1, system - 1] = downward
        for b in range(8):
            if system == 0:
                out_ref[b, 0] = upward
                out_ref[b, 1] = downward
            else:
                out_ref[b, system + 1] = jnp.where(own < b, upward, downward)


def joints(joint_ref, rows, upward, downward):
    rise, fall = [None, upward[0]], [None] * 7 + [downward[7]]
    for b in range(2, 8):
        rise.append(upward[b - 1] + joint_ref[b, 0, rows] * rise[b - 1])
    for b in range(6, 0, -1):
        fall[b] = downward[b] + joint_ref[b, 1, rows] * fall[b + 1]
    none = jnp.zeros_like(upward[0])
    alpha = [none] + [rise[b] + joint_ref[b, 2, rows] * fall[b] for b in range(1, 8)]
    beta = [fall[b] + joint_ref[b, 3, rows] * rise[b] for b in range(1, 8)] + [none]
    return alpha, beta


def stream_back_kernel(
    in_ref, local_ref, waves_ref, pressure_ref, table_ref, wall_ref, marks_ref, stream_ref, inverse_ref, gain_ref, share_ref, coef_ref, slope_ref, joint_ref,
    out_ref, alpha_ref, beta_ref,
):
    head, tail = marks_ref[1], marks_ref[2]
    span = slope_ref[0:1, :]
    alpha, beta = joints(
        joint_ref, pl.ds(0, 8), [in_ref[b, 0] for b in range(8)], [in_ref[b, 1] for b in range(8)]
    )
    own = lax.axis_index("wall_0")
    coef = [coef_ref[at] for at in range(11)]
    slope = stream_ref[1]
    upward, downward = [[], [], [], []], [[], [], [], []]
    for b in range(8):
        one, two = alpha[b], beta[b]
        one_x, two_x = slope * pltpu.roll(one, 64, 1), slope * pltpu.roll(two, 64, 1)
        one_z, two_z = span * one, span * two
        high = [
            -(one_x * coef[1] + two_x * coef[0]),
            coef[10] * (one * coef[9] + two * coef[8]) - (one * coef[6] + two * coef[7]),
            one_z * coef[3] + two_z * coef[2],
        ]
        low = [
            -(one_x * coef[0] + two_x * coef[1]),
            -coef[10] * (one * coef[8] + two * coef[9]) - (one * coef[4] + two * coef[5]),
            one_z * coef[2] + two_z * coef[3],
        ]
        for field in range(4):
            up, down = local_ref[0, field], local_ref[1, field]
            up = jnp.where(own == b, up, in_ref[b, field + 2])
            down = jnp.where(own == b, down, in_ref[b, field + 2])
            if field < 3:
                coefs = [joint_ref[b, at, pl.ds(8 + 2 * field, 1)] for at in range(4, 8)]
                up += coefs[0] * high[field] + coefs[1] * low[field]
                down += coefs[2] * low[field] + coefs[3] * high[field]
            upward[field].append(up)
            downward[field].append(down)
    pairs = [
        joints(joint_ref, pl.ds(8 + 2 * field, 1), upward[field], downward[field])
        for field in range(4)
    ]
    for b in range(8):
        for field in range(4):
            rows = slice(LINES * (field + 1), LINES * (field + 2))
            alpha_ref[b, rows] = pairs[field][0][b]
            beta_ref[b, rows] = pairs[field][1][b]
    for b in range(8):
        alpha_ref[b, :8] = alpha[b]
        beta_ref[b, :8] = beta[b]

    def outside(field, tile):
        at = LINES * field + tile
        return alpha_ref[own, at : at + 1] * head + beta_ref[own, at : at + 1] * tail

    def wave(field, tile):
        return lanes_of(waves_ref, BLOCKS * field + tile)

    pressure = [
        lanes_of(pressure_ref, tile) + lanes_of(inverse_ref, tile) * outside(0, tile)
        for tile in range(BLOCKS)
    ]
    lift = wall_times(wall_ref, LIFT, side_by_side(pressure))
    solved = [[], [], [], []]
    for tile in range(BLOCKS):
        p = pressure[tile]
        corrected = (
            wave(0, tile) - stream_ref[1, tile : tile + 1] * pltpu.roll(p, 64, 1),
            wave(1, tile) - lanes_of(lift, tile),
            wave(2, tile) + span * p,
            wave(3, tile),
        )
        for field in range(4):
            value = gain_ref[field] * corrected[field]
            solved[field].append(value + share_ref[field] * outside(field + 1, tile))
    rows = wall_times(wall_ref, SINE_BACK, side_by_side(sum(solved, [])))
    fields = [rows[:, NX * f : NX * (f + 1)] for f in range(4)]
    modes = jnp.concatenate(fields[:3], axis=0)
    parts = []
    for group in range(4):
        cells = times_table(
            modes[:, 2 * LANES * group : 2 * LANES * (group + 1)],
            table_ref[0, group], table_ref[1, group],
        )
        parts.append((cells[:, :LANES], cells[:, LANES:]))
    (c0, c4), (c1, s1), (c2, s2), (c3, s3) = parts
    sum04, dif04 = c0 + c4, c0 - c4
    sum13, dif13 = c1 + c3, HALF * (c1 - c3)
    plus13, minus13 = HALF * (s1 + s3), s1 - s3
    outer_a, outer_b = sum04 + c2, sum04 - c2
    inner_a, inner_b = dif04 + s2, dif04 - s2
    cells = [
        outer_a + sum13,
        inner_a + (dif13 + plus13),
        outer_b + minus13,
        inner_b + (plus13 - dif13),
        outer_a - sum13,
        inner_a - (dif13 + plus13),
        outer_b - minus13,
        inner_b - (plus13 - dif13),
    ]
    for s in range(BLOCKS):
        for part in range(8):
            if part < 6:
                value = cells[s][LINES * part : LINES * (part + 1)]
            else:
                value = lanes_of(fields[3], s)[LINES * (part - 6) : LINES * (part - 5)]
            out_ref[pl.ds(LINES * s + part, LINES, stride=NZ), :] = value


PAIRS = ((0, 0), (0, 1), (0, 2), (1, 1), (1, 2), (2, 2))


def folded(x):
    total = x[:LINES]
    for part in range(1, NZ // LINES):
        total += x[LINES * part : LINES * (part + 1)]
    return total


def cells_kernel(in_ref, vec_ref, table_ref, cur_ref, sums_ref):
    sums = [jnp.zeros((LINES, LANES), jnp.float32) for _ in range(10)]
    for field in range(4):
        for row in range(2):
            part = 2 * field + row
            cells = in_ref[pl.ds(part, NZ, stride=LINES), :]
            if field < 3:
                cells = table_times(table_ref[field // 2], cells)
            cur_ref[field, row] = cells
            vectors = [vec_ref[q, field, row] for q in range(3)]
            for q in range(3):
                sums[q] += folded(vectors[q] * cells)
            sums[3] += folded(cells * cells)
            for at, (q, p) in enumerate(PAIRS):
                sums[4 + at] += folded(vectors[q] * vectors[p])
    lanes = lane_ids(16)
    packed = jnp.zeros((16, LANES), jnp.float32)
    for at in range(10):
        total = jnp.sum(jnp.sum(sums[at], axis=0, keepdims=True), axis=1, keepdims=True)
        packed = jnp.where(lanes == at, total, packed)
    sums_ref[...] = packed


def residual_kernel(sums_ref, cur_ref, vec_ref, out_ref, hess_ref):
    entries = float(4 * NX * NY * NZ)
    totals = jnp.sum(sums_ref[...], axis=0, keepdims=True) * (1.0 / entries)
    lanes = lane_ids(1)

    def pick(at):
        return jnp.sum(jnp.where(lanes == at, totals, 0.0), axis=1, keepdims=True)

    values = [pick(at) for at in range(10)]
    products = values[:3]
    square = values[3]
    for q in range(3):
        square = square - 2.0 * products[q] * products[q]
    for at, (q, p) in enumerate(PAIRS):
        twice = 1.0 if q == p else 2.0
        square = square + twice * products[q] * products[p] * values[4 + at]
    norm = jnp.sqrt(square + EPSILON)
    for q in range(3):
        hess_ref[q] = jnp.sum(products[q])
    hess_ref[3] = jnp.sum(norm)
    scale = 1.0 / norm
    for field in range(4):
        for row in range(2):
            left = cur_ref[field, row]
            for q in range(3):
                left = left - products[q] * vec_ref[q, field, row]
            out_ref[field, row] = left * scale


VMEM = pl.BlockSpec(memory_space=pltpu.VMEM)
SMALL = pltpu.CompilerParams(vmem_limit_bytes=8 * 1024 * 1024)
LARGE = pltpu.CompilerParams(vmem_limit_bytes=54500 * 1024)
SMEM = pl.BlockSpec(memory_space=pltpu.SMEM)


def f32(*dims):
    return jax.ShapeDtypeStruct(dims, jnp.float32)


def shards(krylov_basis, base_state, diffusivity):
    span, span_eigen, span_slope = spanwise_tables()
    span = np.stack([span, span[np.arange(NZ) ^ 1]])
    span_columns = np.stack([span_eigen.reshape(-1), span_slope.reshape(-1)], axis=1)
    span_columns = np.broadcast_to(span_columns[:, :, None], (NZ, 2, LANES)).astype(np.float32)
    stream, stream_columns = stream_tables()
    wall, marks = block_tables()
    stream = np.stack(split(stream))
    span, span_back = joined(span), joined(span.transpose(0, 2, 1))

    rows = f32(8, NZ, LANES)
    first, second = pl.pallas_call(
        copy_kernel,
        in_specs=[pl.BlockSpec(memory_space=pltpu.HBM)] * 2,
        out_specs=[VMEM] * 2,
        out_shape=[rows, rows],
        scratch_shapes=[pltpu.SemaphoreType.DMA((16,))],
        compiler_params=LARGE,
        name="copy",
    )(krylov_basis, base_state)
    size, walls = lax.axis_size(XS), lax.axis_size(WALL)
    down = [[(size * (i + 1) + s, size * i + s) for i in range(walls - 1)] for s in range(size)]
    up = [[(b, a) for a, b in pairs] for pairs in down]
    inner = lax.ppermute(first, WALL + XS, sum([(down, up)[s % 2][s] for s in range(size)], []))
    outer = lax.ppermute(second, WALL + XS, sum([(up, down)[s % 2][s] for s in range(size)], []))
    low_x, high_x, inverse, gain, share, coef, slope, joint = pl.pallas_call(
        edges_kernel,
        in_specs=[SMEM] + [VMEM] * 6,
        out_specs=[VMEM] * 8,
        out_shape=[
            f32(NZ, LANES), f32(NZ, LANES), f32(ROWS, NX), f32(4, ROWS, LANES),
            f32(4, ROWS, LANES), f32(11, LINES, LANES), f32(LINES, LANES), f32(8, 8, ROWS, LANES),
        ],
        compiler_params=SMALL,
        name="edges",
    )(
        diffusivity, first, second, marks, stream_columns, span_columns, wall
    )
    right = lax.ppermute(low_x, XS, [((i + 1) % size, i) for i in range(size)])
    left = lax.ppermute(high_x, XS, [(i, (i + 1) % size) for i in range(size)])

    plane = ("wall_1",) + XS
    part = pl.pallas_call(
        advect_kernel,
        in_specs=[VMEM] * 4,
        out_specs=VMEM,
        out_shape=f32(4, 2, NZ, LANES),
        compiler_params=SMALL,
        name="advect",
    )(first, second, left, right)
    modes = pl.pallas_call(
        update_kernel,
        in_specs=[VMEM] * 6,
        out_specs=VMEM,
        out_shape=f32(NZ * LINES, LANES),
        compiler_params=SMALL,
        name="update",
    )(part, first, second, inner, outer, span)
    lines = lax.all_to_all(modes.reshape(NZ, LINES, LANES), plane, 0, 0, tiled=True)
    waves, pressure, ends, local = pl.pallas_call(
        stream_kernel,
        in_specs=[VMEM] * 10,
        out_specs=[VMEM] * 4,
        out_shape=[
            f32(ROWS, 4 * NX), f32(ROWS, NX), f32(8, 6, LINES, LANES), f32(2, 4, LINES, LANES)
        ],
        scratch_shapes=[pltpu.VMEM((2, 40, LANES), jnp.float32)],
        compiler_params=SMALL,
        name="stream",
    )(
        lines.reshape(-1, LANES), stream, wall, marks, stream_columns, inverse, gain, coef, slope,
        joint,
    )
    ends = lax.all_to_all(ends, "wall_0", 0, 0, tiled=True)
    lines = pl.pallas_call(
        stream_back_kernel,
        in_specs=[VMEM] * 14,
        out_specs=VMEM,
        out_shape=f32(NZ * LINES, LANES),
        scratch_shapes=[pltpu.VMEM((8, 40, LANES), jnp.float32)] * 2,
        compiler_params=SMALL,
        name="stream_back",
    )(
        ends, local, waves, pressure, stream.transpose(0, 1, 3, 2), wall, marks, stream_columns,
        inverse, gain, share, coef, slope, joint,
    )
    modes = lax.all_to_all(lines.reshape(NZ, LINES, LANES), plane, 0, 0, tiled=True)
    current, sums = pl.pallas_call(
        cells_kernel,
        in_specs=[VMEM] * 3,
        out_specs=[VMEM] * 2,
        out_shape=[f32(4, 2, NZ, LANES), f32(16, LANES)],
        compiler_params=SMALL,
        name="cells",
    )(modes.reshape(-1, LANES), krylov_basis, span_back)
    sums = lax.all_to_all(sums, ("wall_0", "xs_1"), 0, 0, tiled=True).sum(axis=0)
    sums = jnp.broadcast_to(sums, (32, LANES))
    sums = lax.all_to_all(sums, ("wall_1", "xs_0"), 0, 0, tiled=True)
    new_vector, hessenberg = pl.pallas_call(
        residual_kernel,
        in_specs=[VMEM] * 3,
        out_specs=[VMEM, SMEM],
        out_shape=[f32(4, 2, NZ, LANES), f32(4)],
        compiler_params=SMALL,
        name="residual",
    )(sums, current, krylov_basis)
    return new_vector, hessenberg


def solution(mesh):
    torus = Mesh(mesh.devices.reshape(8, 8, 4, 2), ("wall_0", "wall_1", "xs_0", "xs_1"))
    return jax.shard_map(
        shards,
        mesh=torus,
        in_specs=(P(None, None, WALL, None, XS), P(None, WALL, None, XS), P()),
        out_specs=(P(None, WALL, None, XS), P()),
        check_vma=False,
    )
```
